32 devices in a mesh: seq: 32 (over z, y, x, core).
Axes of the slice: x: 2, y: 2, z: 4, core: 2. Of those that a mesh axis runs over, the one named last changes fastest.
Arguments:
- tokens: bfloat16 [8192, 1536], P('seq'), may hold values from -6 to 6
- segment_ids: int32 [8192], P('seq'), may hold values from 0 to 3, never falling along the last dimension, each value on 1 to 4096 neighbouring positions
- out_grad: bfloat16 [8192, 1536], P('seq'), may hold values from -6 to 6
- attn_master: float32 [7079424], P('seq'), as said below
- attn_first: float32 [7079424], P('seq'), as said below
- attn_second: float32 [7079424], P('seq'), as said below
- ffn_master: float32 [18875904], P('seq'), as said below
- ffn_first: float32 [18875904], P('seq'), as said below
- ffn_second: float32 [18875904], P('seq'), as said below
Outputs:
- result: bfloat16 [8192, 1536], P('seq')
- input_grad: float32 [8192, 1536], P('seq')
- attn_master_new: float32 [7079424], P('seq')
- attn_first_new: float32 [7079424], P('seq')
- attn_second_new: float32 [7079424], P('seq')
- ffn_master_new: float32 [18875904], P('seq')
- ffn_first_new: float32 [18875904], P('seq')
- ffn_second_new: float32 [18875904], P('seq')
The draws below stay inside these ranges and needn't reach their ends.
Inputs may be any that keep to these rules, and one draw needn't show every extreme that they name: `segment_ids`: item numbers never fall along the pack; each item has 1 to 4096 tokens and one has exactly 4096. `attn_master`: gains near 1, weights of mean 0. `ffn_master`: gains near 1, weights of mean 0. `attn_first`: both signs, none zero. `attn_second`: positive. `ffn_first`: both signs, none zero. `ffn_second`: positive.
All inputs are finite; a program needn't handle non-finite values.
Results may differ from the reference program's by a relative error of at most 0.015.
The reference program's roundings to bfloat16 on the way count: a program that leaves them out, or rounds other values in their place, can miss the bound.
Values may be sent and summed in bfloat16 or wider, within the bound.
No kernel may reach another device: no remote copies, remote signals or barrier semaphores. Data moves between devices by JAX's collectives and lax.ppermute only.
A program may use at most 448 MiB of HBM per device.

```python
import math
import jax
import jax.numpy as jnp
import numpy as np
from jax import lax

D = 1536
HEADS = 16
KV_HEADS = 8
HEAD_DIM = 96
FF = 4096
TOK_DEV = 256
SEG_MOST = 4096
STEP = 7
TOKENS = 8192
SEGMENTS = 4
REACH = 16
N_SEQ = 32


def spread_draw(key, entries, spread):
    return jax.random.normal(key, (entries,), jnp.float32) * spread


def gain_draw(key):
    return 1.0 + 0.1 * jnp.clip(jax.random.normal(key, (D,), jnp.float32), -3.0, 3.0)


def master_draw(key, blocks):
    parts_list = [gain_draw(jax.random.fold_in(key, 0))]
    for number, (entries, spread) in enumerate(blocks):
        parts_list.append(spread_draw(jax.random.fold_in(key, number + 1), entries, spread))
    return jnp.concatenate(parts_list)


def attention_layout():
    q_width = HEADS * HEAD_DIM
    kv_width = KV_HEADS * HEAD_DIM
    return [(D, 3.0), (D * q_width, 1.5), (D * kv_width, 1.5), (D * kv_width, 1.5), (q_width * D, 0.5)]


def ffn_layout():
    return [(D, 0.7), (D * FF, 0.5), (D * FF, 0.5), (FF * D, 0.4)]


def moment_draw(key, layout, second_kind):
    parts_list = []
    base_size = math.sqrt(TOKENS)
    for number, (entries, weight_coef) in enumerate(layout):
        grad_size = base_size * weight_coef
        key_here = jax.random.fold_in(key, number + 11)
        if second_kind:
            factor = jnp.exp(jax.random.uniform(key_here, (entries,), jnp.float32, 0.0, math.log(4.0)))
            parts_list.append(factor * (grad_size * grad_size))
        else:
            key_sign = jax.random.fold_in(key_here, 99)
            factor = jnp.exp(jax.random.uniform(key_here, (entries,), jnp.float32, math.log(0.5), math.log(2.0)))
            sign_values = jnp.where(jax.random.bernoulli(key_sign, 0.5, (entries,)), 1.0, -1.0)
            parts_list.append(factor * sign_values * grad_size)
    return jnp.concatenate(parts_list)


def draw_attn_master(key, part):
    q_width = HEADS * HEAD_DIM
    kv_width = KV_HEADS * HEAD_DIM
    blocks = [(D * q_width, math.sqrt(2.0 / D)), (D * kv_width, math.sqrt(2.0 / D)), (D * kv_width, 1.0 / math.sqrt(D)), (q_width * D, 4.0 / math.sqrt(q_width))]
    return master_draw(jax.random.fold_in(key, 1), blocks)


def draw_ffn_master(key, part):
    blocks = [(D * FF, 1.0 / math.sqrt(D)), (D * FF, 1.0 / math.sqrt(D)), (FF * D, 1.0 / math.sqrt(FF))]
    return master_draw(jax.random.fold_in(key, 2), blocks)


def draw_attn_first(key, part):
    return moment_draw(jax.random.fold_in(key, 3), attention_layout(), False)


def draw_attn_second(key, part):
    return moment_draw(jax.random.fold_in(key, 4), attention_layout(), True)


def draw_ffn_first(key, part):
    return moment_draw(jax.random.fold_in(key, 5), ffn_layout(), False)


def draw_ffn_second(key, part):
    return moment_draw(jax.random.fold_in(key, 6), ffn_layout(), True)


def strengthened(drawn, rng, source, target, parts, factor):
    owner, partner = [(jnp.arange(drawn.shape[dim]) // (drawn.shape[dim] // parts)).reshape([-1 if axis == dim else 1 for axis in range(drawn.ndim)]) for dim in (source, target)]
    chosen = jax.random.permutation(rng, parts)[partner]
    strong = (owner == chosen) | (owner == (partner + parts // 2) % parts)
    return jnp.where(strong, factor * drawn, drawn)


def shard_levels(key, extent, split, smallest, high):
    level = 1.0
    for position, shards_of in split:
        steps = jax.random.uniform(jax.random.fold_in(jax.random.fold_in(key, 6), position), (shards_of,), jnp.float32, smallest / len(split), high / len(split))
        level = level * jnp.repeat(jnp.exp(steps), extent[position] // shards_of).reshape((-1,) + (1,) * (len(extent) - 1 - position))
    return level


def profile(count, total, reach, slope):
    loads = [(1 << 20) // math.isqrt(rank ** slope) + 1 for rank in range(2, count + 1)]
    spare, counts = total - reach - (count - 1), [1] * (count - 1)
    while spare > 0:
        candidates = [i for i in range(count - 1) if counts[i] < reach]
        mass, budget = sum([loads[i] for i in candidates]), spare
        for i in candidates:
            extra = min(reach - counts[i], max(1, budget * loads[i] // mass), spare)
            counts[i] = counts[i] + extra
            spare = spare - extra
    return np.array([reach] + counts)


def uneven(rng, amount, total, bound, skew):
    if amount == 2:
        one = jax.random.randint(rng, (), max(1, total - bound), min(bound, total - 1) + 1)
        return jnp.stack([one, total - one])
    lengths = jnp.asarray(profile(amount, total, bound, skew), jnp.int32)
    couples = (amount - 1) // 2
    donor, receiver = lengths[1:1 + 2 * couples:2], lengths[2:2 + 2 * couples:2]
    room = jnp.minimum(donor - 1, bound - receiver)
    moved = jax.random.randint(jax.random.fold_in(rng, 1), (couples,), 0, 1 << 20) % (room + 1)
    lengths = lengths.at[1:1 + 2 * couples:2].set(donor - moved).at[2:2 + 2 * couples:2].set(receiver + moved)
    return lengths[jax.random.permutation(jax.random.fold_in(rng, 2), amount)]


def gaussian_with(key, extent, scale, reach, cuts, heavy, kind=jnp.bfloat16):
    result = scale * jax.random.normal(key, extent, jnp.float32)
    if cuts:
        result = result * shard_levels(key, extent, cuts, -0.22, 0.18)
    return jnp.clip(strengthened(result, jax.random.fold_in(key, 3), *heavy), -reach, reach).astype(kind)


def setup_inputs(seed: int = 0) -> dict:
    seeds = jax.random.split(jax.random.key(seed), 10)
    return {
        "tokens": gaussian_with(seeds[0], (TOKENS, D), 1.0, 6.0, ((0, 32),), (0, 1, 32, 2.75)),
        "segment_ids": jnp.searchsorted(jnp.cumsum(uneven(seeds[1], SEGMENTS, TOKENS, SEG_MOST, 2)), jnp.arange(TOKENS), side="right").astype(jnp.int32),
        "out_grad": gaussian_with(seeds[2], (TOKENS, D), 1.0, 6.0, ((0, 32),), (0, 1, 32, 2.75)),
        "attn_master": draw_attn_master(jax.random.fold_in(seeds[9], 71), 0),
        "attn_first": draw_attn_first(jax.random.fold_in(seeds[9], 71), 0),
        "attn_second": draw_attn_second(jax.random.fold_in(seeds[9], 71), 0),
        "ffn_master": draw_ffn_master(jax.random.fold_in(seeds[9], 71), 0),
        "ffn_first": draw_ffn_first(jax.random.fold_in(seeds[9], 71), 0),
        "ffn_second": draw_ffn_second(jax.random.fold_in(seeds[9], 71), 0),
    }


ROPE_BASE = 100000.0
NORM_EPS = 1e-05
BETA_ONE = 0.5
BETA_TWO = 0.5
LEARN_RATE = 0.04
DECAY = 0.1
ADAM_EPS = 1e-08
NEG_LARGE = -1e+30
HIGHEST = lax.Precision.HIGHEST

@jax.custom_vjp
def low(v):
    return lax.optimization_barrier(v.astype(jnp.bfloat16)).astype(jnp.float32)

@jax.custom_vjp
def low_back(v):
    return v

def low_keep(v):
    return (low(v), None)

def low_pass(kept, grad):
    return (grad,)

def back_keep(v):
    return (v, None)

def back_low(kept, grad):
    return (low(grad),)
low.defvjp(low_keep, low_pass)
low_back.defvjp(back_keep, back_low)

def rms_norm(values, norm_gain):
    factor = lax.rsqrt(lax.optimization_barrier(jnp.mean(values * values, axis=-1, keepdims=True)) + NORM_EPS)
    return values * factor * norm_gain

def rotation(positions, head_dim):
    half_dim = head_dim // 2
    frequency = jnp.exp(jnp.arange(half_dim).astype(jnp.float32) * (-2.0 * math.log(ROPE_BASE) / head_dim))
    angles = positions.astype(jnp.float32)[:, None] * frequency[None, :]
    return (jnp.cos(angles)[:, None, :], jnp.sin(angles)[:, None, :])

def rotate(values, cosine, sine_part):
    half_dim = values.shape[-1] // 2
    lower_part = values[..., :half_dim]
    upper_part = values[..., half_dim:]
    return jnp.concatenate([lower_part * cosine - upper_part * sine_part, upper_part * cosine + lower_part * sine_part], axis=-1)

def carve(flat_params, shapes):
    pieces = []
    offset = 0
    for shape_now in shapes:
        entries = math.prod(shape_now)
        pieces.append(flat_params[offset:offset + entries].reshape(shape_now))
        offset = offset + entries
    return tuple(pieces)

def split_attention(flat_params):
    q_width = HEADS * HEAD_DIM
    kv_width = KV_HEADS * HEAD_DIM
    return carve(flat_params, [(D,), (D, q_width), (D, kv_width), (D, kv_width), (q_width, D)])

def split_ffn(flat_params):
    return carve(flat_params, [(D,), (D, FF), (D, FF), (FF, D)])

def attention(query_rows, key_rows, value_rows, segments):
    pad_rows = REACH * TOK_DEV
    key_span = (REACH + 1) * TOK_DEV
    group_size = HEADS // KV_HEADS
    score_scale = 1.0 / math.sqrt(HEAD_DIM)
    key_pad = jnp.concatenate([jnp.zeros((pad_rows, KV_HEADS, HEAD_DIM), jnp.float32), key_rows], axis=0)
    value_pad = jnp.concatenate([jnp.zeros((pad_rows, KV_HEADS, HEAD_DIM), jnp.float32), value_rows], axis=0)
    seg_pad = jnp.concatenate([jnp.full((pad_rows,), -1, jnp.int32), segments.astype(jnp.int32)], axis=0)

    def one_block(block_index):
        first_row = (block_index * TOK_DEV).astype(jnp.int32)
        query_block = lax.dynamic_slice_in_dim(query_rows, first_row, TOK_DEV, 0).reshape(TOK_DEV, KV_HEADS, group_size, HEAD_DIM)
        seg_query = lax.dynamic_slice_in_dim(segments.astype(jnp.int32), first_row, TOK_DEV, 0)
        key_block = lax.dynamic_slice_in_dim(key_pad, first_row, key_span, 0)
        value_block = lax.dynamic_slice_in_dim(value_pad, first_row, key_span, 0)
        seg_key = lax.dynamic_slice_in_dim(seg_pad, first_row, key_span, 0)
        query_pos = first_row + jnp.arange(TOK_DEV, dtype=jnp.int32)
        key_pos = first_row - pad_rows + jnp.arange(key_span, dtype=jnp.int32)
        live_mask = (seg_query[:, None] == seg_key[None, :]) & (key_pos[None, :] <= query_pos[:, None]) & (key_pos[None, :] >= 0)
        scores = low_back(jnp.einsum('qkgd,tkd->kgqt', query_block, key_block, precision=HIGHEST) * score_scale)
        masked = jnp.where(live_mask, scores, NEG_LARGE)
        log_total = jax.nn.logsumexp(masked, axis=-1, keepdims=True)
        weights_exp = jnp.where(live_mask, jnp.exp(masked - log_total), 0.0)
        weights_low = low(weights_exp)
        mixed = jnp.einsum('kgqt,tkd->qkgd', weights_low, value_block, precision=HIGHEST)
        return mixed.reshape(TOK_DEV, HEADS * HEAD_DIM)
    outputs = lax.map(jax.checkpoint(one_block), jnp.arange(N_SEQ, dtype=jnp.int32))
    return outputs.reshape(TOKENS, HEADS * HEAD_DIM)

def forward(inputs, attn_parts, ffn_parts, segments):
    norm_one, query_weight, key_weight, value_weight, out_weight = attn_parts
    norm_two, gate_weight, up_weight, down_weight = ffn_parts
    positions = jnp.arange(TOKENS, dtype=jnp.int32)
    cosine, sine_part = rotation(positions, HEAD_DIM)
    normed = low(rms_norm(inputs, norm_one))
    query_pre = low_back(jnp.dot(normed, query_weight, precision=HIGHEST))
    key_pre = low_back(jnp.dot(normed, key_weight, precision=HIGHEST))
    value_rows = low(low_back(jnp.dot(normed, value_weight, precision=HIGHEST)))
    query_rows = low(rotate(query_pre.reshape(TOKENS, HEADS, HEAD_DIM), cosine, sine_part))
    key_rows = low(rotate(key_pre.reshape(TOKENS, KV_HEADS, HEAD_DIM), cosine, sine_part))
    mixed = attention(query_rows, key_rows, value_rows.reshape(TOKENS, KV_HEADS, HEAD_DIM), segments)
    mixed_low = low(low_back(mixed))
    branch_one = low_back(jnp.dot(mixed_low, out_weight, precision=HIGHEST))
    middle = inputs + branch_one
    normed_two = low(rms_norm(middle, norm_two))
    gate_rows = low_back(jnp.dot(normed_two, gate_weight, precision=HIGHEST))
    up_rows = low_back(jnp.dot(normed_two, up_weight, precision=HIGHEST))
    hidden = low(jax.nn.silu(gate_rows) * up_rows)
    branch_two = low_back(jnp.dot(hidden, down_weight, precision=HIGHEST))
    return middle + branch_two

def adam_update(master, moment_one, moment_two, gradient):
    first_new = BETA_ONE * moment_one + (1.0 - BETA_ONE) * gradient
    second_new = BETA_TWO * moment_two + (1.0 - BETA_TWO) * gradient * gradient
    first_hat = first_new / (1.0 - BETA_ONE ** STEP)
    second_hat = second_new / (1.0 - BETA_TWO ** STEP)
    master_new = master - LEARN_RATE * (first_hat / (jnp.sqrt(second_hat) + ADAM_EPS) + DECAY * master)
    return (master_new, first_new, second_new)

def reference(tokens, segment_ids, out_grad, attn_master, attn_first, attn_second, ffn_master, ffn_first, ffn_second):
    attn_parts = split_attention(attn_master.astype(jnp.bfloat16).astype(jnp.float32))
    ffn_parts = split_ffn(ffn_master.astype(jnp.bfloat16).astype(jnp.float32))
    inputs = tokens.astype(jnp.float32)

    def run_layer(inputs_arg, attn_arg, ffn_arg):
        return forward(inputs_arg, attn_arg, ffn_arg, segment_ids)
    outputs, pullback = jax.vjp(run_layer, inputs, attn_parts, ffn_parts)
    input_grad, attn_grads, ffn_grads = pullback(out_grad.astype(jnp.float32))
    attn_flat = jnp.concatenate([piece_grad.reshape(-1) for piece_grad in attn_grads])
    ffn_flat = jnp.concatenate([piece_grad.reshape(-1) for piece_grad in ffn_grads])
    attn_new, attn_one, attn_two = adam_update(attn_master, attn_first, attn_second, attn_flat)
    ffn_new, ffn_one, ffn_two = adam_update(ffn_master, ffn_first, ffn_second, ffn_flat)
    return (outputs.astype(jnp.bfloat16), input_grad, attn_new, attn_one, attn_two, ffn_new, ffn_one, ffn_two)
```

```python
import functools
import math

import jax
import jax.numpy as jnp
from jax import lax
from jax.experimental import pallas as pl
from jax.experimental.pallas import tpu as pltpu
from jax.sharding import PartitionSpec as P

D = 1536
HEADS = 16
KV_HEADS = 8
HEAD_DIM = 96
FF = 4096
SEG_MOST = 4096
STEP = 7


ROPE_BASE = 100000.0
NORM_EPS = 1e-05
BETA_ONE = 0.5
BETA_TWO = 0.5
LEARN_RATE = 0.04
DECAY = 0.1
ADAM_EPS = 1e-08
NEG_LARGE = -1e30
HALF_DIM = HEAD_DIM // 2
QUERY_TILE = 512
KEY_TILE = 1024
CHUNK = 8192
SCORE_BASE_TWO = math.log2(math.e) / math.sqrt(HEAD_DIM)
SCORE_SCALE = 1.0 / math.sqrt(HEAD_DIM)


def rms_norm(values, norm_gain):
    factor = lax.rsqrt(jnp.mean(values * values, axis=-1, keepdims=True) + NORM_EPS)
    return values * factor * norm_gain


def angle_tables(positions):
    frequency = jnp.exp(
        jnp.arange(HALF_DIM).astype(jnp.float32) * (-2.0 * math.log(ROPE_BASE) / HEAD_DIM)
    )
    angles = positions.astype(jnp.float32)[..., None, :] * frequency[:, None]
    return (jnp.cos(angles), jnp.sin(angles))


def rotate(values, cosine, sine_part):
    lower_part = values[..., :HALF_DIM, :]
    upper_part = values[..., HALF_DIM:, :]
    return jnp.concatenate(
        [
            lower_part * cosine - upper_part * sine_part,
            upper_part * cosine + lower_part * sine_part,
        ],
        axis=-2,
    )


def contract(left, left_dim, right, right_dim):
    return lax.dot_general(
        left,
        right,
        (((left_dim,), (right_dim,)), ((), ())),
        preferred_element_type=jnp.float32,
    )


def adam_update(master, moment_one, moment_two, gradient):
    first_new = BETA_ONE * moment_one + (1.0 - BETA_ONE) * gradient
    second_new = BETA_TWO * moment_two + (1.0 - BETA_TWO) * gradient * gradient
    first_hat = first_new / (1.0 - BETA_ONE**STEP)
    second_hat = second_new / (1.0 - BETA_TWO**STEP)
    master_new = master - LEARN_RATE * (
        first_hat / (jnp.sqrt(second_hat) + ADAM_EPS) + DECAY * master
    )
    return (master_new, first_new, second_new)


def units_from_shard(flat_low, index, count):
    edge = D // count
    block = flat_low.shape[0] - edge
    unit = block // 3
    following = lax.ppermute(flat_low[:D], "seq", [(i + 1, i) for i in range(count - 1)])
    extended = jnp.concatenate([flat_low, following])
    aligned = lax.dynamic_slice(extended, (D - edge * index,), (block,)).reshape(3, unit)
    dealt = jnp.stack(
        [
            lax.ppermute(aligned[j], "seq", [(i, (3 * i + j) % count) for i in range(count)])
            for j in range(3)
        ]
    )
    return [
        lax.dynamic_index_in_dim(dealt, slot_of_kind(index, kind, count), 0, keepdims=False)
        for kind in range(3)
    ]


def slot_of_kind(index, kind, count):
    return (index + count * kind) % 3


def shard_from_units(units, gain_grad, index, count):
    edge = D // count
    stacked = jnp.stack(units)
    unit = stacked.shape[1]
    returned = []
    for j in range(3):
        inverse = 1 if count % 3 == 1 else 2
        kind = ((j - index) * inverse) % 3
        piece = lax.dynamic_index_in_dim(stacked, kind, 0, keepdims=False)
        returned.append(
            lax.ppermute(piece, "seq", [((3 * i + j) % count, i) for i in range(count)])
        )
    block = jnp.concatenate(returned)
    before = lax.ppermute(block[-D:], "seq", [(i, i + 1) for i in range(count - 1)])
    before = jnp.where(index == 0, gain_grad.astype(before.dtype), before)
    extended = jnp.concatenate([before, block])
    return lax.dynamic_slice(extended, (edge * index,), (3 * unit + edge,))


AXES = ("z", "y", "x")
GATHER_ORDERS = (("z", "y", "x"), ("z", "x", "y"), ("y", "x", "z"))


def device_grid(count):
    chips = count // 2
    sides = {16: (4, 2, 2), 64: (4, 4, 4)}.get(chips, (chips, 1, 1))
    return dict(zip(AXES + ("core",), sides + (2,)))


def coordinates(index, grid):
    found = {}
    for axis in reversed(list(grid)):
        found[axis] = index % grid[axis]
        index = index // grid[axis]
    return found


def place(found, grid):
    index = 0
    for axis in grid:
        index = index * grid[axis] + found[axis]
    return index


def shifted(value, axis, steps, grid):
    pairs = []
    for source in range(math.prod(grid.values())):
        target = coordinates(source, grid)
        target[axis] = (target[axis] + steps) % grid[axis]
        pairs.append((source, place(target, grid)))
    return lax.ppermute(value, "seq", pairs)


def slot_table(index, grid, axes):
    here = coordinates(index, grid)
    entries = []
    for number in range(math.prod(grid.values())):
        slots = coordinates(number, {axis: grid[axis] for axis in axes})
        there = {axis: (here[axis] - slots[axis]) % grid[axis] for axis in grid}
        entries.append(place(there, grid))
    return jnp.stack(entries).astype(jnp.int32)


def place_kernel(table_ref, *refs, lengths, rows):
    piece_refs, out_ref, sems = (refs[:-2], refs[-2], refs[-1])
    copies = []
    for piece_ref, length in zip(piece_refs, lengths):
        for block in range(length):
            entry = len(copies)
            target = pl.ds(pl.multiple_of(table_ref[entry] * rows, rows), rows)
            copy = pltpu.make_async_copy(
                piece_ref.at[pl.ds(block * rows, rows), :], out_ref.at[target, :], sems.at[entry]
            )
            copy.start()
            copies.append(copy)
    for copy in copies:
        copy.wait()


def placed(pieces, table, rows):
    count = table.shape[0]
    width = pieces[0].shape[1]
    lengths = tuple(piece.shape[0] // rows for piece in pieces)
    anywhere = pl.BlockSpec(memory_space=pl.ANY)
    return pl.pallas_call(
        functools.partial(place_kernel, lengths=lengths, rows=rows),
        grid_spec=pltpu.PrefetchScalarGridSpec(
            num_scalar_prefetch=1,
            grid=(1,),
            in_specs=[anywhere] * len(pieces),
            out_specs=anywhere,
            scratch_shapes=[pltpu.SemaphoreType.DMA((count,))],
        ),
        out_shape=jax.ShapeDtypeStruct((count * rows, width), pieces[0].dtype),
        cost_estimate=pl.CostEstimate(
            flops=0, transcendentals=0, bytes_accessed=4 * count * rows * width
        ),
        name="place_blocks",
    )(table, *pieces)


def gather_rows(block, order, index, grid):
    rows = block.shape[0]
    held = block
    for axis in order:
        arrivals = [held]
        for _ in range(grid[axis] - 1):
            arrivals.append(shifted(arrivals[-1], axis, 1, grid))
        if axis != order[-1]:
            held = jnp.concatenate(arrivals)
    pieces = arrivals + [shifted(piece, "core", 1, grid) for piece in arrivals]
    table = slot_table(index, grid, ("core",) + tuple(reversed(order)))
    return placed(pieces, table, rows)


def reorder_kernel(table_ref, in_ref, out_ref, *, rows):
    for block in range(in_ref.shape[0] // rows):
        source = pl.ds(pl.multiple_of(table_ref[block] * rows, rows), rows)
        out_ref[block * rows : (block + 1) * rows, :] = in_ref[source, :]


def reordered(value, table):
    rows = value.shape[0] // table.shape[0]
    return pl.pallas_call(
        functools.partial(reorder_kernel, rows=rows),
        grid_spec=pltpu.PrefetchScalarGridSpec(
            num_scalar_prefetch=1,
            grid=(1,),
            in_specs=[whole_spec(value)],
            out_specs=whole_spec(value),
        ),
        out_shape=jax.ShapeDtypeStruct(value.shape, value.dtype),
        cost_estimate=pl.CostEstimate(
            flops=0, transcendentals=0, bytes_accessed=4 * value.size
        ),
        name="reorder_blocks",
    )(table, value)


def sum_scatter(left_cols, right, right_dim, order, index, grid):
    count = math.prod(grid.values())
    rows = left_cols.shape[0] // count
    order = ("core",) + tuple(reversed(order))
    left = reordered(left_cols, slot_table(index, grid, order))
    received = []

    def partial(first, last):
        span = slice(first * rows, last * rows)
        total = contract(left[span], 1, right, right_dim)
        for part in received:
            total = total + part[span]
        return total

    window = count
    for axis in order:
        window = window // grid[axis]
        passing = None
        for slot in range(grid[axis] - 1, 0, -1):
            own = partial(slot * window, (slot + 1) * window)
            total = own if passing is None else own + passing
            passing = shifted(total.astype(jnp.bfloat16), axis, -1, grid)
        if passing is not None:
            received.append(passing)
    return partial(0, 1)


def live_pairs(rel_ref, pos, start, base, queries):
    rel = rel_ref[...]
    rel = jnp.concatenate([rel] * (queries // rel.shape[1]), axis=1)
    return (rel >= start - base) & (rel <= pos - base)


def forward_kernel(
    low_ref, high_ref, query_ref, key_ref, value_ref, pos_ref, start_ref, rel_ref, out_ref, lse_ref
):
    tile = pl.program_id(0)
    query_cols = query_ref[0]
    queries = query_cols.shape[1]
    keys = rel_ref.shape[0]
    pos = pos_ref[0]
    start = start_ref[0]

    def body(step, carried):
        run_max, run_total, mixed = carried
        rows = pl.ds(pl.multiple_of(step * keys, keys), keys)
        scores = contract(key_ref[rows, :], 1, query_cols, 0)
        live = live_pairs(rel_ref, pos, start, step * keys, queries)
        scores = jnp.where(live, scores, NEG_LARGE)
        new_max = jnp.maximum(run_max, jnp.max(scores, axis=0, keepdims=True))
        weights = jnp.exp2((scores - new_max) * SCORE_BASE_TWO)
        keep = jnp.exp2((run_max - new_max) * SCORE_BASE_TWO)
        run_total = run_total * keep + jnp.sum(weights, axis=0, keepdims=True)
        mixed = mixed * keep + contract(value_ref[step], 1, weights.astype(jnp.bfloat16), 0)
        return (new_max, run_total, mixed)

    start_state = (
        jnp.full((1, queries), NEG_LARGE, jnp.float32),
        jnp.zeros((1, queries), jnp.float32),
        jnp.zeros((HEAD_DIM, queries), jnp.float32),
    )
    run_max, run_total, mixed = lax.fori_loop(low_ref[tile], high_ref[tile], body, start_state)
    out_ref[0] = mixed / run_total
    lse_ref[0] = run_max * SCORE_BASE_TWO + jnp.log2(run_total)


def backward_kernel(
    low_ref,
    high_ref,
    query_ref,
    query_row_ref,
    dout_ref,
    dout_row_ref,
    out_ref,
    lse_ref,
    key_ref,
    key_col_ref,
    value_ref,
    pos_ref,
    start_ref,
    rel_ref,
    dquery_ref,
    dkey_ref,
    dvalue_ref,
):
    tile = pl.program_id(0)

    @pl.when(tile == 0)
    def _():
        dkey_ref[...] = jnp.zeros_like(dkey_ref)
        dvalue_ref[...] = jnp.zeros_like(dvalue_ref)

    query_cols = query_ref[0]
    query_rows = query_row_ref[0]
    dout_cols = dout_ref[0]
    dout_rows = dout_row_ref[0]
    queries = query_cols.shape[1]
    keys = rel_ref.shape[0]
    pos = pos_ref[0]
    start = start_ref[0]
    lse = lse_ref[0]
    delta = jnp.sum(dout_cols.astype(jnp.float32) * out_ref[0], axis=0, keepdims=True)

    def body(step, dquery):
        rows = pl.ds(pl.multiple_of(step * keys, keys), keys)
        scores = contract(key_ref[rows, :], 1, query_cols, 0)
        live = live_pairs(rel_ref, pos, start, step * keys, queries)
        weights = jnp.where(live, jnp.exp2(scores * SCORE_BASE_TWO - lse), 0.0)
        weight_grad = contract(value_ref[rows, :], 1, dout_cols, 0)
        dscore = (weights * (weight_grad - delta)).astype(jnp.bfloat16)
        dvalue_ref[rows, :] += contract(weights.astype(jnp.bfloat16), 1, dout_rows, 0)
        dkey_ref[rows, :] += contract(dscore, 1, query_rows, 0)
        return dquery + contract(key_col_ref[step], 1, dscore, 0)

    dquery = lax.fori_loop(
        low_ref[tile], high_ref[tile], body, jnp.zeros((HEAD_DIM, queries), jnp.float32)
    )
    dquery_ref[0] = dquery * SCORE_SCALE

    @pl.when(tile == pl.num_programs(0) - 1)
    def _():
        dkey_ref[...] = dkey_ref[...] * SCORE_SCALE


def whole_spec(array):
    return pl.BlockSpec(array.shape, lambda i, *_: (0,) * array.ndim)


def tile_spec(array):
    return pl.BlockSpec((1,) + array.shape[1:], lambda i, *_: (i,) + (0,) * (array.ndim - 1))


def run_kernel(body, name, bounds, inputs, outputs, flops):
    spec = lambda item: tile_spec(item[0]) if item[1] else whole_spec(item[0])
    grid = next(array.shape[0] for array, cut in inputs if cut)
    return pl.pallas_call(
        body,
        grid_spec=pltpu.PrefetchScalarGridSpec(
            num_scalar_prefetch=2,
            grid=(grid,),
            in_specs=[spec(item) for item in inputs],
            out_specs=[spec(item) for item in outputs],
        ),
        out_shape=[item[0] for item in outputs],
        compiler_params=pltpu.CompilerParams(vmem_limit_bytes=52 << 20),
        cost_estimate=pl.CostEstimate(
            flops=flops, transcendentals=flops // 400, bytes_accessed=16 << 20
        ),
        name=name,
    )(*bounds, *[item[0] for item in inputs])


def attend(query_cols, key_rows, value_cols, pos, start, rel, low, high):
    tiles, _, queries = query_cols.shape
    return run_kernel(
        forward_kernel,
        "attention_forward",
        (low, high),
        [
            (query_cols, True),
            (key_rows, False),
            (value_cols, False),
            (pos, True),
            (start, True),
            (rel, False),
        ],
        [
            (jax.ShapeDtypeStruct((tiles, HEAD_DIM, queries), jnp.float32), True),
            (jax.ShapeDtypeStruct((tiles, 1, queries), jnp.float32), True),
        ],
        20_000_000_000,
    )


def attend_back(
    query_cols, dout_cols, out_cols, lse, key_rows, key_cols, value_rows, pos, start, rel, low, high
):
    tiles, _, queries = query_cols.shape
    grads = jax.ShapeDtypeStruct(key_rows.shape, jnp.float32)
    return run_kernel(
        backward_kernel,
        "attention_backward",
        (low, high),
        [
            (query_cols, True),
            (jnp.swapaxes(query_cols, 1, 2), True),
            (dout_cols, True),
            (jnp.swapaxes(dout_cols, 1, 2), True),
            (out_cols, True),
            (lse, True),
            (key_rows, False),
            (key_cols, False),
            (value_rows, False),
            (pos, True),
            (start, True),
            (rel, False),
        ],
        [
            (jax.ShapeDtypeStruct((tiles, HEAD_DIM, queries), jnp.float32), True),
            (grads, False),
            (grads, False),
        ],
        50_000_000_000,
    )


def per_device(
    tokens,
    segment_ids,
    out_grad,
    attn_master,
    attn_first,
    attn_second,
    ffn_master,
    ffn_first,
    ffn_second,
):
    index = lax.axis_index("seq")
    count = lax.axis_size("seq")
    rows = tokens.shape[0]
    total = rows * count
    group = count // KV_HEADS
    parts = group // 2
    span = rows // parts
    half = (index // parts) % 2
    part = index % parts

    def exchange(value):
        return lax.all_to_all(value, "seq", 0, 0, tiled=True)

    def swapped(value, bit):
        return lax.ppermute(value, "seq", [(i, i ^ bit) for i in range(count)])

    attn_low = attn_master.astype(jnp.bfloat16)
    ffn_low = ffn_master.astype(jnp.bfloat16)
    gains = lax.psum(
        jnp.where(
            index == 0, jnp.stack([attn_low[:D], ffn_low[:D]]).astype(jnp.float32), 0.0
        ),
        "seq",
    )
    gain_one, gain_two = (gains[0], gains[1])

    grid = device_grid(count)
    by_axes = (D // count) % 16 == 0

    def gathered(unit, width, color):
        block = unit.reshape(-1, width)
        if by_axes:
            return gather_rows(block, GATHER_ORDERS[color], index, grid)
        return lax.all_gather(block, "seq", axis=0, tiled=True)

    def scattered(left_cols, right, right_dim, color):
        if by_axes:
            return sum_scatter(
                left_cols, right, right_dim, GATHER_ORDERS[color], index, grid
            ).reshape(-1)
        whole = contract(left_cols, 1, right, right_dim).astype(jnp.bfloat16)
        return (
            lax.psum_scatter(whole, "seq", scatter_dimension=0, tiled=True)
            .reshape(-1)
            .astype(jnp.float32)
        )

    q_unit, kv_unit, o_unit = units_from_shard(attn_low, index, count)
    gate_unit, up_unit, down_unit = units_from_shard(ffn_low, index, count)
    query_weight = gathered(q_unit, HEADS * HEAD_DIM, 0)
    key_value_weight = gathered(kv_unit, KV_HEADS * HEAD_DIM, 1)
    key_weight, value_weight = (key_value_weight[:D], key_value_weight[D:])
    out_weight = gathered(o_unit, D, 2)
    gate_weight = gathered(gate_unit, FF, 0)
    up_weight = gathered(up_unit, FF, 1)
    down_weight = gathered(down_unit, D, 2)

    all_ids = lax.all_gather(segment_ids.reshape(1, rows), "seq", axis=0, tiled=True).reshape(-1)

    def item_starts(ids):
        return jnp.sum((all_ids < ids[..., None]).astype(jnp.int32), axis=-1)

    inputs = tokens.astype(jnp.float32)
    normed_one = rms_norm(inputs, gain_one).astype(jnp.bfloat16)
    own_places = index * rows + jnp.arange(rows, dtype=jnp.int32)
    own_cos, own_sin = angle_tables(own_places)
    query_pre = contract(query_weight, 0, normed_one, 1).reshape(HEADS, HEAD_DIM, rows)
    key_pre = contract(key_weight, 0, normed_one, 1).reshape(KV_HEADS, HEAD_DIM, rows)
    value_low = (
        contract(value_weight, 0, normed_one, 1)
        .astype(jnp.bfloat16)
        .reshape(KV_HEADS, HEAD_DIM, rows)
    )
    query_low = rotate(query_pre, own_cos, own_sin).astype(jnp.bfloat16)
    key_low = rotate(key_pre, own_cos, own_sin).astype(jnp.bfloat16)

    def by_owner(value):
        pieces = value.reshape(HEADS, HEAD_DIM, parts, span)
        return jnp.swapaxes(pieces, 1, 2).reshape(count, HEAD_DIM, span)

    def by_head(value):
        pieces = value.reshape(HEADS, parts, HEAD_DIM, span)
        return jnp.swapaxes(pieces, 1, 2).reshape(HEADS, HEAD_DIM, rows)

    def paired(key_part, value_part):
        return jnp.stack([key_part, value_part], axis=1).reshape(HEADS, HEAD_DIM, rows)

    received = exchange(
        jnp.concatenate([by_owner(query_low), by_owner(paired(key_low, value_low))], axis=1)
    )

    sources = QUERY_TILE // span
    tiles = count // sources

    def to_tiles(value):
        pieces = value.reshape(tiles, sources, value.shape[1], span)
        return jnp.swapaxes(pieces, 1, 2).reshape(tiles, value.shape[1], QUERY_TILE)

    def from_tiles(value):
        pieces = value.reshape(tiles, value.shape[1], sources, span)
        return jnp.swapaxes(pieces, 1, 2).reshape(count, value.shape[1], span)

    query_cols = to_tiles(received[:, :HEAD_DIM])
    own_kind = received[:, HEAD_DIM:]
    other_kind = swapped(own_kind, parts)
    pair = jnp.stack(
        [
            jnp.where(half == 0, own_kind, other_kind),
            jnp.where(half == 0, other_kind, own_kind),
        ]
    )[:, None]
    bit = 1
    while bit < parts:
        pair = jnp.concatenate([pair, swapped(pair, bit)], axis=1)
        bit = bit * 2
    key_all, value_all = (pair[0], pair[1])
    devices_per_tile = KEY_TILE // rows
    key_tiles = count // devices_per_tile

    def key_columns(value):
        pieces = value.reshape(parts, key_tiles, devices_per_tile, HEAD_DIM, span)
        return jnp.transpose(pieces, (1, 3, 2, 0, 4)).reshape(key_tiles, HEAD_DIM, KEY_TILE)

    def key_rows_of(value):
        return jnp.transpose(value, (1, 0, 3, 2)).reshape(total, HEAD_DIM)

    key_cols = key_columns(key_all)
    value_cols = key_columns(value_all)
    key_rows = key_rows_of(key_all)
    value_rows = key_rows_of(value_all)
    slot_parts = part ^ jnp.arange(parts, dtype=jnp.int32)
    within = jnp.arange(span, dtype=jnp.int32)
    rel = (
        rows * jnp.arange(devices_per_tile, dtype=jnp.int32)[:, None, None]
        + span * slot_parts[None, :, None]
        + within[None, None, :]
    ).reshape(KEY_TILE, 1)
    rel = jnp.broadcast_to(rel, (KEY_TILE, 128))
    held_places = (
        rows * jnp.arange(count, dtype=jnp.int32)[:, None] + span * part + within[None, :]
    )
    held_ids = lax.dynamic_index_in_dim(
        all_ids.reshape(count, parts, span), part, 1, keepdims=False
    )
    held_starts = item_starts(held_ids.reshape(-1))
    pos = held_places.reshape(tiles, 1, QUERY_TILE)
    start = held_starts.reshape(tiles, 1, QUERY_TILE)
    tile_span = sources * rows
    low = item_starts(all_ids[::tile_span]) // KEY_TILE
    high = (jnp.arange(1, tiles + 1, dtype=jnp.int32) * tile_span + KEY_TILE - 1) // KEY_TILE

    chunks = []
    chunk = min(CHUNK, total)
    for first in range(0, total, chunk):
        first_key = max(0, first - SEG_MOST) // KEY_TILE
        last_key = (first + chunk) // KEY_TILE
        chunks.append(
            (
                slice(first // tile_span, (first + chunk) // tile_span),
                slice(first_key, last_key),
                slice(first_key * KEY_TILE, last_key * KEY_TILE),
            )
        )

    pieces = []
    for of_tiles, of_key_tiles, of_keys in chunks:
        shift = of_key_tiles.start * KEY_TILE
        pieces.append(
            attend(
                query_cols[of_tiles],
                key_rows[of_keys],
                value_cols[of_key_tiles],
                pos[of_tiles] - shift,
                start[of_tiles] - shift,
                rel,
                low[of_tiles] - of_key_tiles.start,
                high[of_tiles] - of_key_tiles.start,
            )
        )
    out_cols = jnp.concatenate([piece[0] for piece in pieces])
    lse = jnp.concatenate([piece[1] for piece in pieces])

    mixed_low = by_head(exchange(from_tiles(out_cols.astype(jnp.bfloat16)))).reshape(
        HEADS * HEAD_DIM, rows
    )

    middle = inputs + contract(mixed_low, 0, out_weight, 0)
    normed_two = rms_norm(middle, gain_two).astype(jnp.bfloat16)
    gate_rows = contract(normed_two, 1, gate_weight, 0)
    up_rows = contract(normed_two, 1, up_weight, 0)
    hidden = (jax.nn.silu(gate_rows) * up_rows).astype(jnp.bfloat16)
    result = (middle + contract(hidden, 1, down_weight, 0)).astype(jnp.bfloat16)
    hidden_grad = contract(out_grad, 1, down_weight, 1)
    sigma_gate = jax.nn.sigmoid(gate_rows)
    silu_gate = gate_rows * sigma_gate
    gate_grad = (
        hidden_grad * up_rows * sigma_gate * (1.0 + gate_rows * (1.0 - sigma_gate))
    ).astype(jnp.bfloat16)
    up_grad = (hidden_grad * silu_gate).astype(jnp.bfloat16)
    normed_two_grad = contract(gate_grad, 1, gate_weight, 1) + contract(up_grad, 1, up_weight, 1)
    _, norm_pull = jax.vjp(rms_norm, middle, gain_two)
    middle_norm_grad, grad_two = norm_pull(normed_two_grad)
    middle_grad = out_grad.astype(jnp.float32) + middle_norm_grad
    middle_low = middle_grad.astype(jnp.bfloat16)

    dout_cols = to_tiles(
        exchange(
            by_owner(
                contract(out_weight, 1, middle_low, 1)
                .astype(jnp.bfloat16)
                .reshape(HEADS, HEAD_DIM, rows)
            )
        )
    )
    normed_two_cols = normed_two.T
    ffn_units = [
        scattered(normed_two_cols, gate_grad, 0, 0),
        scattered(normed_two_cols, up_grad, 0, 1),
        scattered(hidden.T, out_grad, 0, 2),
    ]
    out_unit = scattered(mixed_low, middle_low, 0, 2)

    pieces = []
    dkey_rows = jnp.zeros((total, HEAD_DIM), jnp.float32)
    dvalue_rows = jnp.zeros((total, HEAD_DIM), jnp.float32)
    for of_tiles, of_key_tiles, of_keys in chunks:
        shift = of_key_tiles.start * KEY_TILE
        dquery_piece, dkey_piece, dvalue_piece = attend_back(
            query_cols[of_tiles],
            dout_cols[of_tiles],
            out_cols[of_tiles],
            lse[of_tiles],
            key_rows[of_keys],
            key_cols[of_key_tiles],
            value_rows[of_keys],
            pos[of_tiles] - shift,
            start[of_tiles] - shift,
            rel,
            low[of_tiles] - of_key_tiles.start,
            high[of_tiles] - of_key_tiles.start,
        )
        pieces.append(dquery_piece)
        if len(chunks) == 1:
            dkey_rows, dvalue_rows = (dkey_piece, dvalue_piece)
        else:
            dkey_rows = dkey_rows.at[of_keys].add(dkey_piece)
            dvalue_rows = dvalue_rows.at[of_keys].add(dvalue_piece)
    dquery_rot = from_tiles(jnp.concatenate(pieces))
    held_cos, held_sin = angle_tables(held_places)
    dquery_held = rotate(dquery_rot, held_cos, -held_sin).astype(jnp.bfloat16)

    def by_slot(value):
        return jnp.transpose(value.reshape(count, parts, span, HEAD_DIM), (1, 0, 3, 2))

    grads = jnp.stack([by_slot(dkey_rows), by_slot(dvalue_rows)])
    bit = parts // 2
    while bit >= 1:
        grads = grads[:, :bit] + swapped(grads[:, bit:].astype(jnp.bfloat16), bit)
        bit = bit // 2
    dkey_held, dvalue_held = (grads[0, 0], grads[1, 0])
    sent_kind = jnp.where(half == 0, dvalue_held, dkey_held).astype(jnp.bfloat16)
    kept_kind = jnp.where(half == 0, dkey_held, dvalue_held) + swapped(sent_kind, parts)
    kept_low = jnp.where(half == 0, rotate(kept_kind, held_cos, -held_sin), kept_kind).astype(
        jnp.bfloat16
    )
    returned = exchange(jnp.concatenate([dquery_held, kept_low], axis=1))
    dquery_low = by_head(returned[:, :HEAD_DIM]).reshape(HEADS * HEAD_DIM, rows)
    pair_low = by_head(returned[:, HEAD_DIM:]).reshape(KV_HEADS, 2, HEAD_DIM, rows)
    dkey_low = pair_low[:, 0].reshape(KV_HEADS * HEAD_DIM, rows)
    dvalue_low = pair_low[:, 1].reshape(KV_HEADS * HEAD_DIM, rows)

    normed_one_cols = normed_one.T
    query_unit = scattered(normed_one_cols, dquery_low, 1, 0)
    nothing = jnp.zeros_like(normed_one_cols)
    key_value_cols = jnp.concatenate(
        [
            jnp.concatenate([normed_one_cols, nothing], axis=1),
            jnp.concatenate([nothing, normed_one_cols], axis=1),
        ]
    )
    key_value_unit = scattered(
        key_value_cols, jnp.concatenate([dkey_low, dvalue_low], axis=1), 1, 1
    )
    normed_one_grad = (
        contract(dquery_low, 0, query_weight, 1)
        + contract(dkey_low, 0, key_weight, 1)
        + contract(dvalue_low, 0, value_weight, 1)
    )
    _, first_pull = jax.vjp(rms_norm, inputs, gain_one)
    input_norm_grad, grad_one = first_pull(normed_one_grad)
    input_grad = middle_grad + input_norm_grad

    gain_grads = lax.psum(jnp.stack([grad_one, grad_two]), "seq")
    attn_shard = shard_from_units(
        [query_unit, key_value_unit, out_unit], gain_grads[0], index, count
    )
    ffn_shard = shard_from_units(ffn_units, gain_grads[1], index, count)
    attn_new, attn_one, attn_two = adam_update(
        attn_master, attn_first, attn_second, attn_shard
    )
    ffn_new, ffn_one, ffn_two = adam_update(
        ffn_master, ffn_first, ffn_second, ffn_shard
    )
    return (result, input_grad, attn_new, attn_one, attn_two, ffn_new, ffn_one, ffn_two)


def solution(mesh):
    rows_cut = P("seq", None)
    flat_cut = P("seq")
    in_specs = (rows_cut, flat_cut, rows_cut) + (flat_cut,) * 6
    out_specs = (rows_cut, rows_cut) + (flat_cut,) * 6
    return jax.shard_map(
        per_device, mesh=mesh, in_specs=in_specs, out_specs=out_specs, check_vma=False
    )
```

```python
import functools
import math

import jax
import jax.numpy as jnp
from jax import lax
from jax.experimental import pallas as pl
from jax.experimental.pallas import tpu as pltpu
from jax.sharding import PartitionSpec as P

D = 1536
HEADS = 16
KV_HEADS = 8
HEAD_DIM = 96
FF = 4096
SEG_MOST = 4096
STEP = 7


ROPE_BASE = 100000.0
NORM_EPS = 1e-05
BETA_ONE = 0.5
BETA_TWO = 0.5
LEARN_RATE = 0.04
DECAY = 0.1
ADAM_EPS = 1e-08
NEG_LARGE = -1e30
HALF_DIM = HEAD_DIM // 2
QUERY_TILE = 512
KEY_TILE = 1024
CHUNK = 8192
SCORE_BASE_TWO = math.log2(math.e) / math.sqrt(HEAD_DIM)
SCORE_SCALE = 1.0 / math.sqrt(HEAD_DIM)


def rms_norm(values, norm_gain):
    factor = lax.rsqrt(jnp.mean(values * values, axis=-1, keepdims=True) + NORM_EPS)
    return values * factor * norm_gain


def angle_tables(positions):
    frequency = jnp.exp(
        jnp.arange(HALF_DIM).astype(jnp.float32) * (-2.0 * math.log(ROPE_BASE) / HEAD_DIM)
    )
    angles = positions.astype(jnp.float32)[..., None, :] * frequency[:, None]
    return (jnp.cos(angles), jnp.sin(angles))


def rotate(values, cosine, sine_part):
    lower_part = values[..., :HALF_DIM, :]
    upper_part = values[..., HALF_DIM:, :]
    return jnp.concatenate(
        [
            lower_part * cosine - upper_part * sine_part,
            upper_part * cosine + lower_part * sine_part,
        ],
        axis=-2,
    )


def contract(left, left_dim, right, right_dim):
    return lax.dot_general(
        left,
        right,
        (((left_dim,), (right_dim,)), ((), ())),
        preferred_element_type=jnp.float32,
    )


def adam_update(master, moment_one, moment_two, gradient):
    first_new = BETA_ONE * moment_one + (1.0 - BETA_ONE) * gradient
    second_new = BETA_TWO * moment_two + (1.0 - BETA_TWO) * gradient * gradient
    first_hat = first_new / (1.0 - BETA_ONE**STEP)
    second_hat = second_new / (1.0 - BETA_TWO**STEP)
    master_new = master - LEARN_RATE * (
        first_hat / (jnp.sqrt(second_hat) + ADAM_EPS) + DECAY * master
    )
    return (master_new, first_new, second_new)


def units_from_shard(flat_low, index, count):
    edge = D // count
    block = flat_low.shape[0] - edge
    unit = block // 3
    following = lax.ppermute(flat_low[:D], "seq", [(i + 1, i) for i in range(count - 1)])
    extended = jnp.concatenate([flat_low, following])
    aligned = lax.dynamic_slice(extended, (D - edge * index,), (block,)).reshape(3, unit)
    dealt = jnp.stack(
        [
            lax.ppermute(aligned[j], "seq", [(i, (3 * i + j) % count) for i in range(count)])
            for j in range(3)
        ]
    )
    return [
        lax.dynamic_index_in_dim(dealt, slot_of_kind(index, kind, count), 0, keepdims=False)
        for kind in range(3)
    ]


def slot_of_kind(index, kind, count):
    return (index + count * kind) % 3


def shard_from_units(units, gain_grad, index, count):
    edge = D // count
    stacked = jnp.stack(units)
    unit = stacked.shape[1]
    returned = []
    for j in range(3):
        inverse = 1 if count % 3 == 1 else 2
        kind = ((j - index) * inverse) % 3
        piece = lax.dynamic_index_in_dim(stacked, kind, 0, keepdims=False)
        returned.append(
            lax.ppermute(piece, "seq", [((3 * i + j) % count, i) for i in range(count)])
        )
    block = jnp.concatenate(returned)
    before = lax.ppermute(block[-D:], "seq", [(i, i + 1) for i in range(count - 1)])
    before = jnp.where(index == 0, gain_grad.astype(before.dtype), before)
    extended = jnp.concatenate([before, block])
    return lax.dynamic_slice(extended, (edge * index,), (3 * unit + edge,))


AXES = ("z", "y", "x")
GATHER_ORDERS = (("z", "y", "x"), ("z", "x", "y"), ("y", "x", "z"))


def device_grid(count):
    chips = count // 2
    sides = {16: (4, 2, 2), 64: (4, 4, 4)}.get(chips, (chips, 1, 1))
    return dict(zip(AXES + ("core",), sides + (2,)))


def coordinates(index, grid):
    found = {}
    for axis in reversed(list(grid)):
        found[axis] = index % grid[axis]
        index = index // grid[axis]
    return found


def place(found, grid):
    index = 0
    for axis in grid:
        index = index * grid[axis] + found[axis]
    return index


def shifted(value, axis, steps, grid):
    pairs = []
    for source in range(math.prod(grid.values())):
        target = coordinates(source, grid)
        target[axis] = (target[axis] + steps) % grid[axis]
        pairs.append((source, place(target, grid)))
    return lax.ppermute(value, "seq", pairs)


def slot_table(index, grid, axes):
    here = coordinates(index, grid)
    entries = []
    for number in range(math.prod(grid.values())):
        slots = coordinates(number, {axis: grid[axis] for axis in axes})
        there = {axis: (here[axis] - slots[axis]) % grid[axis] for axis in grid}
        entries.append(place(there, grid))
    return jnp.stack(entries).astype(jnp.int32)


def place_kernel(table_ref, *refs, firsts):
    piece_refs, out_ref = (refs[:-1], refs[-1])
    entry = pl.program_id(0)
    for number, piece_ref in enumerate(piece_refs):

        @pl.when((entry >= firsts[number]) & (entry < firsts[number + 1]))
        def _(piece_ref=piece_ref):
            out_ref[...] = piece_ref[...]


def placed(pieces, table, rows):
    count = table.shape[0]
    width = pieces[0].shape[1]
    firsts = [0]
    for piece in pieces:
        firsts.append(firsts[-1] + piece.shape[0] // rows)

    def block_of(first, last):
        return pl.BlockSpec(
            (rows, width), lambda i, table_ref: (jnp.clip(i, first, last - 1) - first, 0)
        )

    return pl.pallas_call(
        functools.partial(place_kernel, firsts=tuple(firsts)),
        grid_spec=pltpu.PrefetchScalarGridSpec(
            num_scalar_prefetch=1,
            grid=(count,),
            in_specs=[block_of(first, last) for first, last in zip(firsts[:-1], firsts[1:])],
            out_specs=pl.BlockSpec((rows, width), lambda i, table_ref: (table_ref[i], 0)),
        ),
        out_shape=jax.ShapeDtypeStruct((count * rows, width), pieces[0].dtype),
        compiler_params=pltpu.CompilerParams(vmem_limit_bytes=32 << 20),
        cost_estimate=pl.CostEstimate(
            flops=0, transcendentals=0, bytes_accessed=4 * count * rows * width
        ),
        name="place_blocks",
    )(table, *pieces)


def gather_rows(block, order, index, grid):
    rows = block.shape[0]
    held = block
    for axis in order:
        arrivals = [held]
        for _ in range(grid[axis] - 1):
            arrivals.append(shifted(arrivals[-1], axis, 1, grid))
        if axis != order[-1]:
            held = jnp.concatenate(arrivals)
    pieces = arrivals + [shifted(piece, "core", 1, grid) for piece in arrivals]
    table = slot_table(index, grid, ("core",) + tuple(reversed(order)))
    return placed(pieces, table, rows)


def reorder_kernel(table_ref, in_ref, out_ref, *, rows):
    for block in range(in_ref.shape[0] // rows):
        source = pl.ds(pl.multiple_of(table_ref[block] * rows, rows), rows)
        out_ref[block * rows : (block + 1) * rows, :] = in_ref[source, :]


def reordered(value, table):
    rows = value.shape[0] // table.shape[0]
    return pl.pallas_call(
        functools.partial(reorder_kernel, rows=rows),
        grid_spec=pltpu.PrefetchScalarGridSpec(
            num_scalar_prefetch=1,
            grid=(1,),
            in_specs=[whole_spec(value)],
            out_specs=whole_spec(value),
        ),
        out_shape=jax.ShapeDtypeStruct(value.shape, value.dtype),
        cost_estimate=pl.CostEstimate(
            flops=0, transcendentals=0, bytes_accessed=4 * value.size
        ),
        name="reorder_blocks",
    )(table, value)


def summed(value, grid):
    for axis in reversed(list(grid)):
        own = value
        for _ in range(grid[axis] - 1):
            value = own + shifted(value, axis, 1, grid)
    return value


def sum_scatter(left_cols, right, right_dim, order, index, grid):
    count = math.prod(grid.values())
    rows = left_cols.shape[0] // count
    order = ("core",) + tuple(reversed(order))
    left = reordered(left_cols, slot_table(index, grid, order))
    received = []

    def partial(first, last):
        span = slice(first * rows, last * rows)
        total = contract(left[span], 1, right, right_dim)
        for part in received:
            total = total + part[span]
        return total

    window = count
    for axis in order:
        window = window // grid[axis]
        passing = None
        for slot in range(grid[axis] - 1, 0, -1):
            own = partial(slot * window, (slot + 1) * window)
            total = own if passing is None else own + passing
            passing = shifted(total.astype(jnp.bfloat16), axis, -1, grid)
        if passing is not None:
            received.append(passing)
    return partial(0, 1)


def live_pairs(rel_ref, pos, start, base, queries):
    rel = rel_ref[...]
    rel = jnp.concatenate([rel] * (queries // rel.shape[1]), axis=1)
    return (rel >= start - base) & (rel <= pos - base)


def forward_kernel(
    low_ref, high_ref, query_ref, key_ref, value_ref, pos_ref, start_ref, rel_ref, out_ref, lse_ref
):
    tile = pl.program_id(0)
    query_cols = query_ref[0]
    queries = query_cols.shape[1]
    keys = rel_ref.shape[0]
    pos = pos_ref[0]
    start = start_ref[0]

    def body(step, carried):
        run_max, run_total, mixed = carried
        rows = pl.ds(pl.multiple_of(step * keys, keys), keys)
        scores = contract(key_ref[rows, :], 1, query_cols, 0)
        live = live_pairs(rel_ref, pos, start, step * keys, queries)
        scores = jnp.where(live, scores, NEG_LARGE)
        new_max = jnp.maximum(run_max, jnp.max(scores, axis=0, keepdims=True))
        weights = jnp.exp2((scores - new_max) * SCORE_BASE_TWO)
        keep = jnp.exp2((run_max - new_max) * SCORE_BASE_TWO)
        run_total = run_total * keep + jnp.sum(weights, axis=0, keepdims=True)
        mixed = mixed * keep + contract(value_ref[step], 1, weights.astype(jnp.bfloat16), 0)
        return (new_max, run_total, mixed)

    start_state = (
        jnp.full((1, queries), NEG_LARGE, jnp.float32),
        jnp.zeros((1, queries), jnp.float32),
        jnp.zeros((HEAD_DIM, queries), jnp.float32),
    )
    run_max, run_total, mixed = lax.fori_loop(low_ref[tile], high_ref[tile], body, start_state)
    out_ref[0] = mixed / run_total
    lse_ref[0] = run_max * SCORE_BASE_TWO + jnp.log2(run_total)


def backward_kernel(
    low_ref,
    high_ref,
    query_ref,
    query_row_ref,
    dout_ref,
    dout_row_ref,
    out_ref,
    lse_ref,
    key_ref,
    key_col_ref,
    value_ref,
    pos_ref,
    start_ref,
    rel_ref,
    dquery_ref,
    dkey_ref,
    dvalue_ref,
):
    tile = pl.program_id(0)

    @pl.when(tile == 0)
    def _():
        dkey_ref[...] = jnp.zeros_like(dkey_ref)
        dvalue_ref[...] = jnp.zeros_like(dvalue_ref)

    query_cols = query_ref[0]
    query_rows = query_row_ref[0]
    dout_cols = dout_ref[0]
    dout_rows = dout_row_ref[0]
    queries = query_cols.shape[1]
    keys = rel_ref.shape[0]
    pos = pos_ref[0]
    start = start_ref[0]
    lse = lse_ref[0]
    delta = jnp.sum(dout_cols.astype(jnp.float32) * out_ref[0], axis=0, keepdims=True)

    def body(step, dquery):
        rows = pl.ds(pl.multiple_of(step * keys, keys), keys)
        scores = contract(key_ref[rows, :], 1, query_cols, 0)
        live = live_pairs(rel_ref, pos, start, step * keys, queries)
        weights = jnp.where(live, jnp.exp2(scores * SCORE_BASE_TWO - lse), 0.0)
        weight_grad = contract(value_ref[rows, :], 1, dout_cols, 0)
        dscore = (weights * (weight_grad - delta)).astype(jnp.bfloat16)
        dvalue_ref[rows, :] += contract(weights.astype(jnp.bfloat16), 1, dout_rows, 0)
        dkey_ref[rows, :] += contract(dscore, 1, query_rows, 0)
        return dquery + contract(key_col_ref[step], 1, dscore, 0)

    dquery = lax.fori_loop(
        low_ref[tile], high_ref[tile], body, jnp.zeros((HEAD_DIM, queries), jnp.float32)
    )
    dquery_ref[0] = dquery * SCORE_SCALE

    @pl.when(tile == pl.num_programs(0) - 1)
    def _():
        dkey_ref[...] = dkey_ref[...] * SCORE_SCALE


def whole_spec(array):
    return pl.BlockSpec(array.shape, lambda i, *_: (0,) * array.ndim)


def tile_spec(array):
    return pl.BlockSpec((1,) + array.shape[1:], lambda i, *_: (i,) + (0,) * (array.ndim - 1))


def run_kernel(body, name, bounds, inputs, outputs, flops):
    spec = lambda item: tile_spec(item[0]) if item[1] else whole_spec(item[0])
    grid = next(array.shape[0] for array, cut in inputs if cut)
    return pl.pallas_call(
        body,
        grid_spec=pltpu.PrefetchScalarGridSpec(
            num_scalar_prefetch=2,
            grid=(grid,),
            in_specs=[spec(item) for item in inputs],
            out_specs=[spec(item) for item in outputs],
        ),
        out_shape=[item[0] for item in outputs],
        compiler_params=pltpu.CompilerParams(vmem_limit_bytes=52 << 20),
        cost_estimate=pl.CostEstimate(
            flops=flops, transcendentals=flops // 400, bytes_accessed=16 << 20
        ),
        name=name,
    )(*bounds, *[item[0] for item in inputs])


def attend(query_cols, key_rows, value_cols, pos, start, rel, low, high):
    tiles, _, queries = query_cols.shape
    return run_kernel(
        forward_kernel,
        "attention_forward",
        (low, high),
        [
            (query_cols, True),
            (key_rows, False),
            (value_cols, False),
            (pos, True),
            (start, True),
            (rel, False),
        ],
        [
            (jax.ShapeDtypeStruct((tiles, HEAD_DIM, queries), jnp.float32), True),
            (jax.ShapeDtypeStruct((tiles, 1, queries), jnp.float32), True),
        ],
        20_000_000_000,
    )


def attend_back(
    query_cols, dout_cols, out_cols, lse, key_rows, key_cols, value_rows, pos, start, rel, low, high
):
    tiles, _, queries = query_cols.shape
    grads = jax.ShapeDtypeStruct(key_rows.shape, jnp.float32)
    return run_kernel(
        backward_kernel,
        "attention_backward",
        (low, high),
        [
            (query_cols, True),
            (jnp.swapaxes(query_cols, 1, 2), True),
            (dout_cols, True),
            (jnp.swapaxes(dout_cols, 1, 2), True),
            (out_cols, True),
            (lse, True),
            (key_rows, False),
            (key_cols, False),
            (value_rows, False),
            (pos, True),
            (start, True),
            (rel, False),
        ],
        [
            (jax.ShapeDtypeStruct((tiles, HEAD_DIM, queries), jnp.float32), True),
            (grads, False),
            (grads, False),
        ],
        50_000_000_000,
    )


def per_device(
    tokens,
    segment_ids,
    out_grad,
    attn_master,
    attn_first,
    attn_second,
    ffn_master,
    ffn_first,
    ffn_second,
):
    index = lax.axis_index("seq")
    count = lax.axis_size("seq")
    rows = tokens.shape[0]
    total = rows * count
    group = count // KV_HEADS
    parts = group // 2
    span = rows // parts
    half = (index // parts) % 2
    part = index % parts

    def exchange(value):
        return lax.all_to_all(value, "seq", 0, 0, tiled=True)

    def swapped(value, bit):
        return lax.ppermute(value, "seq", [(i, i ^ bit) for i in range(count)])

    attn_low = attn_master.astype(jnp.bfloat16)
    ffn_low = ffn_master.astype(jnp.bfloat16)
    notice = jnp.concatenate(
        [attn_low[:D], ffn_low[:D], segment_ids.astype(jnp.bfloat16)]
    ).reshape(1, -1, 128)
    notices = exchange(jnp.broadcast_to(notice, (count,) + notice.shape[1:]))
    gains = notices[0, : 2 * D // 128].astype(jnp.float32).reshape(2, D)
    gain_one, gain_two = (gains[0], gains[1])
    all_ids = notices[:, 2 * D // 128 :].astype(jnp.int32).reshape(-1)

    grid = device_grid(count)
    by_axes = (D // count) % 16 == 0

    def gathered(unit, width, color):
        block = unit.reshape(-1, width)
        if by_axes:
            return gather_rows(block, GATHER_ORDERS[color], index, grid)
        return lax.all_gather(block, "seq", axis=0, tiled=True)

    def scattered(left_cols, right, right_dim, color):
        if by_axes:
            return sum_scatter(
                left_cols, right, right_dim, GATHER_ORDERS[color], index, grid
            ).reshape(-1)
        whole = contract(left_cols, 1, right, right_dim).astype(jnp.bfloat16)
        return (
            lax.psum_scatter(whole, "seq", scatter_dimension=0, tiled=True)
            .reshape(-1)
            .astype(jnp.float32)
        )

    q_unit, kv_unit, o_unit = units_from_shard(attn_low, index, count)
    gate_unit, up_unit, down_unit = units_from_shard(ffn_low, index, count)
    query_weight = gathered(q_unit, HEADS * HEAD_DIM, 0)
    key_value_weight = gathered(kv_unit, KV_HEADS * HEAD_DIM, 1)
    key_weight, value_weight = (key_value_weight[:D], key_value_weight[D:])
    out_weight = gathered(o_unit, D, 2)
    gate_weight = gathered(gate_unit, FF, 0)
    up_weight = gathered(up_unit, FF, 1)
    down_weight = gathered(down_unit, D, 2)

    def item_starts(ids):
        return jnp.sum((all_ids < ids[..., None]).astype(jnp.int32), axis=-1)

    inputs = tokens.astype(jnp.float32)
    normed_one = rms_norm(inputs, gain_one).astype(jnp.bfloat16)
    own_places = index * rows + jnp.arange(rows, dtype=jnp.int32)
    own_cos, own_sin = angle_tables(own_places)
    query_pre = contract(query_weight, 0, normed_one, 1).reshape(HEADS, HEAD_DIM, rows)
    key_pre = contract(key_weight, 0, normed_one, 1).reshape(KV_HEADS, HEAD_DIM, rows)
    value_low = (
        contract(value_weight, 0, normed_one, 1)
        .astype(jnp.bfloat16)
        .reshape(KV_HEADS, HEAD_DIM, rows)
    )
    query_low = rotate(query_pre, own_cos, own_sin).astype(jnp.bfloat16)
    key_low = rotate(key_pre, own_cos, own_sin).astype(jnp.bfloat16)

    def by_owner(value):
        pieces = value.reshape(HEADS, HEAD_DIM, parts, span)
        return jnp.swapaxes(pieces, 1, 2).reshape(count, HEAD_DIM, span)

    def by_head(value):
        pieces = value.reshape(HEADS, parts, HEAD_DIM, span)
        return jnp.swapaxes(pieces, 1, 2).reshape(HEADS, HEAD_DIM, rows)

    def paired(key_part, value_part):
        return jnp.stack([key_part, value_part], axis=1).reshape(HEADS, HEAD_DIM, rows)

    received = exchange(
        jnp.concatenate([by_owner(query_low), by_owner(paired(key_low, value_low))], axis=1)
    )

    sources = QUERY_TILE // span
    tiles = count // sources

    def to_tiles(value):
        pieces = value.reshape(tiles, sources, value.shape[1], span)
        return jnp.swapaxes(pieces, 1, 2).reshape(tiles, value.shape[1], QUERY_TILE)

    def from_tiles(value):
        pieces = value.reshape(tiles, value.shape[1], sources, span)
        return jnp.swapaxes(pieces, 1, 2).reshape(count, value.shape[1], span)

    query_cols = to_tiles(received[:, :HEAD_DIM])
    own_kind = received[:, HEAD_DIM:]
    other_kind = swapped(own_kind, parts)
    pair = jnp.stack(
        [
            jnp.where(half == 0, own_kind, other_kind),
            jnp.where(half == 0, other_kind, own_kind),
        ]
    )[:, None]
    bit = 1
    while bit < parts:
        pair = jnp.concatenate([pair, swapped(pair, bit)], axis=1)
        bit = bit * 2
    key_all, value_all = (pair[0], pair[1])
    devices_per_tile = KEY_TILE // rows
    key_tiles = count // devices_per_tile

    def key_columns(value):
        pieces = value.reshape(parts, key_tiles, devices_per_tile, HEAD_DIM, span)
        return jnp.transpose(pieces, (1, 3, 2, 0, 4)).reshape(key_tiles, HEAD_DIM, KEY_TILE)

    def key_rows_of(value):
        return jnp.transpose(value, (1, 0, 3, 2)).reshape(total, HEAD_DIM)

    key_cols = key_columns(key_all)
    value_cols = key_columns(value_all)
    key_rows = key_rows_of(key_all)
    value_rows = key_rows_of(value_all)
    slot_parts = part ^ jnp.arange(parts, dtype=jnp.int32)
    within = jnp.arange(span, dtype=jnp.int32)
    rel = (
        rows * jnp.arange(devices_per_tile, dtype=jnp.int32)[:, None, None]
        + span * slot_parts[None, :, None]
        + within[None, None, :]
    ).reshape(KEY_TILE, 1)
    rel = jnp.broadcast_to(rel, (KEY_TILE, 128))
    held_places = (
        rows * jnp.arange(count, dtype=jnp.int32)[:, None] + span * part + within[None, :]
    )
    held_ids = lax.dynamic_index_in_dim(
        all_ids.reshape(count, parts, span), part, 1, keepdims=False
    )
    held_starts = item_starts(held_ids.reshape(-1))
    pos = held_places.reshape(tiles, 1, QUERY_TILE)
    start = held_starts.reshape(tiles, 1, QUERY_TILE)
    tile_span = sources * rows
    low = item_starts(all_ids[::tile_span]) // KEY_TILE
    high = (jnp.arange(1, tiles + 1, dtype=jnp.int32) * tile_span + KEY_TILE - 1) // KEY_TILE

    chunks = []
    chunk = min(CHUNK, total)
    for first in range(0, total, chunk):
        first_key = max(0, first - SEG_MOST) // KEY_TILE
        last_key = (first + chunk) // KEY_TILE
        chunks.append(
            (
                slice(first // tile_span, (first + chunk) // tile_span),
                slice(first_key, last_key),
                slice(first_key * KEY_TILE, last_key * KEY_TILE),
            )
        )

    pieces = []
    for of_tiles, of_key_tiles, of_keys in chunks:
        shift = of_key_tiles.start * KEY_TILE
        pieces.append(
            attend(
                query_cols[of_tiles],
                key_rows[of_keys],
                value_cols[of_key_tiles],
                pos[of_tiles] - shift,
                start[of_tiles] - shift,
                rel,
                low[of_tiles] - of_key_tiles.start,
                high[of_tiles] - of_key_tiles.start,
            )
        )
    out_cols = jnp.concatenate([piece[0] for piece in pieces])
    lse = jnp.concatenate([piece[1] for piece in pieces])

    mixed_low = by_head(exchange(from_tiles(out_cols.astype(jnp.bfloat16)))).reshape(
        HEADS * HEAD_DIM, rows
    )

    middle = inputs + contract(mixed_low, 0, out_weight, 0)
    normed_two = rms_norm(middle, gain_two).astype(jnp.bfloat16)
    gate_rows = contract(normed_two, 1, gate_weight, 0)
    up_rows = contract(normed_two, 1, up_weight, 0)
    hidden = (jax.nn.silu(gate_rows) * up_rows).astype(jnp.bfloat16)
    result = (middle + contract(hidden, 1, down_weight, 0)).astype(jnp.bfloat16)
    hidden_grad = contract(out_grad, 1, down_weight, 1)
    sigma_gate = jax.nn.sigmoid(gate_rows)
    silu_gate = gate_rows * sigma_gate
    gate_grad = (
        hidden_grad * up_rows * sigma_gate * (1.0 + gate_rows * (1.0 - sigma_gate))
    ).astype(jnp.bfloat16)
    up_grad = (hidden_grad * silu_gate).astype(jnp.bfloat16)
    normed_two_grad = contract(gate_grad, 1, gate_weight, 1) + contract(up_grad, 1, up_weight, 1)
    _, norm_pull = jax.vjp(rms_norm, middle, gain_two)
    middle_norm_grad, grad_two = norm_pull(normed_two_grad)
    middle_grad = out_grad.astype(jnp.float32) + middle_norm_grad
    middle_low = middle_grad.astype(jnp.bfloat16)

    dout_cols = to_tiles(
        exchange(
            by_owner(
                contract(out_weight, 1, middle_low, 1)
                .astype(jnp.bfloat16)
                .reshape(HEADS, HEAD_DIM, rows)
            )
        )
    )
    normed_two_cols = normed_two.T
    ffn_units = [
        scattered(normed_two_cols, gate_grad, 0, 0),
        scattered(normed_two_cols, up_grad, 0, 1),
        scattered(hidden.T, out_grad, 0, 2),
    ]
    out_unit = scattered(mixed_low, middle_low, 0, 2)

    pieces = []
    dkey_rows = jnp.zeros((total, HEAD_DIM), jnp.float32)
    dvalue_rows = jnp.zeros((total, HEAD_DIM), jnp.float32)
    for of_tiles, of_key_tiles, of_keys in chunks:
        shift = of_key_tiles.start * KEY_TILE
        dquery_piece, dkey_piece, dvalue_piece = attend_back(
            query_cols[of_tiles],
            dout_cols[of_tiles],
            out_cols[of_tiles],
            lse[of_tiles],
            key_rows[of_keys],
            key_cols[of_key_tiles],
            value_rows[of_keys],
            pos[of_tiles] - shift,
            start[of_tiles] - shift,
            rel,
            low[of_tiles] - of_key_tiles.start,
            high[of_tiles] - of_key_tiles.start,
        )
        pieces.append(dquery_piece)
        if len(chunks) == 1:
            dkey_rows, dvalue_rows = (dkey_piece, dvalue_piece)
        else:
            dkey_rows = dkey_rows.at[of_keys].add(dkey_piece)
            dvalue_rows = dvalue_rows.at[of_keys].add(dvalue_piece)
    dquery_rot = from_tiles(jnp.concatenate(pieces))
    held_cos, held_sin = angle_tables(held_places)
    dquery_held = rotate(dquery_rot, held_cos, -held_sin).astype(jnp.bfloat16)

    def by_slot(value):
        return jnp.transpose(value.reshape(count, parts, span, HEAD_DIM), (1, 0, 3, 2))

    grads = jnp.stack([by_slot(dkey_rows), by_slot(dvalue_rows)])
    bit = parts // 2
    while bit >= 1:
        grads = grads[:, :bit] + swapped(grads[:, bit:].astype(jnp.bfloat16), bit)
        bit = bit // 2
    dkey_held, dvalue_held = (grads[0, 0], grads[1, 0])
    sent_kind = jnp.where(half == 0, dvalue_held, dkey_held).astype(jnp.bfloat16)
    kept_kind = jnp.where(half == 0, dkey_held, dvalue_held) + swapped(sent_kind, parts)
    kept_low = jnp.where(half == 0, rotate(kept_kind, held_cos, -held_sin), kept_kind).astype(
        jnp.bfloat16
    )
    returned = exchange(jnp.concatenate([dquery_held, kept_low], axis=1))
    dquery_low = by_head(returned[:, :HEAD_DIM]).reshape(HEADS * HEAD_DIM, rows)
    pair_low = by_head(returned[:, HEAD_DIM:]).reshape(KV_HEADS, 2, HEAD_DIM, rows)
    dkey_low = pair_low[:, 0].reshape(KV_HEADS * HEAD_DIM, rows)
    dvalue_low = pair_low[:, 1].reshape(KV_HEADS * HEAD_DIM, rows)

    normed_one_cols = normed_one.T
    query_unit = scattered(normed_one_cols, dquery_low, 1, 0)
    nothing = jnp.zeros_like(normed_one_cols)
    key_value_cols = jnp.concatenate(
        [
            jnp.concatenate([normed_one_cols, nothing], axis=1),
            jnp.concatenate([nothing, normed_one_cols], axis=1),
        ]
    )
    key_value_unit = scattered(
        key_value_cols, jnp.concatenate([dkey_low, dvalue_low], axis=1), 1, 1
    )
    normed_one_grad = (
        contract(dquery_low, 0, query_weight, 1)
        + contract(dkey_low, 0, key_weight, 1)
        + contract(dvalue_low, 0, value_weight, 1)
    )
    _, first_pull = jax.vjp(rms_norm, inputs, gain_one)
    input_norm_grad, grad_one = first_pull(normed_one_grad)
    input_grad = middle_grad + input_norm_grad

    gain_grads = summed(jnp.stack([grad_one, grad_two]).reshape(-1, 128), grid).reshape(2, D)
    attn_shard = shard_from_units(
        [query_unit, key_value_unit, out_unit], gain_grads[0], index, count
    )
    ffn_shard = shard_from_units(ffn_units, gain_grads[1], index, count)
    attn_new, attn_one, attn_two = adam_update(
        attn_master, attn_first, attn_second, attn_shard
    )
    ffn_new, ffn_one, ffn_two = adam_update(
        ffn_master, ffn_first, ffn_second, ffn_shard
    )
    return (result, input_grad, attn_new, attn_one, attn_two, ffn_new, ffn_one, ffn_two)


def solution(mesh):
    rows_cut = P("seq", None)
    flat_cut = P("seq")
    in_specs = (rows_cut, flat_cut, rows_cut) + (flat_cut,) * 6
    out_specs = (rows_cut, rows_cut) + (flat_cut,) * 6
    return jax.shard_map(
        per_device, mesh=mesh, in_specs=in_specs, out_specs=out_specs, check_vma=False
    )
```

```python
import functools
import math

import jax
import jax.numpy as jnp
from jax import lax
from jax.experimental import pallas as pl
from jax.experimental.pallas import tpu as pltpu
from jax.sharding import PartitionSpec as P

D = 1536
HEADS = 16
KV_HEADS = 8
HEAD_DIM = 96
FF = 4096
SEG_MOST = 4096
STEP = 7


ROPE_BASE = 100000.0
NORM_EPS = 1e-05
BETA_ONE = 0.5
BETA_TWO = 0.5
LEARN_RATE = 0.04
DECAY = 0.1
ADAM_EPS = 1e-08
NEG_LARGE = -1e30
HALF_DIM = HEAD_DIM // 2
QUERY_TILE = 512
KEY_TILE = 1024
CHUNK = 8192
FF_TILE = 512
SCORE_BASE_TWO = math.log2(math.e) / math.sqrt(HEAD_DIM)
SCORE_SCALE = 1.0 / math.sqrt(HEAD_DIM)


def rms_norm(values, norm_gain):
    factor = lax.rsqrt(jnp.mean(values * values, axis=-1, keepdims=True) + NORM_EPS)
    return values * factor * norm_gain


def angle_tables(positions):
    frequency = jnp.exp(
        jnp.arange(HALF_DIM).astype(jnp.float32) * (-2.0 * math.log(ROPE_BASE) / HEAD_DIM)
    )
    angles = positions.astype(jnp.float32)[..., None, :] * frequency[:, None]
    return (jnp.cos(angles), jnp.sin(angles))


def rotate(values, cosine, sine_part):
    lower_part = values[..., :HALF_DIM, :]
    upper_part = values[..., HALF_DIM:, :]
    return jnp.concatenate(
        [
            lower_part * cosine - upper_part * sine_part,
            upper_part * cosine + lower_part * sine_part,
        ],
        axis=-2,
    )


def contract(left, left_dim, right, right_dim):
    return lax.dot_general(
        left,
        right,
        (((left_dim,), (right_dim,)), ((), ())),
        preferred_element_type=jnp.float32,
    )


def adam_update(master, moment_one, moment_two, gradient):
    first_new = BETA_ONE * moment_one + (1.0 - BETA_ONE) * gradient
    second_new = BETA_TWO * moment_two + (1.0 - BETA_TWO) * gradient * gradient
    first_hat = first_new / (1.0 - BETA_ONE**STEP)
    second_hat = second_new / (1.0 - BETA_TWO**STEP)
    master_new = master - LEARN_RATE * (
        first_hat / (jnp.sqrt(second_hat) + ADAM_EPS) + DECAY * master
    )
    return (master_new, first_new, second_new)


def aligned_block(flat_low, index, count):
    edge = D // count
    block = flat_low.shape[0] - edge
    following = lax.ppermute(flat_low[:D], "seq", [(i + 1, i) for i in range(count - 1)])
    extended = jnp.concatenate([flat_low, following])
    return lax.dynamic_slice(extended, (D - edge * index,), (block,))


def tiles_of(unit, width):
    pieces = unit.reshape(-1, 8, width // 128, 128)
    return jnp.swapaxes(pieces, 1, 2).reshape(-1, 8, 128)


def matrix_of(tiles, width):
    pieces = tiles.reshape(-1, width // 128, 8, 128)
    return jnp.swapaxes(pieces, 1, 2).reshape(-1, width)


def unit_tiles(block, widths, index, count):
    units = block.reshape(3, -1)
    made = []
    for j in range(3):
        kind = (3 * index + j) // count
        made.append(
            lax.select_n(kind, *[tiles_of(units[j], width) for width in widths])
        )
    return jnp.concatenate(made)


def units_from_block(block, index, count):
    aligned = block.reshape(3, -1)
    dealt = jnp.stack(
        [
            lax.ppermute(aligned[j], "seq", [(i, (3 * i + j) % count) for i in range(count)])
            for j in range(3)
        ]
    )
    return [
        lax.dynamic_index_in_dim(dealt, slot_of_kind(index, kind, count), 0, keepdims=False)
        for kind in range(3)
    ]


def slot_of_kind(index, kind, count):
    return (index + count * kind) % 3


def shard_from_units(units, gain_grad, index, count):
    edge = D // count
    units = [unit.astype(jnp.bfloat16) for unit in units]
    unit = units[0].shape[0]
    returned = []
    for j in range(3):
        inverse = 1 if count % 3 == 1 else 2
        kind = ((j - index) * inverse) % 3
        piece = jnp.where(kind == 0, units[0], jnp.where(kind == 1, units[1], units[2]))
        returned.append(
            lax.ppermute(piece, "seq", [((3 * i + j) % count, i) for i in range(count)])
        )
    before = lax.ppermute(returned[2][-D:], "seq", [(i, i + 1) for i in range(count - 1)])
    before = jnp.where(index == 0, gain_grad, before.astype(jnp.float32))
    extended = jnp.concatenate([before] + [piece.astype(jnp.float32) for piece in returned])
    return lax.dynamic_slice(extended, (edge * index,), (3 * unit + edge,))


AXES = ("z", "y", "x")
GATHER_ORDERS = (("core", "x", "y", "z"), ("core", "y", "x", "z"))
GATE_ORDER = ("core", "x", "z", "y")
UP_ORDER = ("core", "y", "z", "x")
DOWN_ORDER = ("core", "x", "y", "z")
OUT_ORDER = ("core", "y", "x", "z")


def device_grid(count):
    chips = count // 2
    sides = {16: (4, 2, 2), 64: (4, 4, 4)}.get(chips, (chips, 1, 1))
    return dict(zip(AXES + ("core",), sides + (2,)))


def coordinates(index, grid):
    found = {}
    for axis in reversed(list(grid)):
        found[axis] = index % grid[axis]
        index = index // grid[axis]
    return found


def place(found, grid):
    index = 0
    for axis in grid:
        index = index * grid[axis] + found[axis]
    return index


def shifted(value, axis, steps, grid):
    pairs = []
    for source in range(math.prod(grid.values())):
        target = coordinates(source, grid)
        target[axis] = (target[axis] + steps) % grid[axis]
        pairs.append((source, place(target, grid)))
    return lax.ppermute(value, "seq", pairs)


def slot_table(index, grid, axes):
    here = coordinates(index, grid)
    entries = []
    for number in range(math.prod(grid.values())):
        slots = coordinates(number, {axis: grid[axis] for axis in axes})
        there = {axis: (here[axis] - slots[axis]) % grid[axis] for axis in grid}
        entries.append(place(there, grid))
    return jnp.stack(entries).astype(jnp.int32)


def place_kernel(table_ref, *refs, lengths):
    pieces = len(lengths)
    piece_refs, out_ref = (refs[:pieces], refs[pieces])
    held, in_sems, out_sems = refs[pieces + 1 :]
    size = held.shape[1]
    loads = []
    for piece_ref, length in zip(piece_refs, lengths):
        for block in range(length):
            entry = len(loads)
            load = pltpu.make_async_copy(
                piece_ref.at[pl.ds(block * size, size)], held.at[entry], in_sems.at[entry]
            )
            load.start()
            loads.append(load)
    stores = []
    for entry, load in enumerate(loads):
        load.wait()
        target = pl.ds(pl.multiple_of(table_ref[entry] * size, size), size)
        store = pltpu.make_async_copy(held.at[entry], out_ref.at[target], out_sems.at[entry])
        store.start()
        stores.append(store)
    for store in stores:
        store.wait()


def placed(pieces, table):
    count = table.shape[0]
    size = sum(piece.shape[0] for piece in pieces) // count
    shape = pieces[0].shape[1:]
    anywhere = pl.BlockSpec(memory_space=pl.ANY)
    return pl.pallas_call(
        functools.partial(
            place_kernel, lengths=tuple(piece.shape[0] // size for piece in pieces)
        ),
        grid_spec=pltpu.PrefetchScalarGridSpec(
            num_scalar_prefetch=1,
            grid=(1,),
            in_specs=[anywhere] * len(pieces),
            out_specs=anywhere,
            scratch_shapes=[
                pltpu.VMEM((count, size) + shape, pieces[0].dtype),
                pltpu.SemaphoreType.DMA((count,)),
                pltpu.SemaphoreType.DMA((count,)),
            ],
        ),
        out_shape=jax.ShapeDtypeStruct((count * size,) + shape, pieces[0].dtype),
        compiler_params=pltpu.CompilerParams(vmem_limit_bytes=48 << 20),
        cost_estimate=pl.CostEstimate(
            flops=0, transcendentals=0, bytes_accessed=4 * count * size * math.prod(shape)
        ),
        name="place_blocks",
    )(table, *pieces)


def gather_tiles(block, index, grid, notices, later, beside_of):
    arrived = [block] + [shifted(block, "z", k, grid) for k in range(1, grid["z"])]
    arrived, notices = together(arrived, notices)
    beside = beside_of(notices)
    half = block.shape[0] // 2
    held = [
        jnp.concatenate([each[color * half : (color + 1) * half] for each in arrived])
        for color in range(2)
    ]
    for turn in (2, 1):
        arrivals = []
        for color, order in enumerate(GATHER_ORDERS):
            axis = order[turn]
            arrivals.append(
                [held[color]]
                + [shifted(held[color], axis, k, grid) for k in range(1, grid[axis])]
            )
        if turn == 1:
            arrivals, beside = together(arrivals, beside)
        else:
            arrivals, later = together(arrivals, later)
            held = [jnp.concatenate(each) for each in arrivals]
    pieces = []
    tables = []
    for color, order in enumerate(GATHER_ORDERS):
        pieces = pieces + arrivals[color]
        pieces = pieces + [shifted(piece, "core", 1, grid) for piece in arrivals[color]]
        tables.append(2 * slot_table(index, grid, order) + color)
    return placed(pieces, jnp.concatenate(tables)), later, beside


def reorder_kernel(table_ref, in_ref, out_ref, *, rows):
    for block in range(in_ref.shape[0] // rows):
        source = pl.ds(pl.multiple_of(table_ref[block] * rows, rows), rows)
        out_ref[block * rows : (block + 1) * rows, :] = in_ref[source, :]


def reordered(value, table):
    rows = value.shape[0] // table.shape[0]
    return pl.pallas_call(
        functools.partial(reorder_kernel, rows=rows),
        grid_spec=pltpu.PrefetchScalarGridSpec(
            num_scalar_prefetch=1,
            grid=(1,),
            in_specs=[whole_spec(value)],
            out_specs=whole_spec(value),
        ),
        out_shape=jax.ShapeDtypeStruct(value.shape, value.dtype),
        cost_estimate=pl.CostEstimate(
            flops=0, transcendentals=0, bytes_accessed=4 * value.size
        ),
        name="reorder_blocks",
    )(table, value)


class SummedRows:

    def __init__(self, left, right, right_dim, order, grid):
        self.left = left
        self.right = right
        self.right_dim = right_dim
        self.grid = grid
        self.rows = left.shape[0] // math.prod(grid.values())
        self.window = left.shape[0]
        self.turns = [(axis, slot) for axis in order for slot in range(grid[axis] - 1, 0, -1)]
        self.received = []
        self.passing = []

    def partial(self, span):
        total = contract(self.left[span], 1, self.right, self.right_dim)
        for part in self.received:
            total = total + part[span]
        return total

    def make(self):
        axis, slot = self.turns[0]
        if slot == self.grid[axis] - 1:
            self.window = self.window // self.grid[axis]
        total = self.partial(slice(slot * self.window, (slot + 1) * self.window))
        for part in self.passing:
            total = total + part
        self.made = total.astype(jnp.bfloat16)

    def send(self):
        axis, slot = self.turns.pop(0)
        arrived = [shifted(self.made, axis, -1, self.grid)]
        if slot > 1:
            self.passing = arrived
        else:
            self.passing = []
            self.received = self.received + arrived

    def result(self):
        return self.partial(slice(0, self.rows)).reshape(-1)


def together(values, others):
    return lax.optimization_barrier((values, others))


def made_before(sums, value):
    for each in sums:
        each.make()
    value, made = together(value, [each.made for each in sums])
    for each, now in zip(sums, made):
        each.made = now
    return value


def taken_after(sums, value):
    value, arrived = together(value, [(each.received, each.passing) for each in sums])
    for each, now in zip(sums, arrived):
        each.received, each.passing = now
    return value


def one_round(sums):
    taken_after(sums, ())
    make_and_send(sums)


def make_and_send(sums):
    for each in sums:
        each.make()
        each.send()


def feed_forward_kernel(
    tokens_ref,
    mixed_piece_ref,
    gain_ref,
    out_grad_ref,
    out_weight_ref,
    gate_weight_ref,
    up_weight_ref,
    down_weight_ref,
    result_ref,
    middle_grad_ref,
    middle_low_ref,
    dout_piece_ref,
    gain_grad_ref,
    gate_grad_ref,
    up_grad_ref,
    hidden_col_ref,
    normed_col_ref,
    mixed_col_ref,
    middle_ref,
    normed_ref,
    total_ref,
    normed_grad_ref,
):
    step = pl.program_id(0)
    pieces, _, cols = mixed_piece_ref.shape
    per_head = pieces // HEADS

    def factor_of(middle):
        return lax.rsqrt(jnp.mean(middle * middle, axis=-1, keepdims=True) + NORM_EPS)

    def place_of(piece):
        head, part = divmod(piece, per_head)
        return (slice(head * HEAD_DIM, (head + 1) * HEAD_DIM), slice(part * cols, (part + 1) * cols))

    @pl.when(step == 0)
    def _():
        for piece in range(pieces):
            mixed_col_ref[place_of(piece)] = mixed_piece_ref[piece]
        middle = tokens_ref[...].astype(jnp.float32) + contract(
            mixed_col_ref[...].T, 1, out_weight_ref[...], 0
        )
        middle_ref[...] = middle
        normed = (middle * factor_of(middle) * gain_ref[...]).astype(jnp.bfloat16)
        normed_ref[...] = normed
        normed_col_ref[...] = normed.T
        total_ref[...] = jnp.zeros_like(total_ref)
        normed_grad_ref[...] = jnp.zeros_like(normed_grad_ref)

    normed = normed_ref[...]
    gate_weight = gate_weight_ref[...]
    up_weight = up_weight_ref[...]
    down_weight = down_weight_ref[...]
    gate = contract(normed, 1, gate_weight, 0)
    up = contract(normed, 1, up_weight, 0)
    sigma = jax.nn.sigmoid(gate)
    silu = gate * sigma
    hidden = (silu * up).astype(jnp.bfloat16)
    hidden_col_ref[...] = hidden.T
    total_ref[...] += contract(hidden, 1, down_weight, 0)
    hidden_grad = contract(out_grad_ref[...], 1, down_weight, 1)
    gate_grad = (hidden_grad * up * sigma * (1.0 + gate * (1.0 - sigma))).astype(jnp.bfloat16)
    up_grad = (hidden_grad * silu).astype(jnp.bfloat16)
    gate_grad_ref[...] = gate_grad
    up_grad_ref[...] = up_grad
    normed_grad_ref[...] += contract(gate_grad, 1, gate_weight, 1) + contract(
        up_grad, 1, up_weight, 1
    )

    @pl.when(step == pl.num_programs(0) - 1)
    def _():
        middle = middle_ref[...]
        factor = factor_of(middle)
        normed_grad = normed_grad_ref[...]
        result_ref[...] = (middle + total_ref[...]).astype(jnp.bfloat16)
        scaled = normed_grad * gain_ref[...]
        slope = jnp.mean(scaled * middle, axis=-1, keepdims=True)
        middle_grad = out_grad_ref[...].astype(jnp.float32) + factor * (
            scaled - middle * (factor * factor * slope)
        )
        middle_grad_ref[...] = middle_grad
        middle_low = middle_grad.astype(jnp.bfloat16)
        middle_low_ref[...] = middle_low
        dout_cols = contract(out_weight_ref[...], 1, middle_low, 1).astype(jnp.bfloat16)
        for piece in range(pieces):
            dout_piece_ref[piece] = dout_cols[place_of(piece)]
        gain_grad_ref[...] = jnp.sum(normed_grad * middle * factor, axis=0, keepdims=True)


def fixed_spec(shape):
    return pl.BlockSpec(shape, lambda i, *_: (0,) * len(shape), pipeline_mode=pl.Buffered(1))


def feed_forward(tokens, mixed_pieces, gain, out_grad, out, gate, up, down):
    rows = tokens.shape[0]
    wide = pl.BlockSpec((rows, FF_TILE), lambda i: (0, i))
    out_first, gate_first, up_first = (out[1] // D, gate[1] // D, up[1] // D)
    down_first = down[1] // FF_TILE
    square = (rows, D)
    flipped = (D, rows)
    outs = [
        (fixed_spec(square), square, jnp.bfloat16),
        (fixed_spec(square), square, jnp.float32),
        (fixed_spec(square), square, jnp.bfloat16),
        (fixed_spec(mixed_pieces.shape), mixed_pieces.shape, jnp.bfloat16),
        (fixed_spec((1, D)), (1, D), jnp.float32),
        (wide, (rows, FF), jnp.bfloat16),
        (wide, (rows, FF), jnp.bfloat16),
        (pl.BlockSpec((FF_TILE, rows), lambda i: (i, 0)), (FF, rows), jnp.bfloat16),
        (fixed_spec(flipped), flipped, jnp.bfloat16),
        (fixed_spec(flipped), flipped, jnp.bfloat16),
    ]
    return pl.pallas_call(
        feed_forward_kernel,
        grid=(FF // FF_TILE,),
        in_specs=[
            fixed_spec(square),
            fixed_spec(mixed_pieces.shape),
            fixed_spec((1, D)),
            fixed_spec(square),
            pl.BlockSpec((D, D), lambda i: (out_first, 0), pipeline_mode=pl.Buffered(1)),
            pl.BlockSpec((D, FF_TILE), lambda i: (gate_first, i)),
            pl.BlockSpec((D, FF_TILE), lambda i: (up_first, i)),
            pl.BlockSpec((FF_TILE, D), lambda i: (down_first + i, 0)),
        ],
        out_specs=[spec for spec, _, _ in outs],
        out_shape=[jax.ShapeDtypeStruct(shape, kind) for _, shape, kind in outs],
        scratch_shapes=[
            pltpu.VMEM(square, jnp.float32),
            pltpu.VMEM(square, jnp.bfloat16),
            pltpu.VMEM(square, jnp.float32),
            pltpu.VMEM(square, jnp.float32),
        ],
        compiler_params=pltpu.CompilerParams(vmem_limit_bytes=48 << 20),
        cost_estimate=pl.CostEstimate(
            flops=12 * rows * D * FF, transcendentals=rows * FF, bytes_accessed=6 * D * FF
        ),
        name="feed_forward",
    )(tokens, mixed_pieces, gain.reshape(1, D), out_grad, out[0], gate[0], up[0], down[0])


def project_kernel(
    normed_ref, query_weight_ref, key_weight_ref, value_weight_ref, cos_ref, sin_ref, piece_ref
):
    normed = normed_ref[...]
    cosine = cos_ref[...]
    sine_part = sin_ref[...]
    query_cols = contract(normed, 1, query_weight_ref[...], 0).T
    key_cols = contract(normed, 1, key_weight_ref[...], 0).T
    value_cols = contract(normed, 1, value_weight_ref[...], 0).T
    key_heads = key_cols.shape[0] // HEAD_DIM
    pieces, _, cols = piece_ref.shape
    parts = pieces // (2 * key_heads)

    def head(columns, number):
        return columns[number * HEAD_DIM : (number + 1) * HEAD_DIM]

    for key_head in range(key_heads):
        for half in range(2):
            owner = 2 * key_head + half
            query = rotate(head(query_cols, owner), cosine, sine_part)
            if half == 0:
                other = rotate(head(key_cols, key_head), cosine, sine_part)
            else:
                other = head(value_cols, key_head)
            both = jnp.concatenate([query, other], axis=0).astype(jnp.bfloat16)
            for part in range(parts):
                piece_ref[owner * parts + part] = both[:, part * cols : (part + 1) * cols]


def project(normed, query, key, value, cosine, sine_part, cols):
    rows = normed.shape[0]
    steps = 2
    pieces = HEADS * rows // cols
    query_first, key_first, value_first = (query[1] // D, key[1] // D, value[1] // D)
    query_cols = HEADS * HEAD_DIM // steps
    key_cols = KV_HEADS * HEAD_DIM // steps
    return pl.pallas_call(
        project_kernel,
        grid=(steps,),
        in_specs=[
            fixed_spec(normed.shape),
            pl.BlockSpec((D, query_cols), lambda i: (query_first, i)),
            pl.BlockSpec((D, key_cols), lambda i: (key_first, i)),
            pl.BlockSpec((D, key_cols), lambda i: (value_first, i)),
            fixed_spec(cosine.shape),
            fixed_spec(sine_part.shape),
        ],
        out_specs=pl.BlockSpec((pieces // steps, 2 * HEAD_DIM, cols), lambda i: (i, 0, 0)),
        out_shape=jax.ShapeDtypeStruct((pieces, 2 * HEAD_DIM, cols), jnp.bfloat16),
        compiler_params=pltpu.CompilerParams(vmem_limit_bytes=40 << 20),
        cost_estimate=pl.CostEstimate(
            flops=4 * rows * D * 2 * D, transcendentals=0, bytes_accessed=4 * D * 2 * D
        ),
        name="project",
    )(normed, query[0], key[0], value[0], cosine, sine_part)


def live_pairs(rel_ref, pos, start, base, queries):
    rel = rel_ref[...]
    rel = jnp.concatenate([rel] * (queries // rel.shape[1]), axis=1)
    return (rel >= start - base) & (rel <= pos - base)


def forward_kernel(
    low_ref, high_ref, query_ref, key_ref, value_ref, pos_ref, start_ref, rel_ref, out_ref, lse_ref
):
    tile = pl.program_id(0)
    query_cols = query_ref[0]
    queries = query_cols.shape[1]
    keys = rel_ref.shape[0]
    pos = pos_ref[0]
    start = start_ref[0]

    def body(step, carried):
        run_max, run_total, mixed = carried
        rows = pl.ds(pl.multiple_of(step * keys, keys), keys)
        scores = contract(key_ref[rows, :], 1, query_cols, 0)
        live = live_pairs(rel_ref, pos, start, step * keys, queries)
        scores = jnp.where(live, scores, NEG_LARGE)
        new_max = jnp.maximum(run_max, jnp.max(scores, axis=0, keepdims=True))
        weights = jnp.exp2((scores - new_max) * SCORE_BASE_TWO)
        keep = jnp.exp2((run_max - new_max) * SCORE_BASE_TWO)
        run_total = run_total * keep + jnp.sum(weights, axis=0, keepdims=True)
        mixed = mixed * keep + contract(value_ref[step], 1, weights.astype(jnp.bfloat16), 0)
        return (new_max, run_total, mixed)

    start_state = (
        jnp.full((1, queries), NEG_LARGE, jnp.float32),
        jnp.zeros((1, queries), jnp.float32),
        jnp.zeros((HEAD_DIM, queries), jnp.float32),
    )
    run_max, run_total, mixed = lax.fori_loop(low_ref[tile], high_ref[tile], body, start_state)
    out_ref[0] = mixed / run_total
    lse_ref[0] = run_max * SCORE_BASE_TWO + jnp.log2(run_total)


def backward_kernel(
    low_ref,
    high_ref,
    query_ref,
    query_row_ref,
    dout_ref,
    dout_row_ref,
    out_ref,
    lse_ref,
    key_ref,
    key_col_ref,
    value_ref,
    pos_ref,
    start_ref,
    rel_ref,
    dquery_ref,
    dkey_ref,
    dvalue_ref,
):
    tile = pl.program_id(0)

    @pl.when(tile == 0)
    def _():
        dkey_ref[...] = jnp.zeros_like(dkey_ref)
        dvalue_ref[...] = jnp.zeros_like(dvalue_ref)

    query_cols = query_ref[0]
    query_rows = query_row_ref[0]
    dout_cols = dout_ref[0]
    dout_rows = dout_row_ref[0]
    queries = query_cols.shape[1]
    keys = rel_ref.shape[0]
    pos = pos_ref[0]
    start = start_ref[0]
    lse = lse_ref[0]
    delta = jnp.sum(dout_cols.astype(jnp.float32) * out_ref[0], axis=0, keepdims=True)

    def body(step, dquery):
        rows = pl.ds(pl.multiple_of(step * keys, keys), keys)
        scores = contract(key_ref[rows, :], 1, query_cols, 0)
        live = live_pairs(rel_ref, pos, start, step * keys, queries)
        weights = jnp.where(live, jnp.exp2(scores * SCORE_BASE_TWO - lse), 0.0)
        weight_grad = contract(value_ref[rows, :], 1, dout_cols, 0)
        dscore = (weights * (weight_grad - delta)).astype(jnp.bfloat16)
        dvalue_ref[rows, :] += contract(weights.astype(jnp.bfloat16), 1, dout_rows, 0)
        dkey_ref[rows, :] += contract(dscore, 1, query_rows, 0)
        return dquery + contract(key_col_ref[step], 1, dscore, 0)

    dquery = lax.fori_loop(
        low_ref[tile], high_ref[tile], body, jnp.zeros((HEAD_DIM, queries), jnp.float32)
    )
    dquery_ref[0] = dquery * SCORE_SCALE

    @pl.when(tile == pl.num_programs(0) - 1)
    def _():
        dkey_ref[...] = dkey_ref[...] * SCORE_SCALE


def whole_spec(array):
    return pl.BlockSpec(array.shape, lambda i, *_: (0,) * array.ndim)


def tile_spec(array):
    return pl.BlockSpec((1,) + array.shape[1:], lambda i, *_: (i,) + (0,) * (array.ndim - 1))


def run_kernel(body, name, bounds, inputs, outputs, flops):
    spec = lambda item: tile_spec(item[0]) if item[1] else whole_spec(item[0])
    grid = next(array.shape[0] for array, cut in inputs if cut)
    return pl.pallas_call(
        body,
        grid_spec=pltpu.PrefetchScalarGridSpec(
            num_scalar_prefetch=2,
            grid=(grid,),
            in_specs=[spec(item) for item in inputs],
            out_specs=[spec(item) for item in outputs],
        ),
        out_shape=[item[0] for item in outputs],
        compiler_params=pltpu.CompilerParams(vmem_limit_bytes=52 << 20),
        cost_estimate=pl.CostEstimate(
            flops=flops, transcendentals=flops // 400, bytes_accessed=16 << 20
        ),
        name=name,
    )(*bounds, *[item[0] for item in inputs])


def attend(query_cols, key_rows, value_cols, pos, start, rel, low, high):
    tiles, _, queries = query_cols.shape
    return run_kernel(
        forward_kernel,
        "attention_forward",
        (low, high),
        [
            (query_cols, True),
            (key_rows, False),
            (value_cols, False),
            (pos, True),
            (start, True),
            (rel, False),
        ],
        [
            (jax.ShapeDtypeStruct((tiles, HEAD_DIM, queries), jnp.float32), True),
            (jax.ShapeDtypeStruct((tiles, 1, queries), jnp.float32), True),
        ],
        20_000_000_000,
    )


def attend_back(
    query_cols, dout_cols, out_cols, lse, key_rows, key_cols, value_rows, pos, start, rel, low, high
):
    tiles, _, queries = query_cols.shape
    grads = jax.ShapeDtypeStruct(key_rows.shape, jnp.float32)
    return run_kernel(
        backward_kernel,
        "attention_backward",
        (low, high),
        [
            (query_cols, True),
            (jnp.swapaxes(query_cols, 1, 2), True),
            (dout_cols, True),
            (jnp.swapaxes(dout_cols, 1, 2), True),
            (out_cols, True),
            (lse, True),
            (key_rows, False),
            (key_cols, False),
            (value_rows, False),
            (pos, True),
            (start, True),
            (rel, False),
        ],
        [
            (jax.ShapeDtypeStruct((tiles, HEAD_DIM, queries), jnp.float32), True),
            (grads, False),
            (grads, False),
        ],
        50_000_000_000,
    )


def per_device(
    tokens,
    segment_ids,
    out_grad,
    attn_master,
    attn_first,
    attn_second,
    ffn_master,
    ffn_first,
    ffn_second,
):
    index = lax.axis_index("seq")
    count = lax.axis_size("seq")
    rows = tokens.shape[0]
    total = rows * count
    group = count // KV_HEADS
    parts = group // 2
    span = rows // parts
    half = (index // parts) % 2
    part = index % parts

    def exchange(value):
        return lax.all_to_all(value, "seq", 0, 0, tiled=True)

    def swapped(value, bit):
        return lax.ppermute(value, "seq", [(i, i ^ bit) for i in range(count)])

    attn_low = attn_master.astype(jnp.bfloat16)
    ffn_low = ffn_master.astype(jnp.bfloat16)
    notice = jnp.concatenate(
        [attn_low[:D], ffn_low[:D], segment_ids.astype(jnp.bfloat16)]
    ).reshape(1, -1, 128)
    notices = exchange(jnp.broadcast_to(notice, (count,) + notice.shape[1:]))

    inputs = tokens.astype(jnp.float32)

    def from_notices(notices):
        gains = notices[0, : 2 * D // 128].astype(jnp.float32).reshape(2, D)
        all_ids = notices[:, 2 * D // 128 :].astype(jnp.int32).reshape(-1)
        held_ids = lax.dynamic_index_in_dim(
            all_ids.reshape(count, parts, span), part, 1, keepdims=False
        )

        def item_starts(ids):
            return jnp.sum((all_ids < ids[..., None]).astype(jnp.int32), axis=-1)

        return (
            gains[0],
            gains[1],
            rms_norm(inputs, gains[0]).astype(jnp.bfloat16),
            item_starts(held_ids.reshape(-1)),
            item_starts(all_ids[:: QUERY_TILE // span * rows]) // KEY_TILE,
        )

    grid = device_grid(count)
    by_axes = (D // count) % 16 == 0

    def sum_of(left_cols, right, right_dim, order):
        left = reordered(left_cols, slot_table(index, grid, order))
        return SummedRows(left, right, right_dim, order, grid)

    def scattered(left_cols, right, right_dim):
        whole = contract(left_cols, 1, right, right_dim).astype(jnp.bfloat16)
        return (
            lax.psum_scatter(whole, "seq", scatter_dimension=0, tiled=True)
            .reshape(-1)
            .astype(jnp.float32)
        )

    attn_block = aligned_block(attn_low, index, count)
    ffn_block = aligned_block(ffn_low, index, count)
    if by_axes:
        own_tiles = unit_tiles(ffn_block, (FF, FF, D), index, count)
        attn_tiles, own_tiles, beside = gather_tiles(
            unit_tiles(attn_block, (D, KV_HEADS * HEAD_DIM, D), index, count),
            index,
            grid,
            notices,
            own_tiles,
            from_notices,
        )
        ffn_tiles = lax.all_gather(own_tiles, "seq", axis=0, tiled=True)
        wide_rows = matrix_of(ffn_tiles, FF)
        gate_weight = (wide_rows, 0)
        up_weight = (wide_rows, D)
        down_weight = (matrix_of(ffn_tiles, D), 2 * FF)
        attn_wide = matrix_of(attn_tiles, D)
        attn_narrow = matrix_of(attn_tiles, KV_HEADS * HEAD_DIM)
        query_weight = (attn_wide, 0)
        key_weight = (attn_narrow, 2 * D)
        value_weight = (attn_narrow, 3 * D)
        out_weight = (attn_wide, 2 * D)
    else:

        def gathered(unit, width):
            return lax.all_gather(unit.reshape(-1, width), "seq", axis=0, tiled=True)

        q_unit, kv_unit, o_unit = units_from_block(attn_block, index, count)
        gate_unit, up_unit, down_unit = units_from_block(ffn_block, index, count)
        query_weight = (gathered(q_unit, HEADS * HEAD_DIM), 0)
        key_value_weight = gathered(kv_unit, KV_HEADS * HEAD_DIM)
        key_weight = (key_value_weight, 0)
        value_weight = (key_value_weight, D)
        out_weight = (gathered(o_unit, D), 0)
        gate_weight = (gathered(gate_unit, FF), 0)
        up_weight = (gathered(up_unit, FF), 0)
        down_weight = (gathered(down_unit, D), 0)

    gain_one, gain_two, normed_one, held_starts, low = (
        beside if by_axes else from_notices(notices)
    )

    own_places = index * rows + jnp.arange(rows, dtype=jnp.int32)
    own_cos, own_sin = angle_tables(own_places)

    cols = span if span % 128 == 0 else rows

    def by_owner(value):
        if value.shape[0] == count:
            return value
        pieces = value.reshape(HEADS, value.shape[1], parts, span)
        return jnp.swapaxes(pieces, 1, 2).reshape(count, value.shape[1], span)

    def by_head(value):
        pieces = value.reshape(HEADS, parts, value.shape[1], span)
        return jnp.swapaxes(pieces, 1, 2).reshape(HEADS, value.shape[1], rows)

    received = exchange(
        by_owner(
            project(normed_one, query_weight, key_weight, value_weight, own_cos, own_sin, cols)
        )
    )

    sources = QUERY_TILE // span
    tiles = count // sources

    def to_tiles(value):
        pieces = value.reshape(tiles, sources, value.shape[1], span)
        return jnp.swapaxes(pieces, 1, 2).reshape(tiles, value.shape[1], QUERY_TILE)

    def from_tiles(value):
        pieces = value.reshape(tiles, value.shape[1], sources, span)
        return jnp.swapaxes(pieces, 1, 2).reshape(count, value.shape[1], span)

    query_cols = to_tiles(received[:, :HEAD_DIM])
    own_kind = received[:, HEAD_DIM:]
    other_kind = swapped(own_kind, parts)
    pair = jnp.stack(
        [
            jnp.where(half == 0, own_kind, other_kind),
            jnp.where(half == 0, other_kind, own_kind),
        ]
    )[:, None]
    bit = 1
    while bit < parts:
        pair = jnp.concatenate([pair, swapped(pair, bit)], axis=1)
        bit = bit * 2
    key_all, value_all = (pair[0], pair[1])
    devices_per_tile = KEY_TILE // rows
    key_tiles = count // devices_per_tile

    def key_columns(value):
        pieces = value.reshape(parts, key_tiles, devices_per_tile, HEAD_DIM, span)
        return jnp.transpose(pieces, (1, 3, 2, 0, 4)).reshape(key_tiles, HEAD_DIM, KEY_TILE)

    def key_rows_of(value):
        return jnp.transpose(value, (1, 0, 3, 2)).reshape(total, HEAD_DIM)

    key_cols = key_columns(key_all)
    value_cols = key_columns(value_all)
    key_rows = key_rows_of(key_all)
    value_rows = key_rows_of(value_all)
    slot_parts = part ^ jnp.arange(parts, dtype=jnp.int32)
    within = jnp.arange(span, dtype=jnp.int32)
    rel = (
        rows * jnp.arange(devices_per_tile, dtype=jnp.int32)[:, None, None]
        + span * slot_parts[None, :, None]
        + within[None, None, :]
    ).reshape(KEY_TILE, 1)
    rel = jnp.broadcast_to(rel, (KEY_TILE, 128))
    held_places = (
        rows * jnp.arange(count, dtype=jnp.int32)[:, None] + span * part + within[None, :]
    )
    pos = held_places.reshape(tiles, 1, QUERY_TILE)
    start = held_starts.reshape(tiles, 1, QUERY_TILE)
    tile_span = sources * rows
    high = (jnp.arange(1, tiles + 1, dtype=jnp.int32) * tile_span + KEY_TILE - 1) // KEY_TILE

    chunks = []
    chunk = min(CHUNK, total)
    for first in range(0, total, chunk):
        first_key = max(0, first - SEG_MOST) // KEY_TILE
        last_key = (first + chunk) // KEY_TILE
        chunks.append(
            (
                slice(first // tile_span, (first + chunk) // tile_span),
                slice(first_key, last_key),
                slice(first_key * KEY_TILE, last_key * KEY_TILE),
            )
        )

    pieces = []
    for of_tiles, of_key_tiles, of_keys in chunks:
        shift = of_key_tiles.start * KEY_TILE
        pieces.append(
            attend(
                query_cols[of_tiles],
                key_rows[of_keys],
                value_cols[of_key_tiles],
                pos[of_tiles] - shift,
                start[of_tiles] - shift,
                rel,
                low[of_tiles] - of_key_tiles.start,
                high[of_tiles] - of_key_tiles.start,
            )
        )
    out_cols = jnp.concatenate([piece[0] for piece in pieces])
    lse = jnp.concatenate([piece[1] for piece in pieces])

    mixed_pieces = exchange(from_tiles(out_cols.astype(jnp.bfloat16)))
    mixed_pieces, (key_cols, value_rows) = together(mixed_pieces, (key_cols, value_rows))
    if cols == rows:
        mixed_pieces = by_head(mixed_pieces)

    (
        result,
        middle_grad,
        middle_low,
        dout_pieces,
        grad_two,
        gate_grad,
        up_grad,
        hidden_cols,
        normed_two_cols,
        mixed_low,
    ) = feed_forward(
        tokens,
        mixed_pieces,
        gain_two,
        out_grad,
        out_weight,
        gate_weight,
        up_weight,
        down_weight,
    )
    dout_received = exchange(by_owner(dout_pieces))
    if by_axes:
        gate_sum = sum_of(normed_two_cols, gate_grad, 0, GATE_ORDER)
        up_sum = sum_of(normed_two_cols, up_grad, 0, UP_ORDER)
        down_sum = sum_of(hidden_cols, out_grad, 0, DOWN_ORDER)
        first_sums = [gate_sum, up_sum]
        make_and_send(first_sums + [down_sum])
        dout_received = made_before(first_sums, dout_received)
        for each in first_sums:
            each.send()
    else:
        ffn_units = [
            scattered(normed_two_cols, gate_grad, 0),
            scattered(normed_two_cols, up_grad, 0),
            scattered(hidden_cols, out_grad, 0),
        ]
        out_unit = scattered(mixed_low, middle_low, 0)
    dout_cols = to_tiles(dout_received)

    pieces = []
    dkey_rows = jnp.zeros((total, HEAD_DIM), jnp.float32)
    dvalue_rows = jnp.zeros((total, HEAD_DIM), jnp.float32)
    for of_tiles, of_key_tiles, of_keys in chunks:
        shift = of_key_tiles.start * KEY_TILE
        dquery_piece, dkey_piece, dvalue_piece = attend_back(
            query_cols[of_tiles],
            dout_cols[of_tiles],
            out_cols[of_tiles],
            lse[of_tiles],
            key_rows[of_keys],
            key_cols[of_key_tiles],
            value_rows[of_keys],
            pos[of_tiles] - shift,
            start[of_tiles] - shift,
            rel,
            low[of_tiles] - of_key_tiles.start,
            high[of_tiles] - of_key_tiles.start,
        )
        pieces.append(dquery_piece)
        if len(chunks) == 1:
            dkey_rows, dvalue_rows = (dkey_piece, dvalue_piece)
        else:
            dkey_rows = dkey_rows.at[of_keys].add(dkey_piece)
            dvalue_rows = dvalue_rows.at[of_keys].add(dvalue_piece)
    dquery_rot = from_tiles(jnp.concatenate(pieces))
    held_cos, held_sin = angle_tables(held_places)
    dquery_held = rotate(dquery_rot, held_cos, -held_sin).astype(jnp.bfloat16)

    def by_slot(value):
        return jnp.transpose(value.reshape(count, parts, span, HEAD_DIM), (1, 0, 3, 2))

    if by_axes:
        dkey_rows = taken_after(first_sums, dkey_rows)
        mixed_late, dkey_rows = together(mixed_low, dkey_rows)
        out_sum = sum_of(mixed_late, middle_low, 0, OUT_ORDER)
    grads = jnp.stack([by_slot(dkey_rows), by_slot(dvalue_rows)])
    bit = parts // 2
    while bit >= 1:
        grads = grads[:, :bit] + swapped(grads[:, bit:].astype(jnp.bfloat16), bit)
        bit = bit // 2
    dkey_held, dvalue_held = (grads[0, 0], grads[1, 0])
    sent_kind = jnp.where(half == 0, dvalue_held, dkey_held).astype(jnp.bfloat16)
    kept_kind = jnp.where(half == 0, dkey_held, dvalue_held) + swapped(sent_kind, parts)
    kept_low = jnp.where(half == 0, rotate(kept_kind, held_cos, -held_sin), kept_kind).astype(
        jnp.bfloat16
    )
    sent_back = jnp.concatenate([dquery_held, kept_low], axis=1)
    if by_axes:
        early_sums = first_sums + [down_sum]
        sent_back = made_before(early_sums, sent_back)
        for each in early_sums:
            each.send()
    returned = exchange(sent_back)
    if by_axes:
        make_and_send([out_sum])
        returned = made_before(first_sums, returned)
        for each in first_sums:
            each.send()
    dquery_low = by_head(returned[:, :HEAD_DIM]).reshape(HEADS * HEAD_DIM, rows)
    pair_low = by_head(returned[:, HEAD_DIM:]).reshape(KV_HEADS, 2, HEAD_DIM, rows)
    dkey_low = pair_low[:, 0].reshape(KV_HEADS * HEAD_DIM, rows)
    dvalue_low = pair_low[:, 1].reshape(KV_HEADS * HEAD_DIM, rows)

    normed_one_cols = normed_one.T
    nothing = jnp.zeros_like(normed_one_cols)
    key_value_cols = jnp.concatenate(
        [
            jnp.concatenate([normed_one_cols, nothing], axis=1),
            jnp.concatenate([nothing, normed_one_cols], axis=1),
        ]
    )
    key_value_right = jnp.concatenate([dkey_low, dvalue_low], axis=1)
    normed_one_grad = (
        contract(dquery_low, 0, query_weight[0][:D], 1)
        + contract(dkey_low, 0, key_weight[0][key_weight[1] : key_weight[1] + D], 1)
        + contract(dvalue_low, 0, value_weight[0][value_weight[1] : value_weight[1] + D], 1)
    )
    _, first_pull = jax.vjp(rms_norm, inputs, gain_one)
    input_norm_grad, grad_one = first_pull(normed_one_grad)
    input_grad = middle_grad + input_norm_grad

    gain_grads = jnp.sum(
        exchange(
            jnp.broadcast_to(
                jnp.concatenate([grad_one, grad_two[0]]).reshape(1, -1, 128),
                (count, 2 * D // 128, 128),
            )
        ),
        axis=0,
    ).reshape(2, D)
    if by_axes:
        query_sum = sum_of(normed_one_cols, dquery_low, 1, GATE_ORDER)
        key_value_sum = sum_of(key_value_cols, key_value_right, 1, UP_ORDER)
        last_sums = [query_sum, key_value_sum]
        make_and_send(last_sums)
        dquery_low = made_before(last_sums, dquery_low)
        for each in last_sums:
            each.send()
        make_and_send([gate_sum, up_sum, down_sum, out_sum])
        attn_sums = last_sums + [out_sum]
        gain_grads, input_grad = taken_after(
            attn_sums + early_sums, (gain_grads, input_grad)
        )
        make_and_send(attn_sums + early_sums)
        one_round(attn_sums + [down_sum])
        one_round(attn_sums + [down_sum])
        ffn_units = [gate_sum.result(), up_sum.result(), down_sum.result()]
        one_round(attn_sums)
        query_unit, key_value_unit, out_unit = [each.result() for each in attn_sums]
    else:
        query_unit = scattered(normed_one_cols, dquery_low, 1)
        key_value_unit = scattered(key_value_cols, key_value_right, 1)
    ffn_shard = shard_from_units(ffn_units, gain_grads[1], index, count)
    if by_axes:
        (query_unit, key_value_unit, out_unit), ffn_shard = together(
            (query_unit, key_value_unit, out_unit), ffn_shard
        )
    attn_shard = shard_from_units(
        [query_unit, key_value_unit, out_unit], gain_grads[0], index, count
    )
    attn_new, attn_one, attn_two = adam_update(
        attn_master, attn_first, attn_second, attn_shard
    )
    ffn_new, ffn_one, ffn_two = adam_update(
        ffn_master, ffn_first, ffn_second, ffn_shard
    )
    return (result, input_grad, attn_new, attn_one, attn_two, ffn_new, ffn_one, ffn_two)


def solution(mesh):
    rows_cut = P("seq", None)
    flat_cut = P("seq")
    in_specs = (rows_cut, flat_cut, rows_cut) + (flat_cut,) * 6
    out_specs = (rows_cut, rows_cut) + (flat_cut,) * 6
    return jax.shard_map(
        per_device, mesh=mesh, in_specs=in_specs, out_specs=out_specs, check_vma=False
    )
```

```python
import functools
import math

import jax
import jax.numpy as jnp
from jax import lax
from jax.experimental import pallas as pl
from jax.experimental.pallas import tpu as pltpu
from jax.sharding import PartitionSpec as P

D = 1536
HEADS = 16
KV_HEADS = 8
HEAD_DIM = 96
FF = 4096
SEG_MOST = 4096
STEP = 7


ROPE_BASE = 100000.0
NORM_EPS = 1e-05
BETA_ONE = 0.5
BETA_TWO = 0.5
LEARN_RATE = 0.04
DECAY = 0.1
ADAM_EPS = 1e-08
NEG_LARGE = -1e30
HALF_DIM = HEAD_DIM // 2
QUERY_TILE = 512
KEY_TILE = 1024
CHUNK = 8192
LANES = 128
FF_TILE = 512
SCORE_BASE_TWO = math.log2(math.e) / math.sqrt(HEAD_DIM)
SCORE_SCALE = 1.0 / math.sqrt(HEAD_DIM)


def rms_norm(values, norm_gain):
    factor = lax.rsqrt(jnp.mean(values * values, axis=-1, keepdims=True) + NORM_EPS)
    return values * factor * norm_gain


def angle_tables(positions):
    frequency = jnp.exp(
        jnp.arange(HALF_DIM).astype(jnp.float32) * (-2.0 * math.log(ROPE_BASE) / HEAD_DIM)
    )
    angles = positions.astype(jnp.float32)[..., None, :] * frequency[:, None]
    return (jnp.cos(angles), jnp.sin(angles))


def rotate(values, cosine, sine_part):
    lower_part = values[..., :HALF_DIM, :]
    upper_part = values[..., HALF_DIM:, :]
    return jnp.concatenate(
        [
            lower_part * cosine - upper_part * sine_part,
            upper_part * cosine + lower_part * sine_part,
        ],
        axis=-2,
    )


def contract(left, left_dim, right, right_dim):
    return lax.dot_general(
        left,
        right,
        (((left_dim,), (right_dim,)), ((), ())),
        preferred_element_type=jnp.float32,
    )


def adam_update(master, moment_one, moment_two, gradient):
    first_new = BETA_ONE * moment_one + (1.0 - BETA_ONE) * gradient
    second_new = BETA_TWO * moment_two + (1.0 - BETA_TWO) * gradient * gradient
    first_hat = first_new / (1.0 - BETA_ONE**STEP)
    second_hat = second_new / (1.0 - BETA_TWO**STEP)
    master_new = master - LEARN_RATE * (
        first_hat / (jnp.sqrt(second_hat) + ADAM_EPS) + DECAY * master
    )
    return (master_new, first_new, second_new)


def aligned_block(flat_low, index, count):
    edge = D // count
    block = flat_low.shape[0] - edge
    following = lax.ppermute(flat_low[:D], "seq", [(i + 1, i) for i in range(count - 1)])
    extended = jnp.concatenate([flat_low, following])
    return lax.dynamic_slice(extended, (D - edge * index,), (block,))


def tiles_of(unit, width):
    pieces = unit.reshape(-1, 8, width // 128, 128)
    return jnp.swapaxes(pieces, 1, 2).reshape(-1, 8, 128)


def matrix_of(tiles, width):
    pieces = tiles.reshape(-1, width // 128, 8, 128)
    return jnp.swapaxes(pieces, 1, 2).reshape(-1, width)


def unit_tiles(block, widths, index, count):
    units = block.reshape(3, -1)
    made = []
    for j in range(3):
        kind = (3 * index + j) // count
        made.append(
            lax.select_n(kind, *[tiles_of(units[j], width) for width in widths])
        )
    return jnp.concatenate(made)


def units_from_block(block, index, count):
    aligned = block.reshape(3, -1)
    dealt = jnp.stack(
        [
            lax.ppermute(aligned[j], "seq", [(i, (3 * i + j) % count) for i in range(count)])
            for j in range(3)
        ]
    )
    return [
        lax.dynamic_index_in_dim(dealt, slot_of_kind(index, kind, count), 0, keepdims=False)
        for kind in range(3)
    ]


def slot_of_kind(index, kind, count):
    return (index + count * kind) % 3


def shard_from_units(units, gain_grad, index, count):
    edge = D // count
    units = [unit.astype(jnp.bfloat16) for unit in units]
    unit = units[0].shape[0]
    returned = []
    for j in range(3):
        inverse = 1 if count % 3 == 1 else 2
        kind = ((j - index) * inverse) % 3
        piece = jnp.where(kind == 0, units[0], jnp.where(kind == 1, units[1], units[2]))
        returned.append(
            lax.ppermute(piece, "seq", [((3 * i + j) % count, i) for i in range(count)])
        )
    before = lax.ppermute(returned[2][-D:], "seq", [(i, i + 1) for i in range(count - 1)])
    before = jnp.where(index == 0, gain_grad, before.astype(jnp.float32))
    extended = jnp.concatenate([before] + [piece.astype(jnp.float32) for piece in returned])
    return lax.dynamic_slice(extended, (edge * index,), (3 * unit + edge,))


AXES = ("z", "y", "x")
GATHER_ORDERS = (("core", "x", "y", "z"), ("core", "y", "x", "z"))
GATE_ORDER = ("core", "x", "z", "y")
UP_ORDER = ("core", "y", "z", "x")
DOWN_ORDER = ("core", "y", "x", "z")
OUT_ORDER = ("core", "y", "x", "z")


def device_grid(count):
    chips = count // 2
    sides = {16: (4, 2, 2), 64: (4, 4, 4)}.get(chips, (chips, 1, 1))
    return dict(zip(AXES + ("core",), sides + (2,)))


def coordinates(index, grid):
    found = {}
    for axis in reversed(list(grid)):
        found[axis] = index % grid[axis]
        index = index // grid[axis]
    return found


def place(found, grid):
    index = 0
    for axis in grid:
        index = index * grid[axis] + found[axis]
    return index


def shifted(value, axis, steps, grid):
    pairs = []
    for source in range(math.prod(grid.values())):
        target = coordinates(source, grid)
        target[axis] = (target[axis] + steps) % grid[axis]
        pairs.append((source, place(target, grid)))
    return lax.ppermute(value, "seq", pairs)


def slot_table(index, grid, axes):
    here = coordinates(index, grid)
    entries = []
    for number in range(math.prod(grid.values())):
        slots = coordinates(number, {axis: grid[axis] for axis in axes})
        there = {axis: (here[axis] - slots[axis]) % grid[axis] for axis in grid}
        entries.append(place(there, grid))
    return jnp.stack(entries).astype(jnp.int32)


def place_kernel(table_ref, *refs, lengths):
    pieces = len(lengths)
    piece_refs, out_ref = (refs[:pieces], refs[pieces])
    held, in_sems, out_sems = refs[pieces + 1 :]
    size = held.shape[1]
    loads = []
    for piece_ref, length in zip(piece_refs, lengths):
        for block in range(length):
            entry = len(loads)
            load = pltpu.make_async_copy(
                piece_ref.at[pl.ds(block * size, size)], held.at[entry], in_sems.at[entry]
            )
            load.start()
            loads.append(load)
    stores = []
    for entry, load in enumerate(loads):
        load.wait()
        target = pl.ds(pl.multiple_of(table_ref[entry] * size, size), size)
        store = pltpu.make_async_copy(held.at[entry], out_ref.at[target], out_sems.at[entry])
        store.start()
        stores.append(store)
    for store in stores:
        store.wait()


def placed(pieces, table):
    count = table.shape[0]
    size = sum(piece.shape[0] for piece in pieces) // count
    shape = pieces[0].shape[1:]
    anywhere = pl.BlockSpec(memory_space=pl.ANY)
    return pl.pallas_call(
        functools.partial(
            place_kernel, lengths=tuple(piece.shape[0] // size for piece in pieces)
        ),
        grid_spec=pltpu.PrefetchScalarGridSpec(
            num_scalar_prefetch=1,
            grid=(1,),
            in_specs=[anywhere] * len(pieces),
            out_specs=anywhere,
            scratch_shapes=[
                pltpu.VMEM((count, size) + shape, pieces[0].dtype),
                pltpu.SemaphoreType.DMA((count,)),
                pltpu.SemaphoreType.DMA((count,)),
            ],
        ),
        out_shape=jax.ShapeDtypeStruct((count * size,) + shape, pieces[0].dtype),
        compiler_params=pltpu.CompilerParams(vmem_limit_bytes=48 << 20),
        cost_estimate=pl.CostEstimate(
            flops=0, transcendentals=0, bytes_accessed=4 * count * size * math.prod(shape)
        ),
        name="place_blocks",
    )(table, *pieces)


def gather_tiles(block, index, grid, notices, later, beside_of):
    arrived = [block] + [shifted(block, "z", k, grid) for k in range(1, grid["z"])]
    arrived, notices = together(arrived, notices)
    beside = beside_of(notices)
    half = block.shape[0] // 2
    held = [
        jnp.concatenate([each[color * half : (color + 1) * half] for each in arrived])
        for color in range(2)
    ]
    for turn in (2, 1):
        arrivals = []
        for color, order in enumerate(GATHER_ORDERS):
            axis = order[turn]
            arrivals.append(
                [held[color]]
                + [shifted(held[color], axis, k, grid) for k in range(1, grid[axis])]
            )
        if turn == 1:
            arrivals, beside = together(arrivals, beside)
        else:
            arrivals, later = together(arrivals, later)
            held = [jnp.concatenate(each) for each in arrivals]
    pieces = []
    tables = []
    for color, order in enumerate(GATHER_ORDERS):
        pieces = pieces + arrivals[color]
        pieces = pieces + [shifted(piece, "core", 1, grid) for piece in arrivals[color]]
        tables.append(2 * slot_table(index, grid, order) + color)
    return placed(pieces, jnp.concatenate(tables)), later, beside


def reorder_kernel(table_ref, in_ref, out_ref, *, rows):
    for block in range(in_ref.shape[0] // rows):
        source = pl.ds(pl.multiple_of(table_ref[block] * rows, rows), rows)
        out_ref[block * rows : (block + 1) * rows, :] = in_ref[source, :]


def reordered(value, table):
    rows = value.shape[0] // table.shape[0]
    return pl.pallas_call(
        functools.partial(reorder_kernel, rows=rows),
        grid_spec=pltpu.PrefetchScalarGridSpec(
            num_scalar_prefetch=1,
            grid=(1,),
            in_specs=[whole_spec(value)],
            out_specs=whole_spec(value),
        ),
        out_shape=jax.ShapeDtypeStruct(value.shape, value.dtype),
        cost_estimate=pl.CostEstimate(
            flops=0, transcendentals=0, bytes_accessed=4 * value.size
        ),
        name="reorder_blocks",
    )(table, value)


class SummedRows:

    def __init__(self, left, right, right_dim, order, grid):
        self.left = left
        self.right = right
        self.right_dim = right_dim
        self.grid = grid
        self.rows = left.shape[0] // math.prod(grid.values())
        self.window = left.shape[0]
        self.turns = [(axis, slot) for axis in order for slot in range(grid[axis] - 1, 0, -1)]
        self.received = []
        self.passing = []

    def partial(self, span):
        total = contract(self.left[span], 1, self.right, self.right_dim)
        for part in self.received:
            total = total + part[span]
        return total

    def make(self):
        axis, slot = self.turns[0]
        if slot == self.grid[axis] - 1:
            self.window = self.window // self.grid[axis]
        total = self.partial(slice(slot * self.window, (slot + 1) * self.window))
        for part in self.passing:
            total = total + part
        self.made = total.astype(jnp.bfloat16)

    def send(self):
        axis, slot = self.turns.pop(0)
        arrived = [shifted(self.made, axis, -1, self.grid)]
        if slot > 1:
            self.passing = arrived
        else:
            self.passing = []
            self.received = self.received + arrived

    def result(self):
        return self.partial(slice(0, self.rows)).reshape(-1)


class SummedWhole:

    def __init__(self, value, grid):
        self.value = value
        self.grid = grid
        self.turns = []
        for axis in ("core", "x", "y", "z"):
            step = grid[axis] // 2
            while step >= 1:
                self.turns.append((axis, step))
                step = step // 2
        self.received = []
        self.passing = []

    def make(self):
        for part in self.received:
            self.value = self.value + part
        self.made = self.value

    def send(self):
        axis, step = self.turns.pop(0)
        self.received = [shifted(self.made, axis, step, self.grid)]

    def result(self):
        return self.value + self.received[0]


def together(values, others):
    return lax.optimization_barrier((values, others))


def made_before(sums, value):
    for each in sums:
        each.make()
    value, made = together(value, [each.made for each in sums])
    for each, now in zip(sums, made):
        each.made = now
    return value


def taken_after(sums, value):
    value, arrived = together(value, [(each.received, each.passing) for each in sums])
    for each, now in zip(sums, arrived):
        each.received, each.passing = now
    return value


def one_round(sums):
    taken_after(sums, ())
    make_and_send(sums)


def make_and_send(sums):
    for each in sums:
        each.make()
        each.send()


def feed_forward_kernel(
    tokens_ref,
    mixed_piece_ref,
    gain_ref,
    out_grad_ref,
    out_weight_ref,
    gate_weight_ref,
    up_weight_ref,
    down_weight_ref,
    result_ref,
    middle_grad_ref,
    middle_low_ref,
    dout_piece_ref,
    gain_grad_ref,
    gate_grad_ref,
    up_grad_ref,
    hidden_col_ref,
    normed_col_ref,
    mixed_col_ref,
    middle_ref,
    normed_ref,
    total_ref,
    normed_grad_ref,
):
    step = pl.program_id(0)
    pieces, _, cols = mixed_piece_ref.shape
    per_head = pieces // HEADS

    def factor_of(middle):
        return lax.rsqrt(jnp.mean(middle * middle, axis=-1, keepdims=True) + NORM_EPS)

    def place_of(piece):
        head, part = divmod(piece, per_head)
        return (slice(head * HEAD_DIM, (head + 1) * HEAD_DIM), slice(part * cols, (part + 1) * cols))

    @pl.when(step == 0)
    def _():
        for piece in range(pieces):
            mixed_col_ref[place_of(piece)] = mixed_piece_ref[piece]
        middle = tokens_ref[...].astype(jnp.float32) + contract(
            mixed_col_ref[...].T, 1, out_weight_ref[...], 0
        )
        middle_ref[...] = middle
        normed = (middle * factor_of(middle) * gain_ref[...]).astype(jnp.bfloat16)
        normed_ref[...] = normed
        normed_col_ref[...] = normed.T
        total_ref[...] = jnp.zeros_like(total_ref)
        normed_grad_ref[...] = jnp.zeros_like(normed_grad_ref)

    normed = normed_ref[...]
    gate_weight = gate_weight_ref[...]
    up_weight = up_weight_ref[...]
    down_weight = down_weight_ref[...]
    gate = contract(normed, 1, gate_weight, 0)
    up = contract(normed, 1, up_weight, 0)
    sigma = jax.nn.sigmoid(gate)
    silu = gate * sigma
    hidden = (silu * up).astype(jnp.bfloat16)
    hidden_col_ref[...] = hidden.T
    total_ref[...] += contract(hidden, 1, down_weight, 0)
    hidden_grad = contract(out_grad_ref[...], 1, down_weight, 1)
    gate_grad = (hidden_grad * up * sigma * (1.0 + gate * (1.0 - sigma))).astype(jnp.bfloat16)
    up_grad = (hidden_grad * silu).astype(jnp.bfloat16)
    gate_grad_ref[...] = gate_grad
    up_grad_ref[...] = up_grad
    normed_grad_ref[...] += contract(gate_grad, 1, gate_weight, 1) + contract(
        up_grad, 1, up_weight, 1
    )

    @pl.when(step == pl.num_programs(0) - 1)
    def _():
        middle = middle_ref[...]
        factor = factor_of(middle)
        normed_grad = normed_grad_ref[...]
        result_ref[...] = (middle + total_ref[...]).astype(jnp.bfloat16)
        scaled = normed_grad * gain_ref[...]
        slope = jnp.mean(scaled * middle, axis=-1, keepdims=True)
        middle_grad = out_grad_ref[...].astype(jnp.float32) + factor * (
            scaled - middle * (factor * factor * slope)
        )
        middle_grad_ref[...] = middle_grad
        middle_low = middle_grad.astype(jnp.bfloat16)
        middle_low_ref[...] = middle_low
        dout_cols = contract(out_weight_ref[...], 1, middle_low, 1).astype(jnp.bfloat16)
        for piece in range(pieces):
            dout_piece_ref[piece] = dout_cols[place_of(piece)]
        gain_grad_ref[...] = jnp.sum(normed_grad * middle * factor, axis=0, keepdims=True)


def fixed_spec(shape):
    return pl.BlockSpec(shape, lambda i, *_: (0,) * len(shape), pipeline_mode=pl.Buffered(1))


def feed_forward(tokens, mixed_pieces, gain, out_grad, out, gate, up, down):
    rows = tokens.shape[0]
    wide = pl.BlockSpec((rows, FF_TILE), lambda i: (0, i))
    out_first, gate_first, up_first = (out[1] // D, gate[1] // D, up[1] // D)
    down_first = down[1] // FF_TILE
    square = (rows, D)
    flipped = (D, rows)
    outs = [
        (fixed_spec(square), square, jnp.bfloat16),
        (fixed_spec(square), square, jnp.float32),
        (fixed_spec(square), square, jnp.bfloat16),
        (fixed_spec(mixed_pieces.shape), mixed_pieces.shape, jnp.bfloat16),
        (fixed_spec((1, D)), (1, D), jnp.float32),
        (wide, (rows, FF), jnp.bfloat16),
        (wide, (rows, FF), jnp.bfloat16),
        (pl.BlockSpec((FF_TILE, rows), lambda i: (i, 0)), (FF, rows), jnp.bfloat16),
        (fixed_spec(flipped), flipped, jnp.bfloat16),
        (fixed_spec(flipped), flipped, jnp.bfloat16),
    ]
    return pl.pallas_call(
        feed_forward_kernel,
        grid=(FF // FF_TILE,),
        in_specs=[
            fixed_spec(square),
            fixed_spec(mixed_pieces.shape),
            fixed_spec((1, D)),
            fixed_spec(square),
            pl.BlockSpec((D, D), lambda i: (out_first, 0), pipeline_mode=pl.Buffered(1)),
            pl.BlockSpec((D, FF_TILE), lambda i: (gate_first, i)),
            pl.BlockSpec((D, FF_TILE), lambda i: (up_first, i)),
            pl.BlockSpec((FF_TILE, D), lambda i: (down_first + i, 0)),
        ],
        out_specs=[spec for spec, _, _ in outs],
        out_shape=[jax.ShapeDtypeStruct(shape, kind) for _, shape, kind in outs],
        scratch_shapes=[
            pltpu.VMEM(square, jnp.float32),
            pltpu.VMEM(square, jnp.bfloat16),
            pltpu.VMEM(square, jnp.float32),
            pltpu.VMEM(square, jnp.float32),
        ],
        compiler_params=pltpu.CompilerParams(vmem_limit_bytes=48 << 20),
        cost_estimate=pl.CostEstimate(
            flops=12 * rows * D * FF, transcendentals=rows * FF, bytes_accessed=6 * D * FF
        ),
        name="feed_forward",
    )(tokens, mixed_pieces, gain.reshape(1, D), out_grad, out[0], gate[0], up[0], down[0])


def project_kernel(
    normed_ref, query_weight_ref, key_weight_ref, value_weight_ref, cos_ref, sin_ref, piece_ref
):
    normed = normed_ref[...]
    cosine = cos_ref[...]
    sine_part = sin_ref[...]
    query_cols = contract(normed, 1, query_weight_ref[...], 0).T
    key_cols = contract(normed, 1, key_weight_ref[...], 0).T
    value_cols = contract(normed, 1, value_weight_ref[...], 0).T
    key_heads = key_cols.shape[0] // HEAD_DIM
    pieces, _, cols = piece_ref.shape
    parts = pieces // (2 * key_heads)

    def head(columns, number):
        return columns[number * HEAD_DIM : (number + 1) * HEAD_DIM]

    for key_head in range(key_heads):
        for half in range(2):
            owner = 2 * key_head + half
            query = rotate(head(query_cols, owner), cosine, sine_part)
            if half == 0:
                other = rotate(head(key_cols, key_head), cosine, sine_part)
            else:
                other = head(value_cols, key_head)
            both = jnp.concatenate([query, other], axis=0).astype(jnp.bfloat16)
            for part in range(parts):
                piece_ref[owner * parts + part] = both[:, part * cols : (part + 1) * cols]


def project(normed, query, key, value, cosine, sine_part, cols):
    rows = normed.shape[0]
    steps = 2
    pieces = HEADS * rows // cols
    query_first, key_first, value_first = (query[1] // D, key[1] // D, value[1] // D)
    query_cols = HEADS * HEAD_DIM // steps
    key_cols = KV_HEADS * HEAD_DIM // steps
    return pl.pallas_call(
        project_kernel,
        grid=(steps,),
        in_specs=[
            fixed_spec(normed.shape),
            pl.BlockSpec((D, query_cols), lambda i: (query_first, i)),
            pl.BlockSpec((D, key_cols), lambda i: (key_first, i)),
            pl.BlockSpec((D, key_cols), lambda i: (value_first, i)),
            fixed_spec(cosine.shape),
            fixed_spec(sine_part.shape),
        ],
        out_specs=pl.BlockSpec((pieces // steps, 2 * HEAD_DIM, cols), lambda i: (i, 0, 0)),
        out_shape=jax.ShapeDtypeStruct((pieces, 2 * HEAD_DIM, cols), jnp.bfloat16),
        compiler_params=pltpu.CompilerParams(vmem_limit_bytes=40 << 20),
        cost_estimate=pl.CostEstimate(
            flops=4 * rows * D * 2 * D, transcendentals=0, bytes_accessed=4 * D * 2 * D
        ),
        name="project",
    )(normed, query[0], key[0], value[0], cosine, sine_part)


def live_pairs(rel_ref, pos, start, base, queries):
    rel = rel_ref[...]
    rel = jnp.concatenate([rel] * (queries // rel.shape[1]), axis=1)
    return (rel >= start - base) & (rel <= pos - base)


def side_by_side(ref):
    return jnp.concatenate([ref[piece] for piece in range(ref.shape[0])], axis=1)


def stacked_rows(ref):
    return jnp.concatenate([ref[piece].T for piece in range(ref.shape[0])], axis=0)


def forward_kernel(low_ref, high_ref, half_ref, query_ref, *refs, slots):
    own_refs, other_refs = (refs[:slots], refs[slots : 2 * slots])
    pos_ref, start_ref, rel_ref, out_ref, piece_ref, lse_ref, key_ref, value_ref = refs[2 * slots :]
    tile = pl.program_id(0)
    keys = rel_ref.shape[0]
    per_slot = keys // (slots * LANES)

    def lay_out(key_refs, value_refs):
        def body(step, carried):
            for slot in range(slots):
                for piece in range(per_slot):
                    place = (slot * per_slot + piece) * LANES
                    source = step * per_slot + piece
                    rows = pl.ds(pl.multiple_of(step * keys + place, LANES), LANES)
                    key_ref[rows, :] = key_refs[slot][source].T
                    value_ref[step, :, place : place + LANES] = value_refs[slot][source]
            return carried

        lax.fori_loop(0, value_ref.shape[0], body, 0)

    @pl.when((tile == 0) & (half_ref[0] == 0))
    def _():
        lay_out(own_refs, other_refs)

    @pl.when((tile == 0) & (half_ref[0] != 0))
    def _():
        lay_out(other_refs, own_refs)

    query_cols = side_by_side(query_ref)
    queries = query_cols.shape[1]
    pos = pos_ref[0]
    start = start_ref[0]

    def body(step, carried):
        run_max, run_total, mixed = carried
        rows = pl.ds(pl.multiple_of(step * keys, keys), keys)
        scores = contract(key_ref[rows, :], 1, query_cols, 0)
        live = live_pairs(rel_ref, pos, start, step * keys, queries)
        scores = jnp.where(live, scores, NEG_LARGE)
        new_max = jnp.maximum(run_max, jnp.max(scores, axis=0, keepdims=True))
        weights = jnp.exp2((scores - new_max) * SCORE_BASE_TWO)
        keep = jnp.exp2((run_max - new_max) * SCORE_BASE_TWO)
        run_total = run_total * keep + jnp.sum(weights, axis=0, keepdims=True)
        mixed = mixed * keep + contract(value_ref[step], 1, weights.astype(jnp.bfloat16), 0)
        return (new_max, run_total, mixed)

    start_state = (
        jnp.full((1, queries), NEG_LARGE, jnp.float32),
        jnp.zeros((1, queries), jnp.float32),
        jnp.zeros((HEAD_DIM, queries), jnp.float32),
    )
    run_max, run_total, mixed = lax.fori_loop(low_ref[tile], high_ref[tile], body, start_state)
    mixed = mixed / run_total
    out_ref[0] = mixed
    for piece in range(piece_ref.shape[0]):
        piece_ref[piece] = mixed[:, piece * LANES : (piece + 1) * LANES].astype(jnp.bfloat16)
    lse_ref[0] = run_max * SCORE_BASE_TWO + jnp.log2(run_total)


def backward_kernel(
    low_ref,
    high_ref,
    query_ref,
    dout_ref,
    out_ref,
    lse_ref,
    key_ref,
    key_col_ref,
    value_ref,
    pos_ref,
    start_ref,
    rel_ref,
    cos_ref,
    sin_ref,
    dquery_ref,
    kept_ref,
    sent_ref,
    dkey_ref,
    dvalue_ref,
):
    tile = pl.program_id(0)

    @pl.when(tile == 0)
    def _():
        dkey_ref[...] = jnp.zeros_like(dkey_ref)
        dvalue_ref[...] = jnp.zeros_like(dvalue_ref)

    query_cols = side_by_side(query_ref)
    query_rows = stacked_rows(query_ref)
    dout_cols = side_by_side(dout_ref)
    dout_rows = stacked_rows(dout_ref)
    queries = query_cols.shape[1]
    keys = rel_ref.shape[0]
    pos = pos_ref[0]
    start = start_ref[0]
    lse = lse_ref[0]
    delta = jnp.sum(dout_cols.astype(jnp.float32) * out_ref[0], axis=0, keepdims=True)

    def body(step, dquery):
        rows = pl.ds(pl.multiple_of(step * keys, keys), keys)
        scores = contract(key_ref[rows, :], 1, query_cols, 0)
        live = live_pairs(rel_ref, pos, start, step * keys, queries)
        weights = jnp.where(live, jnp.exp2(scores * SCORE_BASE_TWO - lse), 0.0)
        weight_grad = contract(value_ref[rows, :], 1, dout_cols, 0)
        dscore = (weights * (weight_grad - delta)).astype(jnp.bfloat16)
        dvalue_ref[rows, :] += contract(weights.astype(jnp.bfloat16), 1, dout_rows, 0)
        dkey_ref[rows, :] += contract(dscore, 1, query_rows, 0)
        return dquery + contract(key_col_ref[step], 1, dscore, 0)

    dquery = lax.fori_loop(
        low_ref[tile], high_ref[tile], body, jnp.zeros((HEAD_DIM, queries), jnp.float32)
    )
    dquery = dquery * SCORE_SCALE
    for piece in range(dquery_ref.shape[0]):
        dquery_ref[piece] = rotate(
            dquery[:, piece * LANES : (piece + 1) * LANES], cos_ref[piece], -sin_ref[piece]
        ).astype(jnp.bfloat16)

    @pl.when(tile == pl.num_programs(0) - 1)
    def _():
        kept_slots = kept_ref.shape[1]
        per_slot = keys // (2 * kept_slots * LANES)

        def lay_out(step, carried):
            for slot in range(2 * kept_slots):
                for piece in range(per_slot):
                    place = (slot * per_slot + piece) * LANES
                    source = step * per_slot + piece
                    rows = pl.ds(pl.multiple_of(step * keys + place, LANES), LANES)
                    found = (dkey_ref[rows, :].T * SCORE_SCALE, dvalue_ref[rows, :].T)
                    for kind in range(2):
                        if slot < kept_slots:
                            kept_ref[kind, slot, source] = found[kind]
                        else:
                            sent_ref[kind, slot - kept_slots, source] = found[kind].astype(
                                sent_ref.dtype
                            )
            return carried

        lax.fori_loop(0, dkey_ref.shape[0] // keys, lay_out, 0)


def whole_spec(array):
    return pl.BlockSpec(array.shape, lambda i, *_: (0,) * array.ndim)


def tile_spec(array):
    return pl.BlockSpec((1,) + array.shape[1:], lambda i, *_: (i,) + (0,) * (array.ndim - 1))


def piece_spec(array):
    per_tile = QUERY_TILE // LANES
    return pl.BlockSpec((per_tile, min(array.shape[1], HEAD_DIM), LANES), lambda i, *_: (i, 0, 0))


def run_kernel(body, name, scalars, grid, inputs, outputs, scratch, flops):
    return pl.pallas_call(
        body,
        grid_spec=pltpu.PrefetchScalarGridSpec(
            num_scalar_prefetch=len(scalars),
            grid=(grid,),
            in_specs=[spec for _, spec in inputs],
            out_specs=[spec for _, spec in outputs],
            scratch_shapes=scratch,
        ),
        out_shape=[shape for shape, _ in outputs],
        compiler_params=pltpu.CompilerParams(vmem_limit_bytes=52 << 20),
        cost_estimate=pl.CostEstimate(
            flops=flops, transcendentals=flops // 400, bytes_accessed=16 << 20
        ),
        name=name,
    )(*scalars, *[array for array, _ in inputs])


def attend(query_pieces, own, other, half, pos, start, rel, low, high):
    tiles, _, queries = pos.shape
    key_total = own[0].shape[0] * LANES * len(own)
    key_tile = rel.shape[0]
    kind = jax.ShapeDtypeStruct
    pieces = kind((tiles * queries // LANES, HEAD_DIM, LANES), jnp.bfloat16)
    outputs = [
        kind((tiles, HEAD_DIM, queries), jnp.float32),
        pieces,
        kind((tiles, 1, queries), jnp.float32),
        kind((key_total, HEAD_DIM), jnp.bfloat16),
        kind((key_total // key_tile, HEAD_DIM, key_tile), jnp.bfloat16),
    ]
    return run_kernel(
        functools.partial(forward_kernel, slots=len(own)),
        "attention_forward",
        (low, high, half),
        tiles,
        [(query_pieces, piece_spec(query_pieces))]
        + [(each, fixed_spec(each.shape)) for each in own + other]
        + [(pos, tile_spec(pos)), (start, tile_spec(start)), (rel, fixed_spec(rel.shape))],
        [
            (outputs[0], tile_spec(outputs[0])),
            (outputs[1], piece_spec(outputs[1])),
            (outputs[2], tile_spec(outputs[2])),
            (outputs[3], fixed_spec(outputs[3].shape)),
            (outputs[4], fixed_spec(outputs[4].shape)),
        ],
        [],
        20_000_000_000,
    )


def attend_back(
    query_pieces,
    dout_pieces,
    out_cols,
    lse,
    key_rows,
    key_cols,
    value_rows,
    pos,
    start,
    rel,
    cosine,
    sine_part,
    low,
    high,
    slots,
    sent_kind,
):
    tiles, _, queries = pos.shape
    sources = key_rows.shape[0] // (slots * LANES)
    grads = (2, slots // 2, sources, HEAD_DIM, LANES)
    outputs = [
        jax.ShapeDtypeStruct((tiles * queries // LANES, HEAD_DIM, LANES), jnp.bfloat16),
        jax.ShapeDtypeStruct(grads, jnp.float32),
        jax.ShapeDtypeStruct(grads, sent_kind),
    ]
    return run_kernel(
        backward_kernel,
        "attention_backward",
        (low, high),
        tiles,
        [
            (query_pieces, piece_spec(query_pieces)),
            (dout_pieces, piece_spec(dout_pieces)),
            (out_cols, tile_spec(out_cols)),
            (lse, tile_spec(lse)),
            (key_rows, fixed_spec(key_rows.shape)),
            (key_cols, fixed_spec(key_cols.shape)),
            (value_rows, fixed_spec(value_rows.shape)),
            (pos, tile_spec(pos)),
            (start, tile_spec(start)),
            (rel, fixed_spec(rel.shape)),
            (cosine, piece_spec(cosine)),
            (sine_part, piece_spec(sine_part)),
        ],
        [
            (outputs[0], piece_spec(outputs[0])),
            (outputs[1], fixed_spec(grads)),
            (outputs[2], fixed_spec(grads)),
        ],
        [pltpu.VMEM(key_rows.shape, jnp.float32)] * 2,
        50_000_000_000,
    )


def per_device(
    tokens,
    segment_ids,
    out_grad,
    attn_master,
    attn_first,
    attn_second,
    ffn_master,
    ffn_first,
    ffn_second,
):
    index = lax.axis_index("seq")
    count = lax.axis_size("seq")
    rows = tokens.shape[0]
    total = rows * count
    group = count // KV_HEADS
    parts = group // 2
    span = rows // parts
    half = (index // parts) % 2
    part = index % parts

    def exchange(value):
        return lax.all_to_all(value, "seq", 0, 0, tiled=True)

    def swapped(value, bit):
        return lax.ppermute(value, "seq", [(i, i ^ bit) for i in range(count)])

    attn_low = attn_master.astype(jnp.bfloat16)
    ffn_low = ffn_master.astype(jnp.bfloat16)
    notice = jnp.concatenate(
        [attn_low[:D], ffn_low[:D], segment_ids.astype(jnp.bfloat16)]
    ).reshape(1, -1, 128)
    notices = exchange(jnp.broadcast_to(notice, (count,) + notice.shape[1:]))

    inputs = tokens.astype(jnp.float32)

    def from_notices(notices):
        gains = notices[0, : 2 * D // 128].astype(jnp.float32).reshape(2, D)
        all_ids = notices[:, 2 * D // 128 :].astype(jnp.int32).reshape(-1)
        held_ids = lax.dynamic_index_in_dim(
            all_ids.reshape(count, parts, span), part, 1, keepdims=False
        )

        def item_starts(ids):
            return jnp.sum((all_ids < ids[..., None]).astype(jnp.int32), axis=-1)

        return (
            gains[0],
            gains[1],
            rms_norm(inputs, gains[0]).astype(jnp.bfloat16),
            item_starts(held_ids.reshape(-1)),
            item_starts(all_ids[:: QUERY_TILE // span * rows]) // KEY_TILE,
        )

    grid = device_grid(count)
    by_axes = (D // count) % 16 == 0

    def sum_of(left_cols, right, right_dim, order):
        left = reordered(left_cols, slot_table(index, grid, order))
        return SummedRows(left, right, right_dim, order, grid)

    def scattered(left_cols, right, right_dim):
        whole = contract(left_cols, 1, right, right_dim).astype(jnp.bfloat16)
        return (
            lax.psum_scatter(whole, "seq", scatter_dimension=0, tiled=True)
            .reshape(-1)
            .astype(jnp.float32)
        )

    attn_block = aligned_block(attn_low, index, count)
    ffn_block = aligned_block(ffn_low, index, count)
    if by_axes:
        own_tiles = unit_tiles(ffn_block, (FF, FF, D), index, count)
        attn_tiles, own_tiles, beside = gather_tiles(
            unit_tiles(attn_block, (D, KV_HEADS * HEAD_DIM, D), index, count),
            index,
            grid,
            notices,
            own_tiles,
            from_notices,
        )
        ffn_tiles = lax.all_gather(own_tiles, "seq", axis=0, tiled=True)
        wide_rows = matrix_of(ffn_tiles, FF)
        gate_weight = (wide_rows, 0)
        up_weight = (wide_rows, D)
        down_weight = (matrix_of(ffn_tiles, D), 2 * FF)
        attn_wide = matrix_of(attn_tiles, D)
        attn_narrow = matrix_of(attn_tiles, KV_HEADS * HEAD_DIM)
        query_weight = (attn_wide, 0)
        key_weight = (attn_narrow, 2 * D)
        value_weight = (attn_narrow, 3 * D)
        out_weight = (attn_wide, 2 * D)
    else:

        def gathered(unit, width):
            return lax.all_gather(unit.reshape(-1, width), "seq", axis=0, tiled=True)

        q_unit, kv_unit, o_unit = units_from_block(attn_block, index, count)
        gate_unit, up_unit, down_unit = units_from_block(ffn_block, index, count)
        query_weight = (gathered(q_unit, HEADS * HEAD_DIM), 0)
        key_value_weight = gathered(kv_unit, KV_HEADS * HEAD_DIM)
        key_weight = (key_value_weight, 0)
        value_weight = (key_value_weight, D)
        out_weight = (gathered(o_unit, D), 0)
        gate_weight = (gathered(gate_unit, FF), 0)
        up_weight = (gathered(up_unit, FF), 0)
        down_weight = (gathered(down_unit, D), 0)

    gain_one, gain_two, normed_one, held_starts, low = (
        beside if by_axes else from_notices(notices)
    )

    own_places = index * rows + jnp.arange(rows, dtype=jnp.int32)
    own_cos, own_sin = angle_tables(own_places)

    cols = span if span % 128 == 0 else rows

    def by_owner(value):
        if value.shape[0] == count:
            return value
        pieces = value.reshape(HEADS, value.shape[1], parts, span)
        return jnp.swapaxes(pieces, 1, 2).reshape(count, value.shape[1], span)

    def by_head(value):
        pieces = value.reshape(HEADS, parts, value.shape[1], span)
        return jnp.swapaxes(pieces, 1, 2).reshape(HEADS, value.shape[1], rows)

    received = exchange(
        by_owner(
            project(normed_one, query_weight, key_weight, value_weight, own_cos, own_sin, cols)
        )
    )

    merged = LANES // span

    def to_pieces(value):
        if merged == 1:
            return value
        pieces = value.reshape(count // merged, merged, value.shape[1], span)
        return jnp.swapaxes(pieces, 1, 2).reshape(count // merged, value.shape[1], LANES)

    def from_pieces(value):
        if merged == 1:
            return value
        pieces = value.reshape(count // merged, value.shape[1], merged, span)
        return jnp.swapaxes(pieces, 1, 2).reshape(count, value.shape[1], span)

    own_kind = received[:, HEAD_DIM:]
    both_kinds = [[own_kind], [swapped(own_kind, parts)]]
    bit = 1
    while bit < parts:
        both_kinds = [kind + [swapped(each, bit) for each in kind] for kind in both_kinds]
        bit = bit * 2
    own, other = [[to_pieces(each) for each in kind] for kind in both_kinds]
    query_pieces = to_pieces(received)
    sources = QUERY_TILE // span
    tiles = count // sources
    within = jnp.arange(span, dtype=jnp.int32)
    rel = (
        span * (part ^ jnp.arange(parts, dtype=jnp.int32))[:, None, None]
        + rows * jnp.arange(KEY_TILE // rows, dtype=jnp.int32)[None, :, None]
        + within[None, None, :]
    ).reshape(KEY_TILE, 1)
    rel = jnp.broadcast_to(rel, (KEY_TILE, LANES))
    held_places = (
        rows * jnp.arange(count, dtype=jnp.int32)[:, None] + span * part + within[None, :]
    )
    pos = held_places.reshape(tiles, 1, QUERY_TILE)
    start = held_starts.reshape(tiles, 1, QUERY_TILE)
    tile_span = sources * rows
    high = (jnp.arange(1, tiles + 1, dtype=jnp.int32) * tile_span + KEY_TILE - 1) // KEY_TILE

    chunks = []
    chunk = min(CHUNK, total)
    per_tile = QUERY_TILE // LANES
    for first in range(0, total, chunk):
        of_tiles = slice(first // tile_span, (first + chunk) // tile_span)
        of_queries = slice(of_tiles.start * per_tile, of_tiles.stop * per_tile)
        first_key = max(0, first - SEG_MOST) // KEY_TILE
        last_key = (first + chunk) // KEY_TILE
        per_piece = merged * rows
        of_keys = slice(
            first_key * KEY_TILE // per_piece, last_key * KEY_TILE // per_piece
        )
        chunks.append((of_tiles, of_queries, first_key, of_keys))

    attended = []
    for of_tiles, of_queries, first_key, of_keys in chunks:
        shift = first_key * KEY_TILE
        attended.append(
            attend(
                query_pieces[of_queries],
                [each[of_keys] for each in own],
                [each[of_keys] for each in other],
                half.reshape(1),
                pos[of_tiles] - shift,
                start[of_tiles] - shift,
                rel,
                low[of_tiles] - first_key,
                high[of_tiles] - first_key,
            )
        )
    mixed_pieces = exchange(
        from_pieces(jnp.concatenate([piece[1] for piece in attended]))
    )
    held = []
    for out_cols, _, lse, key_rows, value_cols in attended:
        key_cols = jnp.swapaxes(key_rows.reshape(-1, KEY_TILE, HEAD_DIM), 1, 2)
        value_rows = jnp.swapaxes(value_cols, 1, 2).reshape(-1, HEAD_DIM)
        held.append((out_cols, lse, key_rows, key_cols, value_rows))
    held_cos, held_sin = [to_pieces(table) for table in angle_tables(held_places)]
    mixed_pieces, (held, held_cos, held_sin) = together(
        mixed_pieces, (held, held_cos, held_sin)
    )
    if cols == rows:
        mixed_pieces = by_head(mixed_pieces)

    (
        result,
        middle_grad,
        middle_low,
        dout_pieces,
        grad_two,
        gate_grad,
        up_grad,
        hidden_cols,
        normed_two_cols,
        mixed_low,
    ) = feed_forward(
        tokens,
        mixed_pieces,
        gain_two,
        out_grad,
        out_weight,
        gate_weight,
        up_weight,
        down_weight,
    )
    dout_received = exchange(by_owner(dout_pieces))
    if by_axes:
        gate_sum = sum_of(normed_two_cols, gate_grad, 0, GATE_ORDER)
        up_sum = sum_of(normed_two_cols, up_grad, 0, UP_ORDER)
        down_sum = sum_of(hidden_cols, out_grad, 0, DOWN_ORDER)
        first_sums = [gate_sum, up_sum]
        make_and_send(first_sums + [down_sum])
        dout_received = made_before(first_sums, dout_received)
        for each in first_sums:
            each.send()
    else:
        ffn_units = [
            scattered(normed_two_cols, gate_grad, 0),
            scattered(normed_two_cols, up_grad, 0),
            scattered(hidden_cols, out_grad, 0),
        ]
        out_unit = scattered(mixed_low, middle_low, 0)
    dout_pieces = to_pieces(dout_received)

    one_chunk = len(chunks) == 1
    dquery_pieces = []
    summed = [jnp.zeros((2, max(parts // 2, 1), count // merged, HEAD_DIM, LANES), jnp.float32)] * 2
    for (of_tiles, of_queries, first_key, of_keys), kept_values in zip(chunks, held):
        shift = first_key * KEY_TILE
        dquery_piece, *found = attend_back(
            query_pieces[of_queries],
            dout_pieces[of_queries],
            *kept_values,
            pos[of_tiles] - shift,
            start[of_tiles] - shift,
            rel,
            held_cos[of_queries],
            held_sin[of_queries],
            low[of_tiles] - first_key,
            high[of_tiles] - first_key,
            parts,
            jnp.bfloat16 if one_chunk else jnp.float32,
        )
        dquery_pieces.append(dquery_piece)
        if one_chunk:
            summed = found
        else:
            summed = [
                whole.at[:, :, of_keys].add(piece) for whole, piece in zip(summed, found)
            ]
    dquery_held = from_pieces(jnp.concatenate(dquery_pieces))
    grads, sent = summed
    if by_axes:
        mixed_late, grads = together(mixed_low, grads)
        out_sum = sum_of(mixed_late, middle_low, 0, OUT_ORDER)
    grads = grads + swapped(sent.astype(jnp.bfloat16), parts // 2)
    bit = parts // 4
    while bit >= 1:
        grads = grads[:, :bit] + swapped(grads[:, bit:].astype(jnp.bfloat16), bit)
        bit = bit // 2
    if by_axes:
        grads = taken_after(first_sums, grads)
    dkey_held, dvalue_held = (grads[0, 0], grads[1, 0])
    sent_kind = jnp.where(half == 0, dvalue_held, dkey_held).astype(jnp.bfloat16)
    kept_kind = jnp.where(half == 0, dkey_held, dvalue_held) + swapped(sent_kind, parts)
    kept_low = from_pieces(
        jnp.where(half == 0, rotate(kept_kind, held_cos, -held_sin), kept_kind).astype(
            jnp.bfloat16
        )
    )
    sent_back = jnp.concatenate([dquery_held, kept_low], axis=1)
    if by_axes:
        early_sums = first_sums + [down_sum]
        sent_back = made_before(early_sums, sent_back)
        for each in early_sums:
            each.send()
    returned = exchange(sent_back)
    if by_axes:
        make_and_send([out_sum])
        returned = taken_after([down_sum], made_before(first_sums, returned))
        for each in first_sums:
            each.send()
    dquery_low = by_head(returned[:, :HEAD_DIM]).reshape(HEADS * HEAD_DIM, rows)
    pair_low = by_head(returned[:, HEAD_DIM:]).reshape(KV_HEADS, 2, HEAD_DIM, rows)
    dkey_low = pair_low[:, 0].reshape(KV_HEADS * HEAD_DIM, rows)
    dvalue_low = pair_low[:, 1].reshape(KV_HEADS * HEAD_DIM, rows)

    normed_one_cols = normed_one.T
    nothing = jnp.zeros_like(normed_one_cols)
    key_value_cols = jnp.concatenate(
        [
            jnp.concatenate([normed_one_cols, nothing], axis=1),
            jnp.concatenate([nothing, normed_one_cols], axis=1),
        ]
    )
    key_value_right = jnp.concatenate([dkey_low, dvalue_low], axis=1)
    if by_axes:
        query_sum = sum_of(normed_one_cols, dquery_low, 1, GATE_ORDER)
        key_value_sum = sum_of(key_value_cols, key_value_right, 1, UP_ORDER)
        last_sums = [query_sum, key_value_sum]
        make_and_send(last_sums)
        for each in last_sums:
            each.make()
        taken_after(early_sums + [out_sum], [each.made for each in last_sums])
        for each in last_sums:
            each.send()
        dquery_late = taken_after(last_sums, dquery_low)
        make_and_send([gate_sum, up_sum, down_sum, out_sum])
        normed_one_grad = (
            contract(dquery_late, 0, query_weight[0][:D], 1)
            + contract(dkey_low, 0, key_weight[0][key_weight[1] : key_weight[1] + D], 1)
            + contract(dvalue_low, 0, value_weight[0][value_weight[1] : value_weight[1] + D], 1)
        )
        _, first_pull = jax.vjp(rms_norm, inputs, gain_one)
        input_norm_grad, grad_one = first_pull(normed_one_grad)
        input_grad = middle_grad + input_norm_grad

        gain_sum = SummedWhole(jnp.concatenate([grad_one, grad_two[0]]).reshape(-1, 128), grid)
        attn_sums = last_sums + [out_sum]
        make_and_send([gain_sum])
        one_round(attn_sums + early_sums + [gain_sum])
        one_round(attn_sums + [down_sum, gain_sum])
        one_round(attn_sums + [down_sum, gain_sum])
        ffn_units = [gate_sum.result(), up_sum.result(), down_sum.result()]
        one_round(attn_sums + [gain_sum])
        gain_grads = gain_sum.result().reshape(2, D)
        query_unit, key_value_unit, out_unit = [each.result() for each in attn_sums]
    else:
        query_unit = scattered(normed_one_cols, dquery_low, 1)
        key_value_unit = scattered(key_value_cols, key_value_right, 1)
        normed_one_grad = (
            contract(dquery_low, 0, query_weight[0][:D], 1)
            + contract(dkey_low, 0, key_weight[0][key_weight[1] : key_weight[1] + D], 1)
            + contract(dvalue_low, 0, value_weight[0][value_weight[1] : value_weight[1] + D], 1)
        )
        _, first_pull = jax.vjp(rms_norm, inputs, gain_one)
        input_norm_grad, grad_one = first_pull(normed_one_grad)
        input_grad = middle_grad + input_norm_grad

        gain_grads = lax.psum(jnp.stack([grad_one, grad_two[0]]), "seq")
    ffn_shard = shard_from_units(ffn_units, gain_grads[1], index, count)
    attn_shard = shard_from_units(
        [query_unit, key_value_unit, out_unit], gain_grads[0], index, count
    )
    attn_new, attn_one, attn_two = adam_update(
        attn_master, attn_first, attn_second, attn_shard
    )
    ffn_new, ffn_one, ffn_two = adam_update(
        ffn_master, ffn_first, ffn_second, ffn_shard
    )
    return (result, input_grad, attn_new, attn_one, attn_two, ffn_new, ffn_one, ffn_two)


def solution(mesh):
    rows_cut = P("seq", None)
    flat_cut = P("seq")
    in_specs = (rows_cut, flat_cut, rows_cut) + (flat_cut,) * 6
    out_specs = (rows_cut, rows_cut) + (flat_cut,) * 6
    return jax.shard_map(
        per_device, mesh=mesh, in_specs=in_specs, out_specs=out_specs, check_vma=False
    )
```

```python
import functools
import math

import jax
import jax.numpy as jnp
from jax import lax
from jax.experimental import pallas as pl
from jax.experimental.pallas import tpu as pltpu
from jax.sharding import PartitionSpec as P

D = 1536
HEADS = 16
KV_HEADS = 8
HEAD_DIM = 96
FF = 4096
SEG_MOST = 4096
STEP = 7


ROPE_BASE = 100000.0
NORM_EPS = 1e-05
BETA_ONE = 0.5
BETA_TWO = 0.5
LEARN_RATE = 0.04
DECAY = 0.1
ADAM_EPS = 1e-08
NEG_LARGE = -1e30
HALF_DIM = HEAD_DIM // 2
QUERY_TILE = 512
KEY_TILE = 1024
CHUNK = 8192
LANES = 128
FF_TILE = 512
SCORE_BASE_TWO = math.log2(math.e) / math.sqrt(HEAD_DIM)
SCORE_SCALE = 1.0 / math.sqrt(HEAD_DIM)


def rms_norm(values, norm_gain):
    factor = lax.rsqrt(jnp.mean(values * values, axis=-1, keepdims=True) + NORM_EPS)
    return values * factor * norm_gain


def angle_tables(positions):
    frequency = jnp.exp(
        jnp.arange(HALF_DIM).astype(jnp.float32) * (-2.0 * math.log(ROPE_BASE) / HEAD_DIM)
    )
    angles = positions.astype(jnp.float32)[..., None, :] * frequency[:, None]
    return (jnp.cos(angles), jnp.sin(angles))


def rotate(values, cosine, sine_part):
    lower_part = values[..., :HALF_DIM, :]
    upper_part = values[..., HALF_DIM:, :]
    return jnp.concatenate(
        [
            lower_part * cosine - upper_part * sine_part,
            upper_part * cosine + lower_part * sine_part,
        ],
        axis=-2,
    )


def contract(left, left_dim, right, right_dim):
    return lax.dot_general(
        left,
        right,
        (((left_dim,), (right_dim,)), ((), ())),
        preferred_element_type=jnp.float32,
    )


def adam_update(master, moment_one, moment_two, gradient):
    first_new = BETA_ONE * moment_one + (1.0 - BETA_ONE) * gradient
    second_new = BETA_TWO * moment_two + (1.0 - BETA_TWO) * gradient * gradient
    first_hat = first_new / (1.0 - BETA_ONE**STEP)
    second_hat = second_new / (1.0 - BETA_TWO**STEP)
    master_new = master - LEARN_RATE * (
        first_hat / (jnp.sqrt(second_hat) + ADAM_EPS) + DECAY * master
    )
    return (master_new, first_new, second_new)


def aligned_block(flat_low, index, count):
    edge = D // count
    block = flat_low.shape[0] - edge
    following = lax.ppermute(flat_low[:D], "seq", [(i + 1, i) for i in range(count - 1)])
    extended = jnp.concatenate([flat_low, following])
    return lax.dynamic_slice(extended, (D - edge * index,), (block,))


def tiles_of(unit, width):
    pieces = unit.reshape(-1, 8, width // 128, 128)
    return jnp.swapaxes(pieces, 1, 2).reshape(-1, 8, 128)


def matrix_of(tiles, width):
    pieces = tiles.reshape(-1, width // 128, 8, 128)
    return jnp.swapaxes(pieces, 1, 2).reshape(-1, width)


def unit_tiles(block, widths, index, count):
    units = block.reshape(3, -1)
    made = []
    for j in range(3):
        kind = (3 * index + j) // count
        made.append(
            lax.select_n(kind, *[tiles_of(units[j], width) for width in widths])
        )
    return jnp.concatenate(made)


def units_from_block(block, index, count):
    aligned = block.reshape(3, -1)
    dealt = jnp.stack(
        [
            lax.ppermute(aligned[j], "seq", [(i, (3 * i + j) % count) for i in range(count)])
            for j in range(3)
        ]
    )
    return [
        lax.dynamic_index_in_dim(dealt, slot_of_kind(index, kind, count), 0, keepdims=False)
        for kind in range(3)
    ]


def slot_of_kind(index, kind, count):
    return (index + count * kind) % 3


def shard_from_units(units, gain_grad, index, count):
    edge = D // count
    units = [unit.astype(jnp.bfloat16) for unit in units]
    unit = units[0].shape[0]
    returned = []
    for j in range(3):
        inverse = 1 if count % 3 == 1 else 2
        kind = ((j - index) * inverse) % 3
        piece = jnp.where(kind == 0, units[0], jnp.where(kind == 1, units[1], units[2]))
        returned.append(
            lax.ppermute(piece, "seq", [((3 * i + j) % count, i) for i in range(count)])
        )
    before = lax.ppermute(returned[2][-D:], "seq", [(i, i + 1) for i in range(count - 1)])
    before = jnp.where(index == 0, gain_grad, before.astype(jnp.float32))
    extended = jnp.concatenate([before] + [piece.astype(jnp.float32) for piece in returned])
    return lax.dynamic_slice(extended, (edge * index,), (3 * unit + edge,))


AXES = ("z", "y", "x")
GATHER_ORDERS = (("core", "x", "y", "z"), ("core", "y", "x", "z"))
GATE_ORDER = ("core", "x", "z", "y")
UP_ORDER = ("core", "y", "z", "x")
DOWN_ORDER = ("core", "y", "x", "z")
OUT_ORDER = ("core", "y", "x", "z")


def device_grid(count):
    chips = count // 2
    sides = {16: (4, 2, 2), 64: (4, 4, 4)}.get(chips, (chips, 1, 1))
    return dict(zip(AXES + ("core",), sides + (2,)))


def coordinates(index, grid):
    found = {}
    for axis in reversed(list(grid)):
        found[axis] = index % grid[axis]
        index = index // grid[axis]
    return found


def place(found, grid):
    index = 0
    for axis in grid:
        index = index * grid[axis] + found[axis]
    return index


def shifted(value, axis, steps, grid):
    pairs = []
    for source in range(math.prod(grid.values())):
        target = coordinates(source, grid)
        target[axis] = (target[axis] + steps) % grid[axis]
        pairs.append((source, place(target, grid)))
    return lax.ppermute(value, "seq", pairs)


def slot_table(index, grid, axes):
    here = coordinates(index, grid)
    entries = []
    for number in range(math.prod(grid.values())):
        slots = coordinates(number, {axis: grid[axis] for axis in axes})
        there = {axis: (here[axis] - slots[axis]) % grid[axis] for axis in grid}
        entries.append(place(there, grid))
    return jnp.stack(entries).astype(jnp.int32)


def place_kernel(table_ref, *refs, lengths):
    pieces = len(lengths)
    piece_refs, out_ref = (refs[:pieces], refs[pieces])
    held, in_sems, out_sems = refs[pieces + 1 :]
    size = held.shape[1]
    loads = []
    for piece_ref, length in zip(piece_refs, lengths):
        for block in range(length):
            entry = len(loads)
            load = pltpu.make_async_copy(
                piece_ref.at[pl.ds(block * size, size)], held.at[entry], in_sems.at[entry]
            )
            load.start()
            loads.append(load)
    stores = []
    for entry, load in enumerate(loads):
        load.wait()
        target = pl.ds(pl.multiple_of(table_ref[entry] * size, size), size)
        store = pltpu.make_async_copy(held.at[entry], out_ref.at[target], out_sems.at[entry])
        store.start()
        stores.append(store)
    for store in stores:
        store.wait()


def placed(pieces, table):
    count = table.shape[0]
    size = sum(piece.shape[0] for piece in pieces) // count
    shape = pieces[0].shape[1:]
    anywhere = pl.BlockSpec(memory_space=pl.ANY)
    return pl.pallas_call(
        functools.partial(
            place_kernel, lengths=tuple(piece.shape[0] // size for piece in pieces)
        ),
        grid_spec=pltpu.PrefetchScalarGridSpec(
            num_scalar_prefetch=1,
            grid=(1,),
            in_specs=[anywhere] * len(pieces),
            out_specs=anywhere,
            scratch_shapes=[
                pltpu.VMEM((count, size) + shape, pieces[0].dtype),
                pltpu.SemaphoreType.DMA((count,)),
                pltpu.SemaphoreType.DMA((count,)),
            ],
        ),
        out_shape=jax.ShapeDtypeStruct((count * size,) + shape, pieces[0].dtype),
        compiler_params=pltpu.CompilerParams(vmem_limit_bytes=48 << 20),
        cost_estimate=pl.CostEstimate(
            flops=0, transcendentals=0, bytes_accessed=4 * count * size * math.prod(shape)
        ),
        name="place_blocks",
    )(table, *pieces)


def gather_tiles(block, index, grid, notices, later, beside_of):
    arrived = [block] + [shifted(block, "z", k, grid) for k in range(1, grid["z"])]
    arrived, notices = together(arrived, notices)
    beside = beside_of(notices)
    half = block.shape[0] // 2
    held = [
        jnp.concatenate([each[color * half : (color + 1) * half] for each in arrived])
        for color in range(2)
    ]
    for turn in (2, 1):
        arrivals = []
        for color, order in enumerate(GATHER_ORDERS):
            axis = order[turn]
            arrivals.append(
                [held[color]]
                + [shifted(held[color], axis, k, grid) for k in range(1, grid[axis])]
            )
        if turn == 1:
            arrivals, beside = together(arrivals, beside)
        else:
            arrivals, later = together(arrivals, later)
            held = [jnp.concatenate(each) for each in arrivals]
    pieces = []
    tables = []
    for color, order in enumerate(GATHER_ORDERS):
        pieces = pieces + arrivals[color]
        pieces = pieces + [shifted(piece, "core", 1, grid) for piece in arrivals[color]]
        tables.append(2 * slot_table(index, grid, order) + color)
    return placed(pieces, jnp.concatenate(tables)), later, beside


def reorder_kernel(table_ref, in_ref, out_ref, *, rows):
    for block in range(in_ref.shape[0] // rows):
        source = pl.ds(pl.multiple_of(table_ref[block] * rows, rows), rows)
        out_ref[block * rows : (block + 1) * rows, :] = in_ref[source, :]


def reordered(value, table):
    rows = value.shape[0] // table.shape[0]
    return pl.pallas_call(
        functools.partial(reorder_kernel, rows=rows),
        grid_spec=pltpu.PrefetchScalarGridSpec(
            num_scalar_prefetch=1,
            grid=(1,),
            in_specs=[whole_spec(value)],
            out_specs=whole_spec(value),
        ),
        out_shape=jax.ShapeDtypeStruct(value.shape, value.dtype),
        cost_estimate=pl.CostEstimate(
            flops=0, transcendentals=0, bytes_accessed=4 * value.size
        ),
        name="reorder_blocks",
    )(table, value)


class SummedRows:

    def __init__(self, left, right, right_dim, order, grid):
        self.left = left
        self.right = right
        self.right_dim = right_dim
        self.grid = grid
        self.rows = left.shape[0] // math.prod(grid.values())
        self.window = left.shape[0]
        self.turns = [(axis, slot) for axis in order for slot in range(grid[axis] - 1, 0, -1)]
        self.received = []
        self.passing = []

    def partial(self, span):
        total = contract(self.left[span], 1, self.right, self.right_dim)
        for part in self.received:
            total = total + part[span]
        return total

    def make(self):
        axis, slot = self.turns[0]
        if slot == self.grid[axis] - 1:
            self.window = self.window // self.grid[axis]
        total = self.partial(slice(slot * self.window, (slot + 1) * self.window))
        for part in self.passing:
            total = total + part
        self.made = total.astype(jnp.bfloat16)

    def send(self):
        axis, slot = self.turns.pop(0)
        arrived = [shifted(self.made, axis, -1, self.grid)]
        if slot > 1:
            self.passing = arrived
        else:
            self.passing = []
            self.received = self.received + arrived

    def result(self):
        return self.partial(slice(0, self.rows)).reshape(-1)


class SummedWhole:

    def __init__(self, value, grid):
        self.value = value
        self.grid = grid
        self.turns = []
        for axis in ("core", "x", "y", "z"):
            step = grid[axis] // 2
            while step >= 1:
                self.turns.append((axis, step))
                step = step // 2
        self.received = []
        self.passing = []

    def make(self):
        for part in self.received:
            self.value = self.value + part
        self.made = self.value

    def send(self):
        axis, step = self.turns.pop(0)
        self.received = [shifted(self.made, axis, step, self.grid)]

    def result(self):
        return self.value + self.received[0]


def together(values, others):
    return lax.optimization_barrier((values, others))


def made_before(sums, value):
    for each in sums:
        each.make()
    value, made = together(value, [each.made for each in sums])
    for each, now in zip(sums, made):
        each.made = now
    return value


def taken_after(sums, value):
    value, arrived = together(value, [(each.received, each.passing) for each in sums])
    for each, now in zip(sums, arrived):
        each.received, each.passing = now
    return value


def one_round(sums):
    taken_after(sums, ())
    make_and_send(sums)


def make_and_send(sums):
    for each in sums:
        each.make()
        each.send()


def feed_forward_kernel(
    tokens_ref,
    mixed_piece_ref,
    gain_ref,
    out_grad_ref,
    out_weight_ref,
    gate_weight_ref,
    up_weight_ref,
    down_weight_ref,
    result_ref,
    middle_grad_ref,
    middle_low_ref,
    dout_piece_ref,
    gain_grad_ref,
    gate_grad_ref,
    up_grad_ref,
    hidden_col_ref,
    normed_col_ref,
    mixed_col_ref,
    middle_ref,
    normed_ref,
    total_ref,
    normed_grad_ref,
):
    step = pl.program_id(0)
    pieces, _, cols = mixed_piece_ref.shape
    per_head = pieces // HEADS

    def factor_of(middle):
        return lax.rsqrt(jnp.mean(middle * middle, axis=-1, keepdims=True) + NORM_EPS)

    def place_of(piece):
        head, part = divmod(piece, per_head)
        return (slice(head * HEAD_DIM, (head + 1) * HEAD_DIM), slice(part * cols, (part + 1) * cols))

    @pl.when(step == 0)
    def _():
        for piece in range(pieces):
            mixed_col_ref[place_of(piece)] = mixed_piece_ref[piece]
        middle = tokens_ref[...].astype(jnp.float32) + contract(
            mixed_col_ref[...].T, 1, out_weight_ref[...], 0
        )
        middle_ref[...] = middle
        normed = (middle * factor_of(middle) * gain_ref[...]).astype(jnp.bfloat16)
        normed_ref[...] = normed
        normed_col_ref[...] = normed.T
        total_ref[...] = jnp.zeros_like(total_ref)
        normed_grad_ref[...] = jnp.zeros_like(normed_grad_ref)

    normed = normed_ref[...]
    gate_weight = gate_weight_ref[...]
    up_weight = up_weight_ref[...]
    down_weight = down_weight_ref[...]
    gate = contract(normed, 1, gate_weight, 0)
    up = contract(normed, 1, up_weight, 0)
    sigma = jax.nn.sigmoid(gate)
    silu = gate * sigma
    hidden = (silu * up).astype(jnp.bfloat16)
    hidden_col_ref[...] = hidden.T
    total_ref[...] += contract(hidden, 1, down_weight, 0)
    hidden_grad = contract(out_grad_ref[...], 1, down_weight, 1)
    gate_grad = (hidden_grad * up * sigma * (1.0 + gate * (1.0 - sigma))).astype(jnp.bfloat16)
    up_grad = (hidden_grad * silu).astype(jnp.bfloat16)
    gate_grad_ref[...] = gate_grad
    up_grad_ref[...] = up_grad
    normed_grad_ref[...] += contract(gate_grad, 1, gate_weight, 1) + contract(
        up_grad, 1, up_weight, 1
    )

    @pl.when(step == pl.num_programs(0) - 1)
    def _():
        middle = middle_ref[...]
        factor = factor_of(middle)
        normed_grad = normed_grad_ref[...]
        result_ref[...] = (middle + total_ref[...]).astype(jnp.bfloat16)
        scaled = normed_grad * gain_ref[...]
        slope = jnp.mean(scaled * middle, axis=-1, keepdims=True)
        middle_grad = out_grad_ref[...].astype(jnp.float32) + factor * (
            scaled - middle * (factor * factor * slope)
        )
        middle_grad_ref[...] = middle_grad
        middle_low = middle_grad.astype(jnp.bfloat16)
        middle_low_ref[...] = middle_low
        dout_cols = contract(out_weight_ref[...], 1, middle_low, 1).astype(jnp.bfloat16)
        for piece in range(pieces):
            dout_piece_ref[piece] = dout_cols[place_of(piece)]
        gain_grad_ref[...] = jnp.sum(normed_grad * middle * factor, axis=0, keepdims=True)


def fixed_spec(shape):
    return pl.BlockSpec(shape, lambda i, *_: (0,) * len(shape), pipeline_mode=pl.Buffered(1))


def feed_forward(tokens, mixed_pieces, gain, out_grad, out, gate, up, down):
    rows = tokens.shape[0]
    wide = pl.BlockSpec((rows, FF_TILE), lambda i: (0, i))
    out_first, gate_first, up_first = (out[1] // D, gate[1] // D, up[1] // D)
    down_first = down[1] // FF_TILE
    square = (rows, D)
    flipped = (D, rows)
    outs = [
        (fixed_spec(square), square, jnp.bfloat16),
        (fixed_spec(square), square, jnp.float32),
        (fixed_spec(square), square, jnp.bfloat16),
        (fixed_spec(mixed_pieces.shape), mixed_pieces.shape, jnp.bfloat16),
        (fixed_spec((1, D)), (1, D), jnp.float32),
        (wide, (rows, FF), jnp.bfloat16),
        (wide, (rows, FF), jnp.bfloat16),
        (pl.BlockSpec((FF_TILE, rows), lambda i: (i, 0)), (FF, rows), jnp.bfloat16),
        (fixed_spec(flipped), flipped, jnp.bfloat16),
        (fixed_spec(flipped), flipped, jnp.bfloat16),
    ]
    return pl.pallas_call(
        feed_forward_kernel,
        grid=(FF // FF_TILE,),
        in_specs=[
            fixed_spec(square),
            fixed_spec(mixed_pieces.shape),
            fixed_spec((1, D)),
            fixed_spec(square),
            pl.BlockSpec((D, D), lambda i: (out_first, 0), pipeline_mode=pl.Buffered(1)),
            pl.BlockSpec((D, FF_TILE), lambda i: (gate_first, i)),
            pl.BlockSpec((D, FF_TILE), lambda i: (up_first, i)),
            pl.BlockSpec((FF_TILE, D), lambda i: (down_first + i, 0)),
        ],
        out_specs=[spec for spec, _, _ in outs],
        out_shape=[jax.ShapeDtypeStruct(shape, kind) for _, shape, kind in outs],
        scratch_shapes=[
            pltpu.VMEM(square, jnp.float32),
            pltpu.VMEM(square, jnp.bfloat16),
            pltpu.VMEM(square, jnp.float32),
            pltpu.VMEM(square, jnp.float32),
        ],
        compiler_params=pltpu.CompilerParams(vmem_limit_bytes=48 << 20),
        cost_estimate=pl.CostEstimate(
            flops=12 * rows * D * FF, transcendentals=rows * FF, bytes_accessed=6 * D * FF
        ),
        name="feed_forward",
    )(tokens, mixed_pieces, gain.reshape(1, D), out_grad, out[0], gate[0], up[0], down[0])


def project_kernel(
    normed_ref, query_weight_ref, key_weight_ref, value_weight_ref, cos_ref, sin_ref, piece_ref
):
    normed = normed_ref[...]
    cosine = cos_ref[...]
    sine_part = sin_ref[...]
    query_cols = contract(normed, 1, query_weight_ref[...], 0).T
    key_cols = contract(normed, 1, key_weight_ref[...], 0).T
    value_cols = contract(normed, 1, value_weight_ref[...], 0).T
    key_heads = key_cols.shape[0] // HEAD_DIM
    pieces, _, cols = piece_ref.shape
    parts = pieces // (2 * key_heads)

    def head(columns, number):
        return columns[number * HEAD_DIM : (number + 1) * HEAD_DIM]

    for key_head in range(key_heads):
        for half in range(2):
            owner = 2 * key_head + half
            query = rotate(head(query_cols, owner), cosine, sine_part)
            if half == 0:
                other = rotate(head(key_cols, key_head), cosine, sine_part)
            else:
                other = head(value_cols, key_head)
            both = jnp.concatenate([query, other], axis=0).astype(jnp.bfloat16)
            for part in range(parts):
                piece_ref[owner * parts + part] = both[:, part * cols : (part + 1) * cols]


def project(normed, query, key, value, cosine, sine_part, cols):
    rows = normed.shape[0]
    steps = 2
    pieces = HEADS * rows // cols
    query_first, key_first, value_first = (query[1] // D, key[1] // D, value[1] // D)
    query_cols = HEADS * HEAD_DIM // steps
    key_cols = KV_HEADS * HEAD_DIM // steps
    return pl.pallas_call(
        project_kernel,
        grid=(steps,),
        in_specs=[
            fixed_spec(normed.shape),
            pl.BlockSpec((D, query_cols), lambda i: (query_first, i)),
            pl.BlockSpec((D, key_cols), lambda i: (key_first, i)),
            pl.BlockSpec((D, key_cols), lambda i: (value_first, i)),
            fixed_spec(cosine.shape),
            fixed_spec(sine_part.shape),
        ],
        out_specs=pl.BlockSpec((pieces // steps, 2 * HEAD_DIM, cols), lambda i: (i, 0, 0)),
        out_shape=jax.ShapeDtypeStruct((pieces, 2 * HEAD_DIM, cols), jnp.bfloat16),
        compiler_params=pltpu.CompilerParams(vmem_limit_bytes=40 << 20),
        cost_estimate=pl.CostEstimate(
            flops=4 * rows * D * 2 * D, transcendentals=0, bytes_accessed=4 * D * 2 * D
        ),
        name="project",
    )(normed, query[0], key[0], value[0], cosine, sine_part)


def live_pairs(rel_ref, pos, start, base, queries):
    rel = rel_ref[...]
    rel = jnp.concatenate([rel] * (queries // rel.shape[1]), axis=1)
    return (rel >= start - base) & (rel <= pos - base)


def side_by_side(ref):
    return jnp.concatenate([ref[piece] for piece in range(ref.shape[0])], axis=1)


def stacked_rows(ref):
    return jnp.concatenate([ref[piece].T for piece in range(ref.shape[0])], axis=0)


def forward_kernel(low_ref, high_ref, half_ref, query_ref, *refs, slots):
    own_refs, other_refs = (refs[:slots], refs[slots : 2 * slots])
    pos_ref, start_ref, rel_ref, out_ref, piece_ref, lse_ref, key_ref, value_ref = refs[2 * slots :]
    tile = pl.program_id(0)
    keys = rel_ref.shape[0]
    per_slot = keys // (slots * LANES)

    def lay_out(key_refs, value_refs):
        def body(step, carried):
            for slot in range(slots):
                for piece in range(per_slot):
                    place = (slot * per_slot + piece) * LANES
                    source = step * per_slot + piece
                    rows = pl.ds(pl.multiple_of(step * keys + place, LANES), LANES)
                    key_ref[rows, :] = key_refs[slot][source].T
                    value_ref[step, :, place : place + LANES] = value_refs[slot][source]
            return carried

        lax.fori_loop(0, value_ref.shape[0], body, 0)

    @pl.when((tile == 0) & (half_ref[0] == 0))
    def _():
        lay_out(own_refs, other_refs)

    @pl.when((tile == 0) & (half_ref[0] != 0))
    def _():
        lay_out(other_refs, own_refs)

    query_cols = side_by_side(query_ref)
    queries = query_cols.shape[1]
    pos = pos_ref[0]
    start = start_ref[0]

    def body(step, carried):
        run_max, run_total, mixed = carried
        rows = pl.ds(pl.multiple_of(step * keys, keys), keys)
        scores = contract(key_ref[rows, :], 1, query_cols, 0)
        live = live_pairs(rel_ref, pos, start, step * keys, queries)
        scores = jnp.where(live, scores, NEG_LARGE)
        new_max = jnp.maximum(run_max, jnp.max(scores, axis=0, keepdims=True))
        weights = jnp.exp2((scores - new_max) * SCORE_BASE_TWO)
        keep = jnp.exp2((run_max - new_max) * SCORE_BASE_TWO)
        run_total = run_total * keep + jnp.sum(weights, axis=0, keepdims=True)
        mixed = mixed * keep + contract(value_ref[step], 1, weights.astype(jnp.bfloat16), 0)
        return (new_max, run_total, mixed)

    start_state = (
        jnp.full((1, queries), NEG_LARGE, jnp.float32),
        jnp.zeros((1, queries), jnp.float32),
        jnp.zeros((HEAD_DIM, queries), jnp.float32),
    )
    run_max, run_total, mixed = lax.fori_loop(low_ref[tile], high_ref[tile], body, start_state)
    mixed = mixed / run_total
    out_ref[0] = mixed
    for piece in range(piece_ref.shape[0]):
        piece_ref[piece] = mixed[:, piece * LANES : (piece + 1) * LANES].astype(jnp.bfloat16)
    lse_ref[0] = run_max * SCORE_BASE_TWO + jnp.log2(run_total)


def backward_kernel(
    low_ref,
    high_ref,
    query_ref,
    dout_ref,
    out_ref,
    lse_ref,
    key_ref,
    key_col_ref,
    value_ref,
    pos_ref,
    start_ref,
    rel_ref,
    cos_ref,
    sin_ref,
    dquery_ref,
    kept_ref,
    sent_ref,
    dkey_ref,
    dvalue_ref,
):
    tile = pl.program_id(0)

    @pl.when(tile == 0)
    def _():
        dkey_ref[...] = jnp.zeros_like(dkey_ref)
        dvalue_ref[...] = jnp.zeros_like(dvalue_ref)

    query_cols = side_by_side(query_ref)
    query_rows = stacked_rows(query_ref)
    dout_cols = side_by_side(dout_ref)
    dout_rows = stacked_rows(dout_ref)
    queries = query_cols.shape[1]
    keys = rel_ref.shape[0]
    pos = pos_ref[0]
    start = start_ref[0]
    lse = lse_ref[0]
    delta = jnp.sum(dout_cols.astype(jnp.float32) * out_ref[0], axis=0, keepdims=True)

    def body(step, dquery):
        rows = pl.ds(pl.multiple_of(step * keys, keys), keys)
        scores = contract(key_ref[rows, :], 1, query_cols, 0)
        live = live_pairs(rel_ref, pos, start, step * keys, queries)
        weights = jnp.where(live, jnp.exp2(scores * SCORE_BASE_TWO - lse), 0.0)
        weight_grad = contract(value_ref[rows, :], 1, dout_cols, 0)
        dscore = (weights * (weight_grad - delta)).astype(jnp.bfloat16)
        dvalue_ref[rows, :] += contract(weights.astype(jnp.bfloat16), 1, dout_rows, 0)
        dkey_ref[rows, :] += contract(dscore, 1, query_rows, 0)
        return dquery + contract(key_col_ref[step], 1, dscore, 0)

    dquery = lax.fori_loop(
        low_ref[tile], high_ref[tile], body, jnp.zeros((HEAD_DIM, queries), jnp.float32)
    )
    dquery = dquery * SCORE_SCALE
    for piece in range(dquery_ref.shape[0]):
        dquery_ref[piece] = rotate(
            dquery[:, piece * LANES : (piece + 1) * LANES], cos_ref[piece], -sin_ref[piece]
        ).astype(jnp.bfloat16)

    @pl.when(tile == pl.num_programs(0) - 1)
    def _():
        kept_slots = kept_ref.shape[1]
        per_slot = keys // (2 * kept_slots * LANES)

        def lay_out(step, carried):
            for slot in range(2 * kept_slots):
                for piece in range(per_slot):
                    place = (slot * per_slot + piece) * LANES
                    source = step * per_slot + piece
                    rows = pl.ds(pl.multiple_of(step * keys + place, LANES), LANES)
                    found = (dkey_ref[rows, :].T * SCORE_SCALE, dvalue_ref[rows, :].T)
                    for kind in range(2):
                        if slot < kept_slots:
                            kept_ref[kind, slot, source] = found[kind]
                        else:
                            sent_ref[kind, slot - kept_slots, source] = found[kind].astype(
                                sent_ref.dtype
                            )
            return carried

        lax.fori_loop(0, dkey_ref.shape[0] // keys, lay_out, 0)


def whole_spec(array):
    return pl.BlockSpec(array.shape, lambda i, *_: (0,) * array.ndim)


def tile_spec(array):
    return pl.BlockSpec((1,) + array.shape[1:], lambda i, *_: (i,) + (0,) * (array.ndim - 1))


def piece_spec(array):
    per_tile = QUERY_TILE // LANES
    return pl.BlockSpec((per_tile, min(array.shape[1], HEAD_DIM), LANES), lambda i, *_: (i, 0, 0))


def run_kernel(body, name, scalars, grid, inputs, outputs, scratch, flops):
    return pl.pallas_call(
        body,
        grid_spec=pltpu.PrefetchScalarGridSpec(
            num_scalar_prefetch=len(scalars),
            grid=(grid,),
            in_specs=[spec for _, spec in inputs],
            out_specs=[spec for _, spec in outputs],
            scratch_shapes=scratch,
        ),
        out_shape=[shape for shape, _ in outputs],
        compiler_params=pltpu.CompilerParams(vmem_limit_bytes=52 << 20),
        cost_estimate=pl.CostEstimate(
            flops=flops, transcendentals=flops // 400, bytes_accessed=16 << 20
        ),
        name=name,
    )(*scalars, *[array for array, _ in inputs])


def attend(query_pieces, own, other, half, pos, start, rel, low, high):
    tiles, _, queries = pos.shape
    key_total = own[0].shape[0] * LANES * len(own)
    key_tile = rel.shape[0]
    kind = jax.ShapeDtypeStruct
    pieces = kind((tiles * queries // LANES, HEAD_DIM, LANES), jnp.bfloat16)
    outputs = [
        kind((tiles, HEAD_DIM, queries), jnp.float32),
        pieces,
        kind((tiles, 1, queries), jnp.float32),
        kind((key_total, HEAD_DIM), jnp.bfloat16),
        kind((key_total // key_tile, HEAD_DIM, key_tile), jnp.bfloat16),
    ]
    return run_kernel(
        functools.partial(forward_kernel, slots=len(own)),
        "attention_forward",
        (low, high, half),
        tiles,
        [(query_pieces, piece_spec(query_pieces))]
        + [(each, fixed_spec(each.shape)) for each in own + other]
        + [(pos, tile_spec(pos)), (start, tile_spec(start)), (rel, fixed_spec(rel.shape))],
        [
            (outputs[0], tile_spec(outputs[0])),
            (outputs[1], piece_spec(outputs[1])),
            (outputs[2], tile_spec(outputs[2])),
            (outputs[3], fixed_spec(outputs[3].shape)),
            (outputs[4], fixed_spec(outputs[4].shape)),
        ],
        [],
        20_000_000_000,
    )


def attend_back(
    query_pieces,
    dout_pieces,
    out_cols,
    lse,
    key_rows,
    key_cols,
    value_rows,
    pos,
    start,
    rel,
    cosine,
    sine_part,
    low,
    high,
    slots,
    sent_kind,
):
    tiles, _, queries = pos.shape
    sources = key_rows.shape[0] // (slots * LANES)
    grads = (2, slots // 2, sources, HEAD_DIM, LANES)
    outputs = [
        jax.ShapeDtypeStruct((tiles * queries // LANES, HEAD_DIM, LANES), jnp.bfloat16),
        jax.ShapeDtypeStruct(grads, jnp.float32),
        jax.ShapeDtypeStruct(grads, sent_kind),
    ]
    return run_kernel(
        backward_kernel,
        "attention_backward",
        (low, high),
        tiles,
        [
            (query_pieces, piece_spec(query_pieces)),
            (dout_pieces, piece_spec(dout_pieces)),
            (out_cols, tile_spec(out_cols)),
            (lse, tile_spec(lse)),
            (key_rows, fixed_spec(key_rows.shape)),
            (key_cols, fixed_spec(key_cols.shape)),
            (value_rows, fixed_spec(value_rows.shape)),
            (pos, tile_spec(pos)),
            (start, tile_spec(start)),
            (rel, fixed_spec(rel.shape)),
            (cosine, piece_spec(cosine)),
            (sine_part, piece_spec(sine_part)),
        ],
        [
            (outputs[0], piece_spec(outputs[0])),
            (outputs[1], fixed_spec(grads)),
            (outputs[2], fixed_spec(grads)),
        ],
        [pltpu.VMEM(key_rows.shape, jnp.float32)] * 2,
        50_000_000_000,
    )


def per_device(
    tokens,
    segment_ids,
    out_grad,
    attn_master,
    attn_first,
    attn_second,
    ffn_master,
    ffn_first,
    ffn_second,
):
    index = lax.axis_index("seq")
    count = lax.axis_size("seq")
    rows = tokens.shape[0]
    total = rows * count
    group = count // KV_HEADS
    parts = group // 2
    span = rows // parts
    half = (index // parts) % 2
    part = index % parts

    def exchange(value):
        return lax.all_to_all(value, "seq", 0, 0, tiled=True)

    def swapped(value, bit):
        return lax.ppermute(value, "seq", [(i, i ^ bit) for i in range(count)])

    attn_low = attn_master.astype(jnp.bfloat16)
    ffn_low = ffn_master.astype(jnp.bfloat16)
    notice = jnp.concatenate(
        [attn_low[:D], ffn_low[:D], segment_ids.astype(jnp.bfloat16)]
    ).reshape(1, -1, 128)
    notices = exchange(jnp.broadcast_to(notice, (count,) + notice.shape[1:]))

    inputs = tokens.astype(jnp.float32)

    def from_notices(notices):
        gains = notices[0, : 2 * D // 128].astype(jnp.float32).reshape(2, D)
        all_ids = notices[:, 2 * D // 128 :].astype(jnp.int32).reshape(-1)
        held_ids = lax.dynamic_index_in_dim(
            all_ids.reshape(count, parts, span), part, 1, keepdims=False
        )

        def item_starts(ids):
            return jnp.sum((all_ids < ids[..., None]).astype(jnp.int32), axis=-1)

        return (
            gains[0],
            gains[1],
            rms_norm(inputs, gains[0]).astype(jnp.bfloat16),
            item_starts(held_ids.reshape(-1)),
            item_starts(all_ids[:: QUERY_TILE // span * rows]) // KEY_TILE,
        )

    grid = device_grid(count)
    by_axes = (D // count) % 16 == 0

    def sum_of(left_cols, right, right_dim, order):
        left = reordered(left_cols, slot_table(index, grid, order))
        return SummedRows(left, right, right_dim, order, grid)

    def scattered(left_cols, right, right_dim):
        whole = contract(left_cols, 1, right, right_dim).astype(jnp.bfloat16)
        return (
            lax.psum_scatter(whole, "seq", scatter_dimension=0, tiled=True)
            .reshape(-1)
            .astype(jnp.float32)
        )

    attn_block = aligned_block(attn_low, index, count)
    ffn_block = aligned_block(ffn_low, index, count)
    if by_axes:
        own_tiles = unit_tiles(ffn_block, (FF, FF, D), index, count)
        attn_tiles, own_tiles, beside = gather_tiles(
            unit_tiles(attn_block, (D, KV_HEADS * HEAD_DIM, D), index, count),
            index,
            grid,
            notices,
            own_tiles,
            from_notices,
        )
        ffn_tiles = lax.all_gather(own_tiles, "seq", axis=0, tiled=True)
        wide_rows = matrix_of(ffn_tiles, FF)
        gate_weight = (wide_rows, 0)
        up_weight = (wide_rows, D)
        down_weight = (matrix_of(ffn_tiles, D), 2 * FF)
        attn_wide = matrix_of(attn_tiles, D)
        attn_narrow = matrix_of(attn_tiles, KV_HEADS * HEAD_DIM)
        query_weight = (attn_wide, 0)
        key_weight = (attn_narrow, 2 * D)
        value_weight = (attn_narrow, 3 * D)
        out_weight = (attn_wide, 2 * D)
    else:

        def gathered(unit, width):
            return lax.all_gather(unit.reshape(-1, width), "seq", axis=0, tiled=True)

        q_unit, kv_unit, o_unit = units_from_block(attn_block, index, count)
        gate_unit, up_unit, down_unit = units_from_block(ffn_block, index, count)
        query_weight = (gathered(q_unit, HEADS * HEAD_DIM), 0)
        key_value_weight = gathered(kv_unit, KV_HEADS * HEAD_DIM)
        key_weight = (key_value_weight, 0)
        value_weight = (key_value_weight, D)
        out_weight = (gathered(o_unit, D), 0)
        gate_weight = (gathered(gate_unit, FF), 0)
        up_weight = (gathered(up_unit, FF), 0)
        down_weight = (gathered(down_unit, D), 0)

    gain_one, gain_two, normed_one, held_starts, low = (
        beside if by_axes else from_notices(notices)
    )

    own_places = index * rows + jnp.arange(rows, dtype=jnp.int32)
    own_cos, own_sin = angle_tables(own_places)

    cols = span if span % 128 == 0 else rows

    def by_owner(value):
        if value.shape[0] == count:
            return value
        pieces = value.reshape(HEADS, value.shape[1], parts, span)
        return jnp.swapaxes(pieces, 1, 2).reshape(count, value.shape[1], span)

    def by_head(value):
        pieces = value.reshape(HEADS, parts, value.shape[1], span)
        return jnp.swapaxes(pieces, 1, 2).reshape(HEADS, value.shape[1], rows)

    received = exchange(
        by_owner(
            project(normed_one, query_weight, key_weight, value_weight, own_cos, own_sin, cols)
        )
    )

    merged = LANES // span

    def to_pieces(value):
        if merged == 1:
            return value
        pieces = value.reshape(count // merged, merged, value.shape[1], span)
        return jnp.swapaxes(pieces, 1, 2).reshape(count // merged, value.shape[1], LANES)

    def from_pieces(value):
        if merged == 1:
            return value
        pieces = value.reshape(count // merged, value.shape[1], merged, span)
        return jnp.swapaxes(pieces, 1, 2).reshape(count, value.shape[1], span)

    own_kind = received[:, HEAD_DIM:]
    both_kinds = [[own_kind], [swapped(own_kind, parts)]]
    bit = 1
    while bit < parts:
        both_kinds = [kind + [swapped(each, bit) for each in kind] for kind in both_kinds]
        bit = bit * 2
    own, other = [[to_pieces(each) for each in kind] for kind in both_kinds]
    query_pieces = to_pieces(received)
    sources = QUERY_TILE // span
    tiles = count // sources
    within = jnp.arange(span, dtype=jnp.int32)
    rel = (
        span * (part ^ jnp.arange(parts, dtype=jnp.int32))[:, None, None]
        + rows * jnp.arange(KEY_TILE // rows, dtype=jnp.int32)[None, :, None]
        + within[None, None, :]
    ).reshape(KEY_TILE, 1)
    rel = jnp.broadcast_to(rel, (KEY_TILE, LANES))
    held_places = (
        rows * jnp.arange(count, dtype=jnp.int32)[:, None] + span * part + within[None, :]
    )
    pos = held_places.reshape(tiles, 1, QUERY_TILE)
    start = held_starts.reshape(tiles, 1, QUERY_TILE)
    tile_span = sources * rows
    high = (jnp.arange(1, tiles + 1, dtype=jnp.int32) * tile_span + KEY_TILE - 1) // KEY_TILE

    chunks = []
    chunk = min(CHUNK, total)
    per_tile = QUERY_TILE // LANES
    for first in range(0, total, chunk):
        of_tiles = slice(first // tile_span, (first + chunk) // tile_span)
        of_queries = slice(of_tiles.start * per_tile, of_tiles.stop * per_tile)
        first_key = max(0, first - SEG_MOST) // KEY_TILE
        last_key = (first + chunk) // KEY_TILE
        per_piece = merged * rows
        of_keys = slice(
            first_key * KEY_TILE // per_piece, last_key * KEY_TILE // per_piece
        )
        chunks.append((of_tiles, of_queries, first_key, of_keys))

    attended = []
    for of_tiles, of_queries, first_key, of_keys in chunks:
        shift = first_key * KEY_TILE
        attended.append(
            attend(
                query_pieces[of_queries],
                [each[of_keys] for each in own],
                [each[of_keys] for each in other],
                half.reshape(1),
                pos[of_tiles] - shift,
                start[of_tiles] - shift,
                rel,
                low[of_tiles] - first_key,
                high[of_tiles] - first_key,
            )
        )
    mixed_pieces = exchange(
        from_pieces(jnp.concatenate([piece[1] for piece in attended]))
    )
    held = []
    for out_cols, _, lse, key_rows, value_cols in attended:
        key_cols = jnp.swapaxes(key_rows.reshape(-1, KEY_TILE, HEAD_DIM), 1, 2)
        value_rows = jnp.swapaxes(value_cols, 1, 2).reshape(-1, HEAD_DIM)
        held.append((out_cols, lse, key_rows, key_cols, value_rows))
    held_cos, held_sin = [to_pieces(table) for table in angle_tables(held_places)]
    mixed_pieces, (held, held_cos, held_sin) = together(
        mixed_pieces, (held, held_cos, held_sin)
    )
    if cols == rows:
        mixed_pieces = by_head(mixed_pieces)

    (
        result,
        middle_grad,
        middle_low,
        dout_pieces,
        grad_two,
        gate_grad,
        up_grad,
        hidden_cols,
        normed_two_cols,
        mixed_low,
    ) = feed_forward(
        tokens,
        mixed_pieces,
        gain_two,
        out_grad,
        out_weight,
        gate_weight,
        up_weight,
        down_weight,
    )
    dout_received = exchange(by_owner(dout_pieces))
    if by_axes:
        gate_sum = sum_of(normed_two_cols, gate_grad, 0, GATE_ORDER)
        up_sum = sum_of(normed_two_cols, up_grad, 0, UP_ORDER)
        down_sum = sum_of(hidden_cols, out_grad, 0, DOWN_ORDER)
        first_sums = [gate_sum, up_sum]
        make_and_send(first_sums + [down_sum])
        dout_received = made_before(first_sums, dout_received)
        for each in first_sums:
            each.send()
    else:
        ffn_units = [
            scattered(normed_two_cols, gate_grad, 0),
            scattered(normed_two_cols, up_grad, 0),
            scattered(hidden_cols, out_grad, 0),
        ]
        out_unit = scattered(mixed_low, middle_low, 0)
    dout_pieces = to_pieces(dout_received)

    one_chunk = len(chunks) == 1
    dquery_pieces = []
    summed = [jnp.zeros((2, max(parts // 2, 1), count // merged, HEAD_DIM, LANES), jnp.float32)] * 2
    for (of_tiles, of_queries, first_key, of_keys), kept_values in zip(chunks, held):
        shift = first_key * KEY_TILE
        dquery_piece, *found = attend_back(
            query_pieces[of_queries],
            dout_pieces[of_queries],
            *kept_values,
            pos[of_tiles] - shift,
            start[of_tiles] - shift,
            rel,
            held_cos[of_queries],
            held_sin[of_queries],
            low[of_tiles] - first_key,
            high[of_tiles] - first_key,
            parts,
            jnp.bfloat16 if one_chunk else jnp.float32,
        )
        dquery_pieces.append(dquery_piece)
        if one_chunk:
            summed = found
        else:
            summed = [
                whole.at[:, :, of_keys].add(piece) for whole, piece in zip(summed, found)
            ]
    dquery_held = from_pieces(jnp.concatenate(dquery_pieces))
    grads, sent = summed
    if by_axes:
        mixed_late, grads = together(mixed_low, grads)
        out_sum = sum_of(mixed_late, middle_low, 0, OUT_ORDER)
    grads = grads + swapped(sent.astype(jnp.bfloat16), parts // 2)
    bit = parts // 4
    while bit >= 1:
        grads = grads[:, :bit] + swapped(grads[:, bit:].astype(jnp.bfloat16), bit)
        bit = bit // 2
    if by_axes:
        grads = taken_after(first_sums, grads)
    dkey_held, dvalue_held = (grads[0, 0], grads[1, 0])
    sent_kind = jnp.where(half == 0, dvalue_held, dkey_held).astype(jnp.bfloat16)
    kept_kind = jnp.where(half == 0, dkey_held, dvalue_held) + swapped(sent_kind, parts)
    kept_low = from_pieces(
        jnp.where(half == 0, rotate(kept_kind, held_cos, -held_sin), kept_kind).astype(
            jnp.bfloat16
        )
    )
    sent_back = jnp.concatenate([dquery_held, kept_low], axis=1)
    if by_axes:
        early_sums = first_sums + [down_sum]
        sent_back = made_before(early_sums, sent_back)
        for each in early_sums:
            each.send()
    returned = exchange(sent_back)
    if by_axes:
        make_and_send([out_sum])
        returned = taken_after([down_sum], made_before(first_sums, returned))
        for each in first_sums:
            each.send()
    dquery_low = by_head(returned[:, :HEAD_DIM]).reshape(HEADS * HEAD_DIM, rows)
    pair_low = by_head(returned[:, HEAD_DIM:]).reshape(KV_HEADS, 2, HEAD_DIM, rows)
    dkey_low = pair_low[:, 0].reshape(KV_HEADS * HEAD_DIM, rows)
    dvalue_low = pair_low[:, 1].reshape(KV_HEADS * HEAD_DIM, rows)

    normed_one_cols = normed_one.T
    nothing = jnp.zeros_like(normed_one_cols)
    key_value_cols = jnp.concatenate(
        [
            jnp.concatenate([normed_one_cols, nothing], axis=1),
            jnp.concatenate([nothing, normed_one_cols], axis=1),
        ]
    )
    key_value_right = jnp.concatenate([dkey_low, dvalue_low], axis=1)
    if by_axes:
        query_sum = sum_of(normed_one_cols, dquery_low, 1, GATE_ORDER)
        key_value_sum = sum_of(key_value_cols, key_value_right, 1, UP_ORDER)
        last_sums = [query_sum, key_value_sum]
        make_and_send(last_sums)
        for each in last_sums:
            each.make()
        for other_sum in early_sums + [out_sum]:
            taken_after([other_sum], [each.made for each in last_sums])
        for each in last_sums:
            each.send()
        dquery_late = taken_after(last_sums, dquery_low)
        make_and_send([gate_sum, up_sum, down_sum, out_sum])
        normed_one_grad = (
            contract(dquery_late, 0, query_weight[0][:D], 1)
            + contract(dkey_low, 0, key_weight[0][key_weight[1] : key_weight[1] + D], 1)
            + contract(dvalue_low, 0, value_weight[0][value_weight[1] : value_weight[1] + D], 1)
        )
        _, first_pull = jax.vjp(rms_norm, inputs, gain_one)
        input_norm_grad, grad_one = first_pull(normed_one_grad)
        input_grad = middle_grad + input_norm_grad

        gain_sum = SummedWhole(jnp.concatenate([grad_one, grad_two[0]]).reshape(-1, 128), grid)
        attn_sums = last_sums + [out_sum]
        make_and_send([gain_sum])
        one_round(attn_sums + early_sums + [gain_sum])
        one_round(attn_sums + [down_sum, gain_sum])
        one_round(attn_sums + [down_sum, gain_sum])
        ffn_units = [gate_sum.result(), up_sum.result(), down_sum.result()]
        one_round(attn_sums + [gain_sum])
        gain_grads = gain_sum.result().reshape(2, D)
        query_unit, key_value_unit, out_unit = [each.result() for each in attn_sums]
    else:
        query_unit = scattered(normed_one_cols, dquery_low, 1)
        key_value_unit = scattered(key_value_cols, key_value_right, 1)
        normed_one_grad = (
            contract(dquery_low, 0, query_weight[0][:D], 1)
            + contract(dkey_low, 0, key_weight[0][key_weight[1] : key_weight[1] + D], 1)
            + contract(dvalue_low, 0, value_weight[0][value_weight[1] : value_weight[1] + D], 1)
        )
        _, first_pull = jax.vjp(rms_norm, inputs, gain_one)
        input_norm_grad, grad_one = first_pull(normed_one_grad)
        input_grad = middle_grad + input_norm_grad

        gain_grads = lax.psum(jnp.stack([grad_one, grad_two[0]]), "seq")
    ffn_shard = shard_from_units(ffn_units, gain_grads[1], index, count)
    attn_shard = shard_from_units(
        [query_unit, key_value_unit, out_unit], gain_grads[0], index, count
    )
    attn_new, attn_one, attn_two = adam_update(
        attn_master, attn_first, attn_second, attn_shard
    )
    ffn_new, ffn_one, ffn_two = adam_update(
        ffn_master, ffn_first, ffn_second, ffn_shard
    )
    return (result, input_grad, attn_new, attn_one, attn_two, ffn_new, ffn_one, ffn_two)


def solution(mesh):
    rows_cut = P("seq", None)
    flat_cut = P("seq")
    in_specs = (rows_cut, flat_cut, rows_cut) + (flat_cut,) * 6
    out_specs = (rows_cut, rows_cut) + (flat_cut,) * 6
    return jax.shard_map(
        per_device, mesh=mesh, in_specs=in_specs, out_specs=out_specs, check_vma=False
    )
```

```python
import functools
import math

import jax
import jax.numpy as jnp
from jax import lax
from jax.experimental import pallas as pl
from jax.experimental.pallas import tpu as pltpu
from jax.sharding import PartitionSpec as P

D = 1536
HEADS = 16
KV_HEADS = 8
HEAD_DIM = 96
FF = 4096
SEG_MOST = 4096
STEP = 7


ROPE_BASE = 100000.0
NORM_EPS = 1e-05
BETA_ONE = 0.5
BETA_TWO = 0.5
LEARN_RATE = 0.04
DECAY = 0.1
ADAM_EPS = 1e-08
NEG_LARGE = -1e30
HALF_DIM = HEAD_DIM // 2
QUERY_TILE = 512
KEY_TILE = 1024
CHUNK = 8192
LANES = 128
FF_TILE = 512
SCORE_BASE_TWO = math.log2(math.e) / math.sqrt(HEAD_DIM)
SCORE_SCALE = 1.0 / math.sqrt(HEAD_DIM)


def rms_norm(values, norm_gain):
    factor = lax.rsqrt(jnp.mean(values * values, axis=-1, keepdims=True) + NORM_EPS)
    return values * factor * norm_gain


def angle_tables(positions):
    frequency = jnp.exp(
        jnp.arange(HALF_DIM).astype(jnp.float32) * (-2.0 * math.log(ROPE_BASE) / HEAD_DIM)
    )
    angles = positions.astype(jnp.float32)[..., None, :] * frequency[:, None]
    return (jnp.cos(angles), jnp.sin(angles))


def rotate(values, cosine, sine_part):
    lower_part = values[..., :HALF_DIM, :]
    upper_part = values[..., HALF_DIM:, :]
    return jnp.concatenate(
        [
            lower_part * cosine - upper_part * sine_part,
            upper_part * cosine + lower_part * sine_part,
        ],
        axis=-2,
    )


def contract(left, left_dim, right, right_dim):
    return lax.dot_general(
        left,
        right,
        (((left_dim,), (right_dim,)), ((), ())),
        preferred_element_type=jnp.float32,
    )


def adam_update(master, moment_one, moment_two, gradient):
    first_new = BETA_ONE * moment_one + (1.0 - BETA_ONE) * gradient
    second_new = BETA_TWO * moment_two + (1.0 - BETA_TWO) * gradient * gradient
    first_hat = first_new / (1.0 - BETA_ONE**STEP)
    second_hat = second_new / (1.0 - BETA_TWO**STEP)
    master_new = master - LEARN_RATE * (
        first_hat / (jnp.sqrt(second_hat) + ADAM_EPS) + DECAY * master
    )
    return (master_new, first_new, second_new)


def aligned_block(flat_low, index, count):
    edge = D // count
    block = flat_low.shape[0] - edge
    following = lax.ppermute(flat_low[:D], "seq", [(i + 1, i) for i in range(count - 1)])
    extended = jnp.concatenate([flat_low, following])
    return lax.dynamic_slice(extended, (D - edge * index,), (block,))


def tiles_of(unit, width):
    pieces = unit.reshape(-1, 8, width // 128, 128)
    return jnp.swapaxes(pieces, 1, 2).reshape(-1, 8, 128)


def matrix_of(tiles, width):
    pieces = tiles.reshape(-1, width // 128, 8, 128)
    return jnp.swapaxes(pieces, 1, 2).reshape(-1, width)


def unit_tiles(block, widths, index, count):
    units = block.reshape(3, -1)
    made = []
    for j in range(3):
        kind = (3 * index + j) // count
        made.append(
            lax.select_n(kind, *[tiles_of(units[j], width) for width in widths])
        )
    return jnp.concatenate(made)


def units_from_block(block, index, count):
    aligned = block.reshape(3, -1)
    dealt = jnp.stack(
        [
            lax.ppermute(aligned[j], "seq", [(i, (3 * i + j) % count) for i in range(count)])
            for j in range(3)
        ]
    )
    return [
        lax.dynamic_index_in_dim(dealt, slot_of_kind(index, kind, count), 0, keepdims=False)
        for kind in range(3)
    ]


def slot_of_kind(index, kind, count):
    return (index + count * kind) % 3


def shard_from_units(units, gain_grad, index, count):
    edge = D // count
    units = [unit.astype(jnp.bfloat16) for unit in units]
    unit = units[0].shape[0]
    returned = []
    for j in range(3):
        inverse = 1 if count % 3 == 1 else 2
        kind = ((j - index) * inverse) % 3
        piece = jnp.where(kind == 0, units[0], jnp.where(kind == 1, units[1], units[2]))
        returned.append(
            lax.ppermute(piece, "seq", [((3 * i + j) % count, i) for i in range(count)])
        )
    before = lax.ppermute(returned[2][-D:], "seq", [(i, i + 1) for i in range(count - 1)])
    before = jnp.where(index == 0, gain_grad, before.astype(jnp.float32))
    extended = jnp.concatenate([before] + [piece.astype(jnp.float32) for piece in returned])
    return lax.dynamic_slice(extended, (edge * index,), (3 * unit + edge,))


AXES = ("z", "y", "x")
GATHER_ORDERS = (("core", "x", "y", "z"), ("core", "y", "x", "z"))
GATE_ORDER = ("core", "x", "z", "y")
UP_ORDER = ("core", "y", "z", "x")
DOWN_ORDER = ("core", "y", "x", "z")
OUT_ORDER = ("core", "y", "x", "z")


def device_grid(count):
    chips = count // 2
    sides = {16: (4, 2, 2), 64: (4, 4, 4)}.get(chips, (chips, 1, 1))
    return dict(zip(AXES + ("core",), sides + (2,)))


def coordinates(index, grid):
    found = {}
    for axis in reversed(list(grid)):
        found[axis] = index % grid[axis]
        index = index // grid[axis]
    return found


def place(found, grid):
    index = 0
    for axis in grid:
        index = index * grid[axis] + found[axis]
    return index


def shifted(value, axis, steps, grid):
    pairs = []
    for source in range(math.prod(grid.values())):
        target = coordinates(source, grid)
        target[axis] = (target[axis] + steps) % grid[axis]
        pairs.append((source, place(target, grid)))
    return lax.ppermute(value, "seq", pairs)


def slot_table(index, grid, axes):
    here = coordinates(index, grid)
    entries = []
    for number in range(math.prod(grid.values())):
        slots = coordinates(number, {axis: grid[axis] for axis in axes})
        there = {axis: (here[axis] - slots[axis]) % grid[axis] for axis in grid}
        entries.append(place(there, grid))
    return jnp.stack(entries).astype(jnp.int32)


def place_kernel(table_ref, *refs, lengths):
    pieces = len(lengths)
    piece_refs, out_ref = (refs[:pieces], refs[pieces])
    held, in_sems, out_sems = refs[pieces + 1 :]
    size = held.shape[1]
    loads = []
    for piece_ref, length in zip(piece_refs, lengths):
        for block in range(length):
            entry = len(loads)
            load = pltpu.make_async_copy(
                piece_ref.at[pl.ds(block * size, size)], held.at[entry], in_sems.at[entry]
            )
            load.start()
            loads.append(load)
    stores = []
    for entry, load in enumerate(loads):
        load.wait()
        target = pl.ds(pl.multiple_of(table_ref[entry] * size, size), size)
        store = pltpu.make_async_copy(held.at[entry], out_ref.at[target], out_sems.at[entry])
        store.start()
        stores.append(store)
    for store in stores:
        store.wait()


def placed(pieces, table):
    count = table.shape[0]
    size = sum(piece.shape[0] for piece in pieces) // count
    shape = pieces[0].shape[1:]
    anywhere = pl.BlockSpec(memory_space=pl.ANY)
    return pl.pallas_call(
        functools.partial(
            place_kernel, lengths=tuple(piece.shape[0] // size for piece in pieces)
        ),
        grid_spec=pltpu.PrefetchScalarGridSpec(
            num_scalar_prefetch=1,
            grid=(1,),
            in_specs=[anywhere] * len(pieces),
            out_specs=anywhere,
            scratch_shapes=[
                pltpu.VMEM((count, size) + shape, pieces[0].dtype),
                pltpu.SemaphoreType.DMA((count,)),
                pltpu.SemaphoreType.DMA((count,)),
            ],
        ),
        out_shape=jax.ShapeDtypeStruct((count * size,) + shape, pieces[0].dtype),
        compiler_params=pltpu.CompilerParams(vmem_limit_bytes=48 << 20),
        cost_estimate=pl.CostEstimate(
            flops=0, transcendentals=0, bytes_accessed=4 * count * size * math.prod(shape)
        ),
        name="place_blocks",
    )(table, *pieces)


def gather_tiles(block, index, grid, notices, later, beside_of):
    arrived = [block] + [shifted(block, "z", k, grid) for k in range(1, grid["z"])]
    arrived, notices = together(arrived, notices)
    beside = beside_of(notices)
    half = block.shape[0] // 2
    held = [
        jnp.concatenate([each[color * half : (color + 1) * half] for each in arrived])
        for color in range(2)
    ]
    for turn in (2, 1):
        arrivals = []
        for color, order in enumerate(GATHER_ORDERS):
            axis = order[turn]
            arrivals.append(
                [held[color]]
                + [shifted(held[color], axis, k, grid) for k in range(1, grid[axis])]
            )
        if turn == 1:
            arrivals, beside = together(arrivals, beside)
        else:
            arrivals, later = together(arrivals, later)
            held = [jnp.concatenate(each) for each in arrivals]
    pieces = []
    tables = []
    for color, order in enumerate(GATHER_ORDERS):
        pieces = pieces + arrivals[color]
        pieces = pieces + [shifted(piece, "core", 1, grid) for piece in arrivals[color]]
        tables.append(2 * slot_table(index, grid, order) + color)
    return placed(pieces, jnp.concatenate(tables)), later, beside


def reorder_kernel(table_ref, in_ref, out_ref, *, rows):
    for block in range(in_ref.shape[0] // rows):
        source = pl.ds(pl.multiple_of(table_ref[block] * rows, rows), rows)
        out_ref[block * rows : (block + 1) * rows, :] = in_ref[source, :]


def reordered(value, table):
    rows = value.shape[0] // table.shape[0]
    return pl.pallas_call(
        functools.partial(reorder_kernel, rows=rows),
        grid_spec=pltpu.PrefetchScalarGridSpec(
            num_scalar_prefetch=1,
            grid=(1,),
            in_specs=[whole_spec(value)],
            out_specs=whole_spec(value),
        ),
        out_shape=jax.ShapeDtypeStruct(value.shape, value.dtype),
        cost_estimate=pl.CostEstimate(
            flops=0, transcendentals=0, bytes_accessed=4 * value.size
        ),
        name="reorder_blocks",
    )(table, value)


class SummedRows:

    def __init__(self, left, right, right_dim, order, grid):
        self.left = left
        self.right = right
        self.right_dim = right_dim
        self.grid = grid
        self.rows = left.shape[0] // math.prod(grid.values())
        self.window = left.shape[0]
        self.turns = [(axis, slot) for axis in order for slot in range(grid[axis] - 1, 0, -1)]
        self.received = []
        self.passing = []

    def partial(self, span):
        total = contract(self.left[span], 1, self.right, self.right_dim)
        for part in self.received:
            total = total + part[span]
        return total

    def make(self):
        axis, slot = self.turns[0]
        if slot == self.grid[axis] - 1:
            self.window = self.window // self.grid[axis]
        total = self.partial(slice(slot * self.window, (slot + 1) * self.window))
        for part in self.passing:
            total = total + part
        self.made = total.astype(jnp.bfloat16)

    def send(self):
        axis, slot = self.turns.pop(0)
        arrived = [shifted(self.made, axis, -1, self.grid)]
        if slot > 1:
            self.passing = arrived
        else:
            self.passing = []
            self.received = self.received + arrived

    def result(self):
        return self.partial(slice(0, self.rows)).reshape(-1)


class SummedWhole:

    def __init__(self, value, grid):
        self.value = value
        self.grid = grid
        self.turns = []
        for axis in ("core", "x", "y", "z"):
            step = grid[axis] // 2
            while step >= 1:
                self.turns.append((axis, step))
                step = step // 2
        self.received = []
        self.passing = []

    def make(self):
        for part in self.received:
            self.value = self.value + part
        self.made = self.value

    def send(self):
        axis, step = self.turns.pop(0)
        self.received = [shifted(self.made, axis, step, self.grid)]

    def result(self):
        return self.value + self.received[0]


def together(values, others):
    return lax.optimization_barrier((values, others))


def made_before(sums, value):
    for each in sums:
        each.make()
    value, made = together(value, [each.made for each in sums])
    for each, now in zip(sums, made):
        each.made = now
    return value


def taken_after(sums, value):
    value, arrived = together(value, [(each.received, each.passing) for each in sums])
    for each, now in zip(sums, arrived):
        each.received, each.passing = now
    return value


def one_round(sums):
    taken_after(sums, ())
    make_and_send(sums)


def make_and_send(sums):
    for each in sums:
        each.make()
        each.send()


def feed_forward_kernel(
    tokens_ref,
    mixed_piece_ref,
    gain_ref,
    out_grad_ref,
    out_weight_ref,
    gate_weight_ref,
    up_weight_ref,
    down_weight_ref,
    result_ref,
    middle_grad_ref,
    middle_low_ref,
    dout_piece_ref,
    gain_grad_ref,
    gate_grad_ref,
    up_grad_ref,
    hidden_col_ref,
    normed_col_ref,
    mixed_col_ref,
    middle_ref,
    normed_ref,
    total_ref,
    normed_grad_ref,
):
    step = pl.program_id(0)
    pieces, _, cols = mixed_piece_ref.shape
    per_head = pieces // HEADS

    def factor_of(middle):
        return lax.rsqrt(jnp.mean(middle * middle, axis=-1, keepdims=True) + NORM_EPS)

    def place_of(piece):
        head, part = divmod(piece, per_head)
        return (slice(head * HEAD_DIM, (head + 1) * HEAD_DIM), slice(part * cols, (part + 1) * cols))

    @pl.when(step == 0)
    def _():
        for piece in range(pieces):
            mixed_col_ref[place_of(piece)] = mixed_piece_ref[piece]
        middle = tokens_ref[...].astype(jnp.float32) + contract(
            mixed_col_ref[...].T, 1, out_weight_ref[...], 0
        )
        middle_ref[...] = middle
        normed = (middle * factor_of(middle) * gain_ref[...]).astype(jnp.bfloat16)
        normed_ref[...] = normed
        normed_col_ref[...] = normed.T
        total_ref[...] = jnp.zeros_like(total_ref)
        normed_grad_ref[...] = jnp.zeros_like(normed_grad_ref)

    normed = normed_ref[...]
    gate_weight = gate_weight_ref[...]
    up_weight = up_weight_ref[...]
    down_weight = down_weight_ref[...]
    gate = contract(normed, 1, gate_weight, 0)
    up = contract(normed, 1, up_weight, 0)
    sigma = jax.nn.sigmoid(gate)
    silu = gate * sigma
    hidden = (silu * up).astype(jnp.bfloat16)
    hidden_col_ref[...] = hidden.T
    total_ref[...] += contract(hidden, 1, down_weight, 0)
    hidden_grad = contract(out_grad_ref[...], 1, down_weight, 1)
    gate_grad = (hidden_grad * up * sigma * (1.0 + gate * (1.0 - sigma))).astype(jnp.bfloat16)
    up_grad = (hidden_grad * silu).astype(jnp.bfloat16)
    gate_grad_ref[...] = gate_grad
    up_grad_ref[...] = up_grad
    normed_grad_ref[...] += contract(gate_grad, 1, gate_weight, 1) + contract(
        up_grad, 1, up_weight, 1
    )

    @pl.when(step == pl.num_programs(0) - 1)
    def _():
        middle = middle_ref[...]
        factor = factor_of(middle)
        normed_grad = normed_grad_ref[...]
        result_ref[...] = (middle + total_ref[...]).astype(jnp.bfloat16)
        scaled = normed_grad * gain_ref[...]
        slope = jnp.mean(scaled * middle, axis=-1, keepdims=True)
        middle_grad = out_grad_ref[...].astype(jnp.float32) + factor * (
            scaled - middle * (factor * factor * slope)
        )
        middle_grad_ref[...] = middle_grad
        middle_low = middle_grad.astype(jnp.bfloat16)
        middle_low_ref[...] = middle_low
        dout_cols = contract(out_weight_ref[...], 1, middle_low, 1).astype(jnp.bfloat16)
        for piece in range(pieces):
            dout_piece_ref[piece] = dout_cols[place_of(piece)]
        gain_grad_ref[...] = jnp.sum(normed_grad * middle * factor, axis=0, keepdims=True)


def fixed_spec(shape):
    return pl.BlockSpec(shape, lambda i, *_: (0,) * len(shape), pipeline_mode=pl.Buffered(1))


def feed_forward(tokens, mixed_pieces, gain, out_grad, out, gate, up, down):
    rows = tokens.shape[0]
    wide = pl.BlockSpec((rows, FF_TILE), lambda i: (0, i))
    out_first, gate_first, up_first = (out[1] // D, gate[1] // D, up[1] // D)
    down_first = down[1] // FF_TILE
    square = (rows, D)
    flipped = (D, rows)
    outs = [
        (fixed_spec(square), square, jnp.bfloat16),
        (fixed_spec(square), square, jnp.float32),
        (fixed_spec(square), square, jnp.bfloat16),
        (fixed_spec(mixed_pieces.shape), mixed_pieces.shape, jnp.bfloat16),
        (fixed_spec((1, D)), (1, D), jnp.float32),
        (wide, (rows, FF), jnp.bfloat16),
        (wide, (rows, FF), jnp.bfloat16),
        (pl.BlockSpec((FF_TILE, rows), lambda i: (i, 0)), (FF, rows), jnp.bfloat16),
        (fixed_spec(flipped), flipped, jnp.bfloat16),
        (fixed_spec(flipped), flipped, jnp.bfloat16),
    ]
    return pl.pallas_call(
        feed_forward_kernel,
        grid=(FF // FF_TILE,),
        in_specs=[
            fixed_spec(square),
            fixed_spec(mixed_pieces.shape),
            fixed_spec((1, D)),
            fixed_spec(square),
            pl.BlockSpec((D, D), lambda i: (out_first, 0), pipeline_mode=pl.Buffered(1)),
            pl.BlockSpec((D, FF_TILE), lambda i: (gate_first, i)),
            pl.BlockSpec((D, FF_TILE), lambda i: (up_first, i)),
            pl.BlockSpec((FF_TILE, D), lambda i: (down_first + i, 0)),
        ],
        out_specs=[spec for spec, _, _ in outs],
        out_shape=[jax.ShapeDtypeStruct(shape, kind) for _, shape, kind in outs],
        scratch_shapes=[
            pltpu.VMEM(square, jnp.float32),
            pltpu.VMEM(square, jnp.bfloat16),
            pltpu.VMEM(square, jnp.float32),
            pltpu.VMEM(square, jnp.float32),
        ],
        compiler_params=pltpu.CompilerParams(vmem_limit_bytes=48 << 20),
        cost_estimate=pl.CostEstimate(
            flops=12 * rows * D * FF, transcendentals=rows * FF, bytes_accessed=6 * D * FF
        ),
        name="feed_forward",
    )(tokens, mixed_pieces, gain.reshape(1, D), out_grad, out[0], gate[0], up[0], down[0])


def project_kernel(
    normed_ref, query_weight_ref, key_weight_ref, value_weight_ref, cos_ref, sin_ref, piece_ref
):
    normed = normed_ref[...]
    cosine = cos_ref[...]
    sine_part = sin_ref[...]
    query_cols = contract(normed, 1, query_weight_ref[...], 0).T
    key_cols = contract(normed, 1, key_weight_ref[...], 0).T
    value_cols = contract(normed, 1, value_weight_ref[...], 0).T
    key_heads = key_cols.shape[0] // HEAD_DIM
    pieces, _, cols = piece_ref.shape
    parts = pieces // (2 * key_heads)

    def head(columns, number):
        return columns[number * HEAD_DIM : (number + 1) * HEAD_DIM]

    for key_head in range(key_heads):
        for half in range(2):
            owner = 2 * key_head + half
            query = rotate(head(query_cols, owner), cosine, sine_part)
            if half == 0:
                other = rotate(head(key_cols, key_head), cosine, sine_part)
            else:
                other = head(value_cols, key_head)
            both = jnp.concatenate([query, other], axis=0).astype(jnp.bfloat16)
            for part in range(parts):
                piece_ref[owner * parts + part] = both[:, part * cols : (part + 1) * cols]


def project(normed, query, key, value, cosine, sine_part, cols):
    rows = normed.shape[0]
    steps = 2
    pieces = HEADS * rows // cols
    query_first, key_first, value_first = (query[1] // D, key[1] // D, value[1] // D)
    query_cols = HEADS * HEAD_DIM // steps
    key_cols = KV_HEADS * HEAD_DIM // steps
    return pl.pallas_call(
        project_kernel,
        grid=(steps,),
        in_specs=[
            fixed_spec(normed.shape),
            pl.BlockSpec((D, query_cols), lambda i: (query_first, i)),
            pl.BlockSpec((D, key_cols), lambda i: (key_first, i)),
            pl.BlockSpec((D, key_cols), lambda i: (value_first, i)),
            fixed_spec(cosine.shape),
            fixed_spec(sine_part.shape),
        ],
        out_specs=pl.BlockSpec((pieces // steps, 2 * HEAD_DIM, cols), lambda i: (i, 0, 0)),
        out_shape=jax.ShapeDtypeStruct((pieces, 2 * HEAD_DIM, cols), jnp.bfloat16),
        compiler_params=pltpu.CompilerParams(vmem_limit_bytes=40 << 20),
        cost_estimate=pl.CostEstimate(
            flops=4 * rows * D * 2 * D, transcendentals=0, bytes_accessed=4 * D * 2 * D
        ),
        name="project",
    )(normed, query[0], key[0], value[0], cosine, sine_part)


def live_pairs(rel_ref, pos, start, base, queries):
    rel = rel_ref[...]
    rel = jnp.concatenate([rel] * (queries // rel.shape[1]), axis=1)
    return (rel >= start - base) & (rel <= pos - base)


def side_by_side(ref):
    return jnp.concatenate([ref[piece] for piece in range(ref.shape[0])], axis=1)


def stacked_rows(ref):
    return jnp.concatenate([ref[piece].T for piece in range(ref.shape[0])], axis=0)


def forward_kernel(low_ref, high_ref, half_ref, query_ref, *refs, slots):
    own_refs, other_refs = (refs[:slots], refs[slots : 2 * slots])
    pos_ref, start_ref, rel_ref, out_ref, piece_ref, lse_ref, key_ref, value_ref = refs[2 * slots :]
    tile = pl.program_id(0)
    keys = rel_ref.shape[0]
    per_slot = keys // (slots * LANES)

    def lay_out(key_refs, value_refs):
        def body(step, carried):
            for slot in range(slots):
                for piece in range(per_slot):
                    place = (slot * per_slot + piece) * LANES
                    source = step * per_slot + piece
                    rows = pl.ds(pl.multiple_of(step * keys + place, LANES), LANES)
                    key_ref[rows, :] = key_refs[slot][source].T
                    value_ref[step, :, place : place + LANES] = value_refs[slot][source]
            return carried

        lax.fori_loop(0, value_ref.shape[0], body, 0)

    @pl.when((tile == 0) & (half_ref[0] == 0))
    def _():
        lay_out(own_refs, other_refs)

    @pl.when((tile == 0) & (half_ref[0] != 0))
    def _():
        lay_out(other_refs, own_refs)

    query_cols = side_by_side(query_ref)
    queries = query_cols.shape[1]
    pos = pos_ref[0]
    start = start_ref[0]

    def body(step, carried):
        run_max, run_total, mixed = carried
        rows = pl.ds(pl.multiple_of(step * keys, keys), keys)
        scores = contract(key_ref[rows, :], 1, query_cols, 0)
        live = live_pairs(rel_ref, pos, start, step * keys, queries)
        scores = jnp.where(live, scores, NEG_LARGE)
        new_max = jnp.maximum(run_max, jnp.max(scores, axis=0, keepdims=True))
        weights = jnp.exp2((scores - new_max) * SCORE_BASE_TWO)
        keep = jnp.exp2((run_max - new_max) * SCORE_BASE_TWO)
        run_total = run_total * keep + jnp.sum(weights, axis=0, keepdims=True)
        mixed = mixed * keep + contract(value_ref[step], 1, weights.astype(jnp.bfloat16), 0)
        return (new_max, run_total, mixed)

    start_state = (
        jnp.full((1, queries), NEG_LARGE, jnp.float32),
        jnp.zeros((1, queries), jnp.float32),
        jnp.zeros((HEAD_DIM, queries), jnp.float32),
    )
    run_max, run_total, mixed = lax.fori_loop(low_ref[tile], high_ref[tile], body, start_state)
    mixed = mixed / run_total
    out_ref[0] = mixed
    for piece in range(piece_ref.shape[0]):
        piece_ref[piece] = mixed[:, piece * LANES : (piece + 1) * LANES].astype(jnp.bfloat16)
    lse_ref[0] = run_max * SCORE_BASE_TWO + jnp.log2(run_total)


def backward_kernel(
    low_ref,
    high_ref,
    query_ref,
    dout_ref,
    out_ref,
    lse_ref,
    key_ref,
    key_col_ref,
    value_ref,
    pos_ref,
    start_ref,
    rel_ref,
    cos_ref,
    sin_ref,
    dquery_ref,
    kept_ref,
    sent_ref,
    dkey_ref,
    dvalue_ref,
):
    tile = pl.program_id(0)

    @pl.when(tile == 0)
    def _():
        dkey_ref[...] = jnp.zeros_like(dkey_ref)
        dvalue_ref[...] = jnp.zeros_like(dvalue_ref)

    query_cols = side_by_side(query_ref)
    query_rows = stacked_rows(query_ref)
    dout_cols = side_by_side(dout_ref)
    dout_rows = stacked_rows(dout_ref)
    queries = query_cols.shape[1]
    keys = rel_ref.shape[0]
    pos = pos_ref[0]
    start = start_ref[0]
    lse = lse_ref[0]
    delta = jnp.sum(dout_cols.astype(jnp.float32) * out_ref[0], axis=0, keepdims=True)

    def body(step, dquery):
        rows = pl.ds(pl.multiple_of(step * keys, keys), keys)
        scores = contract(key_ref[rows, :], 1, query_cols, 0)
        live = live_pairs(rel_ref, pos, start, step * keys, queries)
        weights = jnp.where(live, jnp.exp2(scores * SCORE_BASE_TWO - lse), 0.0)
        weight_grad = contract(value_ref[rows, :], 1, dout_cols, 0)
        dscore = (weights * (weight_grad - delta)).astype(jnp.bfloat16)
        dvalue_ref[rows, :] += contract(weights.astype(jnp.bfloat16), 1, dout_rows, 0)
        dkey_ref[rows, :] += contract(dscore, 1, query_rows, 0)
        return dquery + contract(key_col_ref[step], 1, dscore, 0)

    dquery = lax.fori_loop(
        low_ref[tile], high_ref[tile], body, jnp.zeros((HEAD_DIM, queries), jnp.float32)
    )
    dquery = dquery * SCORE_SCALE
    for piece in range(dquery_ref.shape[0]):
        dquery_ref[piece] = rotate(
            dquery[:, piece * LANES : (piece + 1) * LANES], cos_ref[piece], -sin_ref[piece]
        ).astype(jnp.bfloat16)

    @pl.when(tile == pl.num_programs(0) - 1)
    def _():
        kept_slots = kept_ref.shape[1]
        per_slot = keys // (2 * kept_slots * LANES)

        def lay_out(step, carried):
            for slot in range(2 * kept_slots):
                for piece in range(per_slot):
                    place = (slot * per_slot + piece) * LANES
                    source = step * per_slot + piece
                    rows = pl.ds(pl.multiple_of(step * keys + place, LANES), LANES)
                    found = (dkey_ref[rows, :].T * SCORE_SCALE, dvalue_ref[rows, :].T)
                    for kind in range(2):
                        if slot < kept_slots:
                            kept_ref[kind, slot, source] = found[kind]
                        else:
                            sent_ref[kind, slot - kept_slots, source] = found[kind].astype(
                                sent_ref.dtype
                            )
            return carried

        lax.fori_loop(0, dkey_ref.shape[0] // keys, lay_out, 0)


def whole_spec(array):
    return pl.BlockSpec(array.shape, lambda i, *_: (0,) * array.ndim)


def tile_spec(array):
    return pl.BlockSpec((1,) + array.shape[1:], lambda i, *_: (i,) + (0,) * (array.ndim - 1))


def piece_spec(array):
    per_tile = QUERY_TILE // LANES
    return pl.BlockSpec((per_tile, min(array.shape[1], HEAD_DIM), LANES), lambda i, *_: (i, 0, 0))


def run_kernel(body, name, scalars, grid, inputs, outputs, scratch, flops):
    return pl.pallas_call(
        body,
        grid_spec=pltpu.PrefetchScalarGridSpec(
            num_scalar_prefetch=len(scalars),
            grid=(grid,),
            in_specs=[spec for _, spec in inputs],
            out_specs=[spec for _, spec in outputs],
            scratch_shapes=scratch,
        ),
        out_shape=[shape for shape, _ in outputs],
        compiler_params=pltpu.CompilerParams(vmem_limit_bytes=52 << 20),
        cost_estimate=pl.CostEstimate(
            flops=flops, transcendentals=flops // 400, bytes_accessed=16 << 20
        ),
        name=name,
    )(*scalars, *[array for array, _ in inputs])


def attend(query_pieces, own, other, half, pos, start, rel, low, high):
    tiles, _, queries = pos.shape
    key_total = own[0].shape[0] * LANES * len(own)
    key_tile = rel.shape[0]
    kind = jax.ShapeDtypeStruct
    pieces = kind((tiles * queries // LANES, HEAD_DIM, LANES), jnp.bfloat16)
    outputs = [
        kind((tiles, HEAD_DIM, queries), jnp.float32),
        pieces,
        kind((tiles, 1, queries), jnp.float32),
        kind((key_total, HEAD_DIM), jnp.bfloat16),
        kind((key_total // key_tile, HEAD_DIM, key_tile), jnp.bfloat16),
    ]
    return run_kernel(
        functools.partial(forward_kernel, slots=len(own)),
        "attention_forward",
        (low, high, half),
        tiles,
        [(query_pieces, piece_spec(query_pieces))]
        + [(each, fixed_spec(each.shape)) for each in own + other]
        + [(pos, tile_spec(pos)), (start, tile_spec(start)), (rel, fixed_spec(rel.shape))],
        [
            (outputs[0], tile_spec(outputs[0])),
            (outputs[1], piece_spec(outputs[1])),
            (outputs[2], tile_spec(outputs[2])),
            (outputs[3], fixed_spec(outputs[3].shape)),
            (outputs[4], fixed_spec(outputs[4].shape)),
        ],
        [],
        20_000_000_000,
    )


def attend_back(
    query_pieces,
    dout_pieces,
    out_cols,
    lse,
    key_rows,
    key_cols,
    value_rows,
    pos,
    start,
    rel,
    cosine,
    sine_part,
    low,
    high,
    slots,
    sent_kind,
):
    tiles, _, queries = pos.shape
    sources = key_rows.shape[0] // (slots * LANES)
    grads = (2, slots // 2, sources, HEAD_DIM, LANES)
    outputs = [
        jax.ShapeDtypeStruct((tiles * queries // LANES, HEAD_DIM, LANES), jnp.bfloat16),
        jax.ShapeDtypeStruct(grads, jnp.float32),
        jax.ShapeDtypeStruct(grads, sent_kind),
    ]
    return run_kernel(
        backward_kernel,
        "attention_backward",
        (low, high),
        tiles,
        [
            (query_pieces, piece_spec(query_pieces)),
            (dout_pieces, piece_spec(dout_pieces)),
            (out_cols, tile_spec(out_cols)),
            (lse, tile_spec(lse)),
            (key_rows, fixed_spec(key_rows.shape)),
            (key_cols, fixed_spec(key_cols.shape)),
            (value_rows, fixed_spec(value_rows.shape)),
            (pos, tile_spec(pos)),
            (start, tile_spec(start)),
            (rel, fixed_spec(rel.shape)),
            (cosine, piece_spec(cosine)),
            (sine_part, piece_spec(sine_part)),
        ],
        [
            (outputs[0], piece_spec(outputs[0])),
            (outputs[1], fixed_spec(grads)),
            (outputs[2], fixed_spec(grads)),
        ],
        [pltpu.VMEM(key_rows.shape, jnp.float32)] * 2,
        50_000_000_000,
    )


def per_device(
    tokens,
    segment_ids,
    out_grad,
    attn_master,
    attn_first,
    attn_second,
    ffn_master,
    ffn_first,
    ffn_second,
):
    index = lax.axis_index("seq")
    count = lax.axis_size("seq")
    rows = tokens.shape[0]
    total = rows * count
    group = count // KV_HEADS
    parts = group // 2
    span = rows // parts
    half = (index // parts) % 2
    part = index % parts

    def exchange(value):
        return lax.all_to_all(value, "seq", 0, 0, tiled=True)

    def swapped(value, bit):
        return lax.ppermute(value, "seq", [(i, i ^ bit) for i in range(count)])

    attn_low = attn_master.astype(jnp.bfloat16)
    ffn_low = ffn_master.astype(jnp.bfloat16)
    notice = jnp.concatenate(
        [attn_low[:D], ffn_low[:D], segment_ids.astype(jnp.bfloat16)]
    ).reshape(1, -1, 128)
    notices = exchange(jnp.broadcast_to(notice, (count,) + notice.shape[1:]))

    inputs = tokens.astype(jnp.float32)

    def from_notices(notices):
        gains = notices[0, : 2 * D // 128].astype(jnp.float32).reshape(2, D)
        all_ids = notices[:, 2 * D // 128 :].astype(jnp.int32).reshape(-1)
        held_ids = lax.dynamic_index_in_dim(
            all_ids.reshape(count, parts, span), part, 1, keepdims=False
        )

        def item_starts(ids):
            return jnp.sum((all_ids < ids[..., None]).astype(jnp.int32), axis=-1)

        return (
            gains[0],
            gains[1],
            rms_norm(inputs, gains[0]).astype(jnp.bfloat16),
            item_starts(held_ids.reshape(-1)),
            item_starts(all_ids[:: QUERY_TILE // span * rows]) // KEY_TILE,
        )

    grid = device_grid(count)
    by_axes = (D // count) % 16 == 0

    def sum_of(left_cols, right, right_dim, order):
        left = reordered(left_cols, slot_table(index, grid, order))
        return SummedRows(left, right, right_dim, order, grid)

    def scattered(left_cols, right, right_dim):
        whole = contract(left_cols, 1, right, right_dim).astype(jnp.bfloat16)
        return (
            lax.psum_scatter(whole, "seq", scatter_dimension=0, tiled=True)
            .reshape(-1)
            .astype(jnp.float32)
        )

    attn_block = aligned_block(attn_low, index, count)
    ffn_block = aligned_block(ffn_low, index, count)
    if by_axes:
        own_tiles = unit_tiles(ffn_block, (FF, FF, D), index, count)
        attn_tiles, own_tiles, beside = gather_tiles(
            unit_tiles(attn_block, (D, KV_HEADS * HEAD_DIM, D), index, count),
            index,
            grid,
            notices,
            own_tiles,
            from_notices,
        )
        ffn_tiles = lax.all_gather(own_tiles, "seq", axis=0, tiled=True)
        wide_rows = matrix_of(ffn_tiles, FF)
        gate_weight = (wide_rows, 0)
        up_weight = (wide_rows, D)
        down_weight = (matrix_of(ffn_tiles, D), 2 * FF)
        attn_wide = matrix_of(attn_tiles, D)
        attn_narrow = matrix_of(attn_tiles, KV_HEADS * HEAD_DIM)
        query_weight = (attn_wide, 0)
        key_weight = (attn_narrow, 2 * D)
        value_weight = (attn_narrow, 3 * D)
        out_weight = (attn_wide, 2 * D)
    else:

        def gathered(unit, width):
            return lax.all_gather(unit.reshape(-1, width), "seq", axis=0, tiled=True)

        q_unit, kv_unit, o_unit = units_from_block(attn_block, index, count)
        gate_unit, up_unit, down_unit = units_from_block(ffn_block, index, count)
        query_weight = (gathered(q_unit, HEADS * HEAD_DIM), 0)
        key_value_weight = gathered(kv_unit, KV_HEADS * HEAD_DIM)
        key_weight = (key_value_weight, 0)
        value_weight = (key_value_weight, D)
        out_weight = (gathered(o_unit, D), 0)
        gate_weight = (gathered(gate_unit, FF), 0)
        up_weight = (gathered(up_unit, FF), 0)
        down_weight = (gathered(down_unit, D), 0)

    gain_one, gain_two, normed_one, held_starts, low = (
        beside if by_axes else from_notices(notices)
    )

    own_places = index * rows + jnp.arange(rows, dtype=jnp.int32)
    own_cos, own_sin = angle_tables(own_places)

    cols = span if span % 128 == 0 else rows

    def by_owner(value):
        if value.shape[0] == count:
            return value
        pieces = value.reshape(HEADS, value.shape[1], parts, span)
        return jnp.swapaxes(pieces, 1, 2).reshape(count, value.shape[1], span)

    def by_head(value):
        pieces = value.reshape(HEADS, parts, value.shape[1], span)
        return jnp.swapaxes(pieces, 1, 2).reshape(HEADS, value.shape[1], rows)

    received = exchange(
        by_owner(
            project(normed_one, query_weight, key_weight, value_weight, own_cos, own_sin, cols)
        )
    )

    merged = LANES // span

    def to_pieces(value):
        if merged == 1:
            return value
        pieces = value.reshape(count // merged, merged, value.shape[1], span)
        return jnp.swapaxes(pieces, 1, 2).reshape(count // merged, value.shape[1], LANES)

    def from_pieces(value):
        if merged == 1:
            return value
        pieces = value.reshape(count // merged, value.shape[1], merged, span)
        return jnp.swapaxes(pieces, 1, 2).reshape(count, value.shape[1], span)

    own_kind = received[:, HEAD_DIM:]
    both_kinds = [[own_kind], [swapped(own_kind, parts)]]
    bit = 1
    while bit < parts:
        both_kinds = [kind + [swapped(each, bit) for each in kind] for kind in both_kinds]
        bit = bit * 2
    own, other = [[to_pieces(each) for each in kind] for kind in both_kinds]
    query_pieces = to_pieces(received)
    sources = QUERY_TILE // span
    tiles = count // sources
    within = jnp.arange(span, dtype=jnp.int32)
    rel = (
        span * (part ^ jnp.arange(parts, dtype=jnp.int32))[:, None, None]
        + rows * jnp.arange(KEY_TILE // rows, dtype=jnp.int32)[None, :, None]
        + within[None, None, :]
    ).reshape(KEY_TILE, 1)
    rel = jnp.broadcast_to(rel, (KEY_TILE, LANES))
    held_places = (
        rows * jnp.arange(count, dtype=jnp.int32)[:, None] + span * part + within[None, :]
    )
    pos = held_places.reshape(tiles, 1, QUERY_TILE)
    start = held_starts.reshape(tiles, 1, QUERY_TILE)
    tile_span = sources * rows
    high = (jnp.arange(1, tiles + 1, dtype=jnp.int32) * tile_span + KEY_TILE - 1) // KEY_TILE

    chunks = []
    chunk = min(CHUNK, total)
    per_tile = QUERY_TILE // LANES
    for first in range(0, total, chunk):
        of_tiles = slice(first // tile_span, (first + chunk) // tile_span)
        of_queries = slice(of_tiles.start * per_tile, of_tiles.stop * per_tile)
        first_key = max(0, first - SEG_MOST) // KEY_TILE
        last_key = (first + chunk) // KEY_TILE
        per_piece = merged * rows
        of_keys = slice(
            first_key * KEY_TILE // per_piece, last_key * KEY_TILE // per_piece
        )
        chunks.append((of_tiles, of_queries, first_key, of_keys))

    attended = []
    for of_tiles, of_queries, first_key, of_keys in chunks:
        shift = first_key * KEY_TILE
        attended.append(
            attend(
                query_pieces[of_queries],
                [each[of_keys] for each in own],
                [each[of_keys] for each in other],
                half.reshape(1),
                pos[of_tiles] - shift,
                start[of_tiles] - shift,
                rel,
                low[of_tiles] - first_key,
                high[of_tiles] - first_key,
            )
        )
    mixed_pieces = exchange(
        from_pieces(jnp.concatenate([piece[1] for piece in attended]))
    )
    held = []
    for out_cols, _, lse, key_rows, value_cols in attended:
        key_cols = jnp.swapaxes(key_rows.reshape(-1, KEY_TILE, HEAD_DIM), 1, 2)
        value_rows = jnp.swapaxes(value_cols, 1, 2).reshape(-1, HEAD_DIM)
        held.append((out_cols, lse, key_rows, key_cols, value_rows))
    held_cos, held_sin = [to_pieces(table) for table in angle_tables(held_places)]
    mixed_pieces, (held, held_cos, held_sin) = together(
        mixed_pieces, (held, held_cos, held_sin)
    )
    if cols == rows:
        mixed_pieces = by_head(mixed_pieces)

    (
        result,
        middle_grad,
        middle_low,
        dout_pieces,
        grad_two,
        gate_grad,
        up_grad,
        hidden_cols,
        normed_two_cols,
        mixed_low,
    ) = feed_forward(
        tokens,
        mixed_pieces,
        gain_two,
        out_grad,
        out_weight,
        gate_weight,
        up_weight,
        down_weight,
    )
    dout_received = exchange(by_owner(dout_pieces))
    if by_axes:
        gate_sum = sum_of(normed_two_cols, gate_grad, 0, GATE_ORDER)
        up_sum = sum_of(normed_two_cols, up_grad, 0, UP_ORDER)
        down_sum = sum_of(hidden_cols, out_grad, 0, DOWN_ORDER)
        first_sums = [gate_sum, up_sum]
        make_and_send(first_sums + [down_sum])
        dout_received = made_before(first_sums, dout_received)
        for each in first_sums:
            each.send()
    else:
        ffn_units = [
            scattered(normed_two_cols, gate_grad, 0),
            scattered(normed_two_cols, up_grad, 0),
            scattered(hidden_cols, out_grad, 0),
        ]
        out_unit = scattered(mixed_low, middle_low, 0)
    dout_pieces = to_pieces(dout_received)

    one_chunk = len(chunks) == 1
    dquery_pieces = []
    summed = [jnp.zeros((2, max(parts // 2, 1), count // merged, HEAD_DIM, LANES), jnp.float32)] * 2
    for (of_tiles, of_queries, first_key, of_keys), kept_values in zip(chunks, held):
        shift = first_key * KEY_TILE
        dquery_piece, *found = attend_back(
            query_pieces[of_queries],
            dout_pieces[of_queries],
            *kept_values,
            pos[of_tiles] - shift,
            start[of_tiles] - shift,
            rel,
            held_cos[of_queries],
            held_sin[of_queries],
            low[of_tiles] - first_key,
            high[of_tiles] - first_key,
            parts,
            jnp.bfloat16 if one_chunk else jnp.float32,
        )
        dquery_pieces.append(dquery_piece)
        if one_chunk:
            summed = found
        else:
            summed = [
                whole.at[:, :, of_keys].add(piece) for whole, piece in zip(summed, found)
            ]
    dquery_held = from_pieces(jnp.concatenate(dquery_pieces))
    grads, sent = summed
    if by_axes:
        mixed_late, grads = together(mixed_low, grads)
        out_sum = sum_of(mixed_late, middle_low, 0, OUT_ORDER)
    grads = grads + swapped(sent.astype(jnp.bfloat16), parts // 2)
    bit = parts // 4
    while bit >= 1:
        grads = grads[:, :bit] + swapped(grads[:, bit:].astype(jnp.bfloat16), bit)
        bit = bit // 2
    if by_axes:
        grads = taken_after(first_sums, grads)
    dkey_held, dvalue_held = (grads[0, 0], grads[1, 0])
    sent_kind = jnp.where(half == 0, dvalue_held, dkey_held).astype(jnp.bfloat16)
    kept_kind = jnp.where(half == 0, dkey_held, dvalue_held) + swapped(sent_kind, parts)
    kept_low = from_pieces(
        jnp.where(half == 0, rotate(kept_kind, held_cos, -held_sin), kept_kind).astype(
            jnp.bfloat16
        )
    )
    sent_back = jnp.concatenate([dquery_held, kept_low], axis=1)
    if by_axes:
        early_sums = first_sums + [down_sum]
        sent_back = made_before(early_sums, sent_back)
        for each in early_sums:
            each.send()
    returned = exchange(sent_back)
    if by_axes:
        make_and_send([out_sum])
        returned = taken_after([down_sum], made_before(first_sums, returned))
        for each in first_sums:
            each.send()
    dquery_low = by_head(returned[:, :HEAD_DIM]).reshape(HEADS * HEAD_DIM, rows)
    pair_low = by_head(returned[:, HEAD_DIM:]).reshape(KV_HEADS, 2, HEAD_DIM, rows)
    dkey_low = pair_low[:, 0].reshape(KV_HEADS * HEAD_DIM, rows)
    dvalue_low = pair_low[:, 1].reshape(KV_HEADS * HEAD_DIM, rows)

    normed_one_cols = normed_one.T
    nothing = jnp.zeros_like(normed_one_cols)
    key_value_cols = jnp.concatenate(
        [
            jnp.concatenate([normed_one_cols, nothing], axis=1),
            jnp.concatenate([nothing, normed_one_cols], axis=1),
        ]
    )
    key_value_right = jnp.concatenate([dkey_low, dvalue_low], axis=1)
    if by_axes:
        query_sum = sum_of(normed_one_cols, dquery_low, 1, GATE_ORDER)
        key_value_sum = sum_of(key_value_cols, key_value_right, 1, UP_ORDER)
        last_sums = [query_sum, key_value_sum]
        make_and_send(last_sums)
        for each in last_sums:
            each.make()
        for other_sum in early_sums + [out_sum]:
            taken_after([other_sum], [each.made for each in last_sums])
        for each in last_sums:
            each.send()
        dquery_late = taken_after(last_sums, dquery_low)
        make_and_send([gate_sum, up_sum, down_sum, out_sum])
        normed_one_grad = (
            contract(dquery_late, 0, query_weight[0][:D], 1)
            + contract(dkey_low, 0, key_weight[0][key_weight[1] : key_weight[1] + D], 1)
            + contract(dvalue_low, 0, value_weight[0][value_weight[1] : value_weight[1] + D], 1)
        )
        _, first_pull = jax.vjp(rms_norm, inputs, gain_one)
        input_norm_grad, grad_one = first_pull(normed_one_grad)
        input_grad = middle_grad + input_norm_grad

        gain_sum = SummedWhole(jnp.concatenate([grad_one, grad_two[0]]).reshape(-1, 128), grid)
        attn_sums = last_sums + [out_sum]
        make_and_send([gain_sum])
        one_round(attn_sums + early_sums + [gain_sum])
        for _ in range(2):
            one_round(attn_sums + [gain_sum])
            make_and_send([down_sum])
        ffn_units = [gate_sum.result(), up_sum.result(), down_sum.result()]
        one_round(attn_sums + [gain_sum])
        gain_grads = gain_sum.result().reshape(2, D)
        query_unit, key_value_unit, out_unit = [each.result() for each in attn_sums]
    else:
        query_unit = scattered(normed_one_cols, dquery_low, 1)
        key_value_unit = scattered(key_value_cols, key_value_right, 1)
        normed_one_grad = (
            contract(dquery_low, 0, query_weight[0][:D], 1)
            + contract(dkey_low, 0, key_weight[0][key_weight[1] : key_weight[1] + D], 1)
            + contract(dvalue_low, 0, value_weight[0][value_weight[1] : value_weight[1] + D], 1)
        )
        _, first_pull = jax.vjp(rms_norm, inputs, gain_one)
        input_norm_grad, grad_one = first_pull(normed_one_grad)
        input_grad = middle_grad + input_norm_grad

        gain_grads = lax.psum(jnp.stack([grad_one, grad_two[0]]), "seq")
    ffn_shard = shard_from_units(ffn_units, gain_grads[1], index, count)
    attn_shard = shard_from_units(
        [query_unit, key_value_unit, out_unit], gain_grads[0], index, count
    )
    attn_new, attn_one, attn_two = adam_update(
        attn_master, attn_first, attn_second, attn_shard
    )
    ffn_new, ffn_one, ffn_two = adam_update(
        ffn_master, ffn_first, ffn_second, ffn_shard
    )
    return (result, input_grad, attn_new, attn_one, attn_two, ffn_new, ffn_one, ffn_two)


def solution(mesh):
    rows_cut = P("seq", None)
    flat_cut = P("seq")
    in_specs = (rows_cut, flat_cut, rows_cut) + (flat_cut,) * 6
    out_specs = (rows_cut, rows_cut) + (flat_cut,) * 6
    return jax.shard_map(
        per_device, mesh=mesh, in_specs=in_specs, out_specs=out_specs, check_vma=False
    )
```
